32 devices in a mesh: groups: 2 (over x), tile: 16 (over z, y, core).
Axes of the slice: x: 2, y: 2, z: 4, core: 2. Of those that a mesh axis runs over, the one named last changes fastest.
Arguments:
- queries: bfloat16 [2048, 4096], P(('groups', 'tile')), parts along dimension 0, may hold values from -8 to 8
- key_rows: bfloat16 [2048, 4096], P(('groups', 'tile')), parts along dimension 0, may hold values from -8 to 8
- values: bfloat16 [2048, 4096], P(('groups', 'tile')), parts along dimension 0, may hold values from -6 to 6
- modulation: float32 [6, 4096], P('groups'), parts along dimension 0, may hold values from -3 to 3
- expert_in: bfloat16 [4096, 8192], P(None, 'tile'), may hold values from -0.09375 to 0.09375
- expert_out: bfloat16 [8192, 4096], P('tile'), may hold values from -0.125 to 0.125
- routes: int32 [2048, 2], P(('groups', 'tile')), parts along dimension 0, may hold values from 0 to 3, all different within a row; in each aligned block of 64 rows (0 to 63, 64 to 127, ...) at most 48 rows name the same one
- gate_fixed: int32 [2048, 2], P(('groups', 'tile')), parts along dimension 0, may hold values from 64 to 1023
Outputs:
- layer_out: bfloat16 [2048, 4096], P(('groups', 'tile')), parts along dimension 0
The draws below stay inside these ranges and needn't reach their ends.
There are 2 independent parts, one for each index of `groups`. The reference program is written for one: setup_inputs(seed, part) draws one part's arguments, and reference() takes and returns one part's arrays. A program takes and returns all parts, laid end to end along the dimension named above; an argument that names none is the same for every part. Nothing has to cross between parts.
Inputs may be any that keep to these rules, and one draw needn't show every extreme that they name: `routes`: the two experts of a token differ; among the 64 tokens of one tile no expert is named more than 48 times.
All inputs are finite; a program needn't handle non-finite values.
Results may differ from the reference program's by a relative error of at most 0.011.
Values may be sent and summed in bfloat16 or wider, within the bound.
A program may use at most 128 MiB of HBM per device.

```python
import math
import jax
import jax.numpy as jnp
import numpy as np
from jax import lax

HEAD_DIM = 128
D = 4096
SPLIT = 4
EFF_DEV = 512
TILE_COLS = 8
TOK_DEV = 64
TOKENS = 1024
EXPERTS = 4
CAP = 48
N_TILE = 16


def draw_queries(key, part):
    field = jnp.clip(jax.random.normal(jax.random.fold_in(key, 11), (TOKENS, D), jnp.float32), -4.0, 4.0)
    return field.astype(jnp.bfloat16)


def draw_key_rows(key, part):
    field = jnp.clip(jax.random.normal(jax.random.fold_in(key, 13), (TOKENS, D), jnp.float32), -4.0, 4.0)
    return field.astype(jnp.bfloat16)


def place_ends(values, stream_key, smallest, largest):
    longest = values.shape.index(max(values.shape))
    spots = []
    for shift in (0, 1):
        where = [jax.random.randint(jax.random.fold_in(stream_key, axis), (), 0, length) for axis, length in enumerate(values.shape)]
        where[longest] = (where[longest] + shift) % values.shape[longest]
        spots.append(tuple(where))
    return values.at[spots[0]].set(smallest).at[spots[1]].set(largest)


def block_scale(stream_key, extent, cuts, smallest, high):
    def one(position, parts):
        steps = jax.random.uniform(jax.random.fold_in(jax.random.fold_in(stream_key, 6), position), (parts,), jnp.float32, smallest / len(cuts), high / len(cuts))
        return jnp.repeat(jnp.exp(steps), extent[position] // parts).reshape((-1,) + (1,) * (len(extent) - position - 1))

    loudness = one(*cuts[0])
    for cut in cuts[1:]:
        loudness = loudness * one(*cut)
    return loudness


def routed_block(key, own, number, rows, amount, top, most, slope):
    order = jax.random.permutation(key, amount)
    crowded, ordinary = portions_of(amount, rows * top, most, slope, True), portions_of(amount, rows * top, most, slope, False)
    places = jnp.arange(amount)

    def named(sizes, offset_by):
        used = int((sizes > 0).sum())
        fixed = max(1, used // 4)
        moved = fixed + (places - fixed + offset_by * (used - fixed)) % max(1, amount - fixed)
        return jnp.zeros((amount,), jnp.int32).at[order[jnp.where(places < fixed, places, moved)]].set(jnp.asarray(sizes, jnp.int32))

    sizes = jnp.where(number % 4 == 0, named(crowded, number // 4), named(ordinary, number - number // 4 - 1))
    mixed = jax.random.permutation(jax.random.fold_in(own, 3), amount)
    giver, receiver = mixed[0:amount // 2 * 2:2], mixed[1:amount // 2 * 2:2]
    room = jnp.minimum(sizes[giver] - 1, most - sizes[receiver]) // 2
    room = jnp.where((giver == order[0]) | (receiver == order[0]) | (sizes[receiver] == 0), 0, jnp.maximum(room, 0))
    moved = jax.random.randint(jax.random.fold_in(own, 4), (amount // 2,), 0, 1 << 20) % (room + 1)
    sizes = sizes.at[giver].add(-moved).at[receiver].add(moved)
    members = jnp.searchsorted(jnp.cumsum(sizes), jnp.arange(rows * top), side="right").astype(jnp.int32)
    table = members.reshape(top, rows).T
    table = table[jax.random.permutation(jax.random.fold_in(own, 1), rows)]
    offset_by = jax.random.randint(jax.random.fold_in(own, 2), (rows, 1), 0, top)
    return jnp.take_along_axis(table, (jnp.arange(top)[None, :] + offset_by) % top, axis=1)


def portions_of(amount, total, most, skew, full):
    portions = [(1 << 20) // math.isqrt(grade ** skew) + 1 for grade in range(1, amount + 1)]
    largest = most if full else min(most, max(-(-total // amount), total * portions[0] // sum(portions)))
    least = 1 if total - largest >= amount - 1 else 0
    given, rest = [largest] + [least] * (amount - 1), total - largest - least * (amount - 1)
    while rest > 0:
        candidates = [i for i in range(1, amount) if given[i] < largest] or [i for i in range(1, amount) if given[i] < most]
        mass, budget = sum([portions[i] for i in candidates]), rest
        for i in candidates:
            addition = min(most - given[i], max(1, budget * portions[i] // mass), rest)
            given[i] = given[i] + addition
            rest = rest - addition
    return np.array(given)


def gaussian(key, shape, scale, most, cuts=(), kind=jnp.bfloat16):
    entries = jax.random.normal(key, shape, jnp.float32) * scale
    if len(cuts) > 0:
        entries = block_scale(key, shape, cuts, -0.22, 0.18) * entries
    return jnp.clip(entries, min=-most, max=most).astype(kind)


def setup_inputs(seed: int = 0, part: int = 0) -> dict:
    seeds = jax.random.split(jax.random.key(seed), 9)
    own_keys = jax.random.split(jax.random.fold_in(seeds[8], part), 9)
    queries = draw_queries(jax.random.fold_in(jax.random.fold_in(seeds[8], part), 71), part)
    key_rows = draw_key_rows(jax.random.fold_in(jax.random.fold_in(seeds[8], part), 71), part)
    values = gaussian(own_keys[2], (TOKENS, D), 1.0, 6.0, ((0, 16),))
    modulation = gaussian(own_keys[3], (3, D), 0.5, 3.0, (), jnp.float32)
    expert_in = gaussian(seeds[4], (D, EXPERTS * SPLIT * EFF_DEV), D ** -0.5, 0.09375, ((1, 16),))
    expert_out = gaussian(seeds[5], (EXPERTS * SPLIT * EFF_DEV, D), (SPLIT * EFF_DEV) ** -0.5, 0.125, ((0, 16),))
    routes_keys = jax.random.split(jax.random.fold_in(own_keys[6], 1), TOKENS // TOK_DEV)
    routes_turns = jax.random.permutation(jax.random.fold_in(own_keys[6], 3), TOKENS // TOK_DEV)
    routes = jax.vmap(lambda own, number: routed_block(jax.random.fold_in(own_keys[6], 2), own, number, TOK_DEV, EXPERTS, 2, CAP, 2))(routes_keys, routes_turns).reshape((TOKENS, 2))
    gate_fixed = place_ends(jax.random.randint(own_keys[7], (TOKENS, 2), 64, 1024), jax.random.fold_in(own_keys[7], 1), 64, 1023).astype(jnp.int32)
    return {"queries": queries, "key_rows": key_rows, "values": values, "modulation": modulation, "expert_in": expert_in, "expert_out": expert_out, "routes": routes, "gate_fixed": gate_fixed}


EPSILON = 1e-06
MASKED = -1e+30

def attend_tile(query_block, banded, allowed):
    rows_here = query_block.shape[0]
    heads_count = D // HEAD_DIM
    query_heads = query_block.astype(jnp.float32).reshape(rows_here, heads_count, HEAD_DIM)
    key_heads = banded[0].astype(jnp.float32).reshape(banded.shape[1], heads_count, HEAD_DIM)
    value_heads = banded[1].astype(jnp.float32).reshape(banded.shape[1], heads_count, HEAD_DIM)
    scores = jnp.einsum('qhd,khd->hqk', query_heads, key_heads) * (1.0 / math.sqrt(HEAD_DIM))
    scores = jnp.where(allowed[None, None, :], scores, MASKED)
    highest = lax.optimization_barrier(jnp.max(scores, axis=-1, keepdims=True))
    raised = jnp.exp(scores - highest)
    probs = (raised / lax.optimization_barrier(jnp.sum(raised, axis=-1, keepdims=True))).astype(jnp.bfloat16)
    attended = jnp.einsum('hqk,khd->qhd', probs.astype(jnp.float32), value_heads)
    return attended.reshape(rows_here, D).astype(jnp.bfloat16)

def modulate(attended, modulation):
    wide = attended.astype(jnp.float32)
    center = lax.optimization_barrier(jnp.mean(wide, axis=-1, keepdims=True))
    spread = lax.optimization_barrier(jnp.mean(jnp.square(wide - center), axis=-1, keepdims=True))
    normed = (wide - center) * lax.rsqrt(spread + EPSILON)
    return (normed * (1.0 + modulation[1]) + modulation[0]).astype(jnp.bfloat16)

def slot_table(flat, experts_count):
    onehot = (flat[:, None] == jnp.arange(experts_count, dtype=jnp.int32)[None, :]).astype(jnp.int32)
    before = jnp.cumsum(onehot, axis=0) - onehot
    return lax.optimization_barrier(jnp.sum(before * onehot, axis=1)).astype(jnp.int32)

def expert_apply(rows, first_weight, second_weight):
    hidden = jax.nn.gelu(jnp.dot(rows, first_weight, preferred_element_type=jnp.float32), approximate=True).astype(jnp.bfloat16)
    return jnp.dot(hidden, second_weight, preferred_element_type=jnp.float32).astype(jnp.bfloat16)

def reference(queries, key_rows, values, modulation, expert_in, expert_out, routes, gate_fixed):
    experts_count = N_TILE // SPLIT
    capacity = 3 * TOK_DEV // experts_count
    grid_rows = N_TILE // TILE_COLS
    rotation = TILE_COLS // 2
    blocks = jnp.stack([key_rows, values]).reshape(2, N_TILE, TOK_DEV, D)
    tile_order = jnp.roll(blocks, rotation, axis=1)
    stacked = tile_order.reshape(2, grid_rows, TILE_COLS, TOK_DEV, D)
    padded = jnp.pad(stacked, ((0, 0), (1, 1), (1, 1), (0, 0), (0, 0)))

    def one_block(block_number):
        tile_number = ((block_number + rotation) % N_TILE).astype(jnp.int32)
        grid_row = (tile_number // TILE_COLS).astype(jnp.int32)
        grid_col = (tile_number % TILE_COLS).astype(jnp.int32)
        zero = jnp.zeros((), jnp.int32)
        block = lax.dynamic_slice(padded, (zero, grid_row, grid_col, zero, zero), (2, 3, 3, TOK_DEV, D))
        banded = block.reshape(2, 9 * TOK_DEV, D)
        start = (block_number * TOK_DEV).astype(jnp.int32)
        query_block = lax.dynamic_slice_in_dim(queries, start, TOK_DEV, 0)
        rows_ok = jnp.stack([grid_row > 0, grid_row >= 0, grid_row < grid_rows - 1])
        cols_ok = jnp.stack([grid_col > 0, grid_col >= 0, grid_col < TILE_COLS - 1])
        usable = rows_ok[:, None] & cols_ok[None, :]
        allowed = jnp.broadcast_to(usable[:, :, None], (3, 3, TOK_DEV)).reshape(9 * TOK_DEV)
        return attend_tile(query_block, banded, allowed)
    attended = lax.map(one_block, jnp.arange(N_TILE, dtype=jnp.int32)).reshape(TOKENS, D)
    normed = modulate(attended, modulation)
    tile_routes = routes.reshape(N_TILE, 2 * TOK_DEV)
    slots = jax.vmap(slot_table, in_axes=(0, None))(tile_routes, experts_count)
    sources = jnp.arange(N_TILE, dtype=jnp.int32)[:, None]
    place = (tile_routes * (N_TILE * capacity) + sources * capacity + slots).reshape(-1).astype(jnp.int32)
    token_of = (jnp.arange(2 * TOKENS, dtype=jnp.int32) // 2).astype(jnp.int32)
    table = jnp.full((experts_count * N_TILE * capacity,), TOKENS, jnp.int32).at[place].set(token_of)
    extended = jnp.concatenate([normed, jnp.zeros((1, D), normed.dtype)], axis=0)

    def one_expert(expert):
        chosen = lax.dynamic_slice_in_dim(table, (expert * (N_TILE * capacity)).astype(jnp.int32), N_TILE * capacity, 0)
        rows = jnp.take(extended, chosen, axis=0)
        total = jnp.zeros((N_TILE * capacity, D), jnp.float32)
        for quarter in range(SPLIT):
            column = ((expert * SPLIT + quarter) * EFF_DEV).astype(jnp.int32)
            first_weight = lax.dynamic_slice_in_dim(expert_in, column, EFF_DEV, 1)
            second_weight = lax.dynamic_slice_in_dim(expert_out, column, EFF_DEV, 0)
            total = total + expert_apply(rows, first_weight, second_weight).astype(jnp.float32)
        return total.astype(jnp.bfloat16)
    expert_rows = lax.map(one_expert, jnp.arange(experts_count, dtype=jnp.int32)).reshape(experts_count * N_TILE * capacity, D)
    picked = jnp.take(expert_rows, place, axis=0).reshape(TOKENS, 2, D)
    gate_scale = gate_fixed.astype(jnp.float32) / 1024.0
    mixture = lax.optimization_barrier(jnp.sum(picked.astype(jnp.float32) * gate_scale[:, :, None], axis=1))
    return (attended.astype(jnp.float32) + modulation[2] * mixture).astype(jnp.bfloat16)
```

```python
import functools
import math

import jax
import jax.numpy as jnp
from jax import lax
from jax.experimental import pallas as pl
from jax.experimental.pallas import tpu as pltpu
from jax.sharding import PartitionSpec as P

HEAD_DIM = 128
D = 4096
SPLIT = 4
TILE_COLS = 8

EPSILON = 1e-06
MASKED = -1e30
MESH = pl.DeviceIdType.MESH
VMEM_LIMIT = 60 * 1024 * 1024


def when(cond, body):
    if cond is True:
        body()
    else:
        pl.when(cond)(body)


def both(a, b):
    if a is True:
        return b
    if b is True:
        return a
    return jnp.logical_and(a, b)


def remote(src, dst, send_sem, recv_sem, target):
    return pltpu.make_async_remote_copy(
        src_ref=src,
        dst_ref=dst,
        send_sem=send_sem,
        recv_sem=recv_sem,
        device_id={"tile": target},
        device_id_type=MESH,
    )


def halo_levels(n):
    grid_rows = n // TILE_COLS
    if grid_rows < 2:
        return 1
    return 2 if grid_rows == 2 else 3


def attention_kernel(
    n, rows, q_ref, k_ref, v_ref, mod_ref, att_ref, norm_ref, keys, vals, send_sem, recv_sem, own_sem,
):
    me = lax.axis_index("tile")
    grid_rows = n // TILE_COLS
    tile = lax.rem(me + TILE_COLS // 2, n)
    row = lax.div(tile, TILE_COLS)
    col = lax.rem(tile, TILE_COLS)
    if grid_rows < 2:
        verticals = []
    elif grid_rows == 2:
        verticals = [(1, TILE_COLS, True, 1)]
    else:
        verticals = [(1, n - TILE_COLS, row > 0, 2), (2, TILE_COLS, row < grid_rows - 1, 1)]
    sides = [(-1, col > 0), (1, col < TILE_COLS - 1)]
    here = {level: exists for level, _, exists, _ in verticals}
    here[0] = True

    def slot(level, side):
        return level * 3 + 1 + side

    def place(buf, s):
        return buf.at[pl.ds(s * rows, rows), :]

    def over(offset):
        return lax.rem(me + offset + n, n)

    half = rows // 2
    middle = TILE_COLS // 2
    crossing = {side: col == (middle if side < 0 else middle - 1) for side, _ in sides}
    two = grid_rows == 2

    def part_of(buf, s, h):
        return buf.at[pl.ds(pl.multiple_of(s * rows + h * half, half), half), :]

    own = [
        pltpu.make_async_copy(src, place(buf, slot(0, 0)), own_sem.at[i])
        for i, (src, buf) in enumerate(((k_ref, keys), (v_ref, vals)))
    ]
    for copy in own:
        copy.start()

    def beside(side):
        if not two:
            return over(side)
        return jnp.where(crossing[side], over(side + TILE_COLS), over(side))

    def level_there(level, side):
        return jnp.where(crossing[side], 1 - level, level) if two else level

    barrier = pltpu.get_barrier_semaphore()
    partners = [(over(offset), exists) for _, offset, exists, _ in verticals]
    partners += [(beside(side), exists) for side, exists in sides]
    for target, exists in partners:

        def greet(target=target):
            pl.semaphore_signal(barrier, inc=1, device_id={"tile": target}, device_id_type=MESH)

        when(exists, greet)
    expected = sum(1 if exists is True else jnp.where(exists, 1, 0) for _, exists in partners)
    pl.semaphore_wait(barrier, expected)

    sends = []
    pieces = [(i, h) for i in (0, 1) for h in (0, 1)]
    bufs = (keys, vals)

    def push(i, h, src, there, target, exists):
        copy = remote(
            src,
            part_of(bufs[i], there, h),
            send_sem.at[len(sends)],
            recv_sem.at[there, i * 2 + h],
            target,
        )
        when(exists, copy.start)
        sends.append((copy, exists))

    def arrived(s, exists, i, h):
        ref = part_of(bufs[i], s, h)
        when(exists, remote(ref, ref, send_sem.at[0], recv_sem.at[s, i * 2 + h], me).wait_recv)

    def own_part(i, h):
        return (k_ref, v_ref)[i].at[pl.ds(h * half, half), :]

    for i, h in pieces:
        for level, offset, exists, there in verticals:
            push(i, h, own_part(i, h), slot(there, 0), over(offset), exists)
    for i, h in pieces:
        for side, exists in sides:
            push(i, h, own_part(i, h), slot(level_there(0, side), -side), beside(side), exists)
    for s in range(3 * (1 + len(verticals))):
        level, side = s // 3, s % 3 - 1
        exists = here[level]
        for other, side_exists in sides:
            if other == side:
                exists = both(exists, side_exists)
        if exists is True:
            continue

        def clear(s=s):
            for buf in (keys, vals):
                buf[pl.ds(s * rows, rows), :] = jnp.zeros((rows, D), buf.dtype)

        pl.when(jnp.logical_not(exists))(clear)
    for i, h in pieces:
        for level, offset, exists, there in verticals:
            arrived(slot(level, 0), exists, i, h)
            for side, side_exists in sides:
                push(
                    i,
                    h,
                    part_of(bufs[i], slot(level, 0), h),
                    slot(level_there(level, side), -side),
                    beside(side),
                    both(exists, side_exists),
                )
    for copy in own:
        copy.wait()
    for i, h in pieces:
        for level, exists in sorted(here.items(), key=lambda item: item[0]):
            for side, side_exists in sides:
                arrived(slot(level, side), both(exists, side_exists), i, h)

    span = 3 * (1 + len(verticals)) * rows
    where = lax.broadcasted_iota(jnp.int32, (rows, span), 1)
    bias = jnp.zeros((rows, span), jnp.float32)
    for s in range(span // rows):
        level, side = s // 3, s % 3 - 1
        exists = here[level]
        for other, side_exists in sides:
            if other == side:
                exists = both(exists, side_exists)
        if exists is True:
            continue
        penalty = jnp.where(exists, 0.0, MASKED)
        bias = jnp.where((where >= s * rows) & (where < (s + 1) * rows), penalty, bias)
    scale = 1.0 / math.sqrt(HEAD_DIM)
    together = 8

    def heads(step, carry):
        for extra in range(together):
            at = pl.ds(pl.multiple_of((step * together + extra) * HEAD_DIM, HEAD_DIM), HEAD_DIM)
            scores = lax.dot_general(
                q_ref[:, at], keys[:, at], (((1,), (1,)), ((), ())), preferred_element_type=jnp.float32
            )
            scores = scores * scale + bias
            raised = jnp.exp(scores - jnp.max(scores, axis=-1, keepdims=True))
            probs = (raised * (1.0 / jnp.sum(raised, axis=-1, keepdims=True))).astype(jnp.bfloat16)
            att_ref[:, at] = jnp.dot(probs, vals[:, at], preferred_element_type=jnp.float32).astype(
                att_ref.dtype
            )
        return carry

    lax.fori_loop(0, D // HEAD_DIM // together, heads, 0)

    def normalise(step, carry):
        at = pl.ds(pl.multiple_of(step * 16, 16), 16)
        wide = att_ref[at, :].astype(jnp.float32)
        wide = wide - jnp.mean(wide, axis=-1, keepdims=True)
        spread = jnp.mean(wide * wide, axis=-1, keepdims=True)
        normed = wide * lax.rsqrt(spread + EPSILON)
        norm_ref[at, :] = (normed * (1.0 + mod_ref[1:2, :]) + mod_ref[0:1, :]).astype(norm_ref.dtype)
        return carry

    lax.fori_loop(0, rows // 16, normalise, 0)
    for copy, exists in sends:
        when(exists, copy.wait_send)


def attention(queries, key_rows, values, modulation):
    n = lax.axis_size("tile")
    rows = queries.shape[0]
    levels = halo_levels(n)
    slots = 3 * levels
    vmem = pl.BlockSpec(memory_space=pltpu.VMEM)
    hbm = pl.BlockSpec(memory_space=pl.ANY)
    return pl.pallas_call(
        functools.partial(attention_kernel, n, rows),
        name="halo_attention",
        out_shape=(
            jax.ShapeDtypeStruct((rows, D), jnp.bfloat16),
            jax.ShapeDtypeStruct((rows, D), jnp.bfloat16),
        ),
        in_specs=[vmem, hbm, hbm, vmem],
        out_specs=(vmem, vmem),
        scratch_shapes=[
            pltpu.VMEM((slots * rows, D), jnp.bfloat16),
            pltpu.VMEM((slots * rows, D), jnp.bfloat16),
            pltpu.SemaphoreType.DMA((4 * (2 + 3 * (levels - 1)),)),
            pltpu.SemaphoreType.DMA((slots, 4)),
            pltpu.SemaphoreType.DMA((2,)),
        ],
        compiler_params=pltpu.CompilerParams(
            collective_id=0, has_side_effects=True, vmem_limit_bytes=VMEM_LIMIT
        ),
    )(queries, key_rows, values, modulation)


def device(plane, yy, cc):
    return plane * SPLIT + yy * 2 + cc


def layer_kernel(
    n, rows, cap, chunks, q_ref, k_ref, v_ref, mod_ref, routes_ref, gates_ref, first_ref, second_ref,
    out_ref, att, bias, keys, vals, line, tokens, stage, chooser, tables, stats, normed, first, second,
    hidden, part, r1, r2, pair, acc_in, acc_out,
    own_sem, kv_send, kv_recv, table_send, table_recv, stat_send, stat_recv, out_send, line_recv,
    token_recv, back_send, s1_recv, s2_recv, pair_recv, acc_recv,
):
    planes = n // SPLIT
    width = first.shape[1]
    wide = D // chunks
    me = lax.axis_index("tile")
    p = lax.div(me, SPLIT)
    y = lax.div(lax.rem(me, SPLIT), 2)
    c = lax.rem(me, 2)
    beside = device(p, 1 - y, c)
    twin = device(p, y, 1 - c)
    low_half = p < planes // 2
    toward = jnp.where(low_half, 1, -1)
    inner = p + toward
    outer = p - toward
    at_end = jnp.logical_or(p == 0, p == planes - 1)
    middle = jnp.logical_not(at_end)
    outer_expert = jnp.where(low_half, 0, planes - 1)
    inner_device = device(inner, y, c)
    outer_device = device(jnp.where(at_end, p, outer), y, c)

    tile = lax.rem(me + TILE_COLS // 2, n)
    column = lax.rem(tile, TILE_COLS)
    partner = lax.rem(me + TILE_COLS, n)
    sides = [(-1, column > 0), (1, column < TILE_COLS - 1)]
    half_way = TILE_COLS // 2
    crossing = {-1: column == half_way, 1: column == half_way - 1}

    def cols(j):
        return pl.ds(pl.multiple_of(j * wide, wide), wide)

    def lines(buf, s):
        return buf.at[pl.ds(pl.multiple_of(s * rows, rows), rows), :]

    loads = [
        pltpu.make_async_copy(k_ref, lines(keys, 1), own_sem.at[0]),
        pltpu.make_async_copy(v_ref, lines(vals, 1), own_sem.at[1]),
        pltpu.make_async_copy(first_ref, first, own_sem.at[2]),
        pltpu.make_async_copy(second_ref, second, own_sem.at[3]),
    ]
    for load in loads:
        load.start()

    barrier = pltpu.get_barrier_semaphore()
    others = [lax.rem(me + step, n) for step in range(1, n)]
    for target in others:
        pl.semaphore_signal(barrier, inc=1, device_id={"tile": target}, device_id_type=MESH)
    pl.semaphore_wait(barrier, n - 1)

    def beside_tile(side):
        return lax.rem(me + side + jnp.where(crossing[side], TILE_COLS, 0) + n, n)

    def slot_there(level, side):
        return jnp.where(crossing[side], 1 - level, level) * 3 + 1 - side

    bufs = (keys, vals)

    def place(i, s, j):
        return bufs[i].at[pl.ds(pl.multiple_of(s * rows, rows), rows), cols(j)]

    def over_vertical(i, j):
        return remote(
            (k_ref, v_ref)[i].at[:, cols(j)], place(i, 4, j), kv_send.at[i, j], kv_recv.at[8 + i, j], partner
        )

    def over_side(level, index, i, j):
        side = sides[index][0]
        there = slot_there(level, side)
        source = (k_ref, v_ref)[i].at[:, cols(j)] if level == 0 else place(i, 4, j)
        return remote(
            source,
            place(i, there, j),
            kv_send.at[2 + level * 4 + index * 2 + i, j],
            kv_recv.at[there * 2 + i, j],
            beside_tile(side),
        )

    def landed(ref, sem):
        remote(ref, ref, own_sem.at[0], sem, me).wait_recv()

    def send_own(j):
        for i in (0, 1):
            over_vertical(i, j).start()
        for i in (0, 1):
            for index, (_, exists) in enumerate(sides):
                when(exists, over_side(0, index, i, j).start)

    def send_vertical(j):
        for i in (0, 1):
            landed(place(i, 4, j), kv_recv.at[8 + i, j])
            for index, (_, exists) in enumerate(sides):
                when(exists, over_side(1, index, i, j).start)

    for j in range(min(2, chunks)):
        send_own(j)

    expert = lax.broadcasted_iota(jnp.int32, (8, rows), 0)
    named = [routes_ref[k : k + 1, :] == expert for k in (0, 1)]
    member = jnp.logical_or(named[0], named[1])
    upto = (
        lax.broadcasted_iota(jnp.int32, (rows, rows), 0) <= lax.broadcasted_iota(jnp.int32, (rows, rows), 1)
    ).astype(jnp.float32).astype(jnp.bfloat16)
    count = jnp.dot(
        member.astype(jnp.float32).astype(jnp.bfloat16), upto, preferred_element_type=jnp.float32
    )
    gate = sum(
        jnp.where(named[k], gates_ref[k : k + 1, :].astype(jnp.float32), 0.0) for k in (0, 1)
    )
    tables[me, 0:8, :] = jnp.where(member, count - 1.0, -1.0)
    tables[me, 8:16, :] = gate / 1024.0

    def tell(ref, send, recv):
        return [
            remote(ref.at[me], ref.at[me], send.at[step], recv.at[me], target)
            for step, target in enumerate(others)
        ]

    for copy in tell(tables, table_send, table_recv):
        copy.start()

    span = 6 * rows
    where = lax.broadcasted_iota(jnp.int32, (rows, span), 1)
    penalty = jnp.zeros((rows, span), jnp.float32)
    for s in range(6):
        for side, exists in sides:
            if side != s % 3 - 1:
                continue
            here = (where >= s * rows) & (where < (s + 1) * rows)
            penalty = jnp.where(here, jnp.where(exists, 0.0, MASKED), penalty)

            def clear(s=s):
                for buf in bufs:
                    buf[s * rows : (s + 1) * rows, :] = jnp.zeros((rows, D), buf.dtype)

            pl.when(jnp.logical_not(exists))(clear)
    bias[...] = penalty
    for load in loads[:2]:
        load.wait()
    for target in others:
        landed(tables.at[target], table_recv.at[target])

    slot_line = lax.broadcasted_iota(jnp.int32, (cap, rows), 0).astype(jnp.float32)

    def chosen(tile_there, e):
        return tables[tile_there, pl.ds(e, 1), :] == slot_line

    for plane in range(planes):
        for place_in, e in ((0, p), (1, outer_expert)):
            chooser[plane, place_in * cap : (place_in + 1) * cap, :] = (
                chosen(device(plane, y, c), e).astype(jnp.float32).astype(jnp.bfloat16)
            )

    scale = 1.0 / math.sqrt(HEAD_DIM)

    def attend(j):
        for level in (0, 1):
            for side, exists in sides:
                s = level * 3 + 1 + side
                for i in (0, 1):
                    when(exists, functools.partial(landed, place(i, s, j), kv_recv.at[s * 2 + i, j]))
        for extra in range(wide // HEAD_DIM):
            at = pl.ds(pl.multiple_of(j * wide + extra * HEAD_DIM, HEAD_DIM), HEAD_DIM)
            scores = lax.dot_general(
                q_ref[:, at], keys[:, at], (((1,), (1,)), ((), ())), preferred_element_type=jnp.float32
            )
            scores = scores * scale + bias[...]
            raised = jnp.exp(scores - jnp.max(scores, axis=-1, keepdims=True))
            probs = (raised * (1.0 / jnp.sum(raised, axis=-1, keepdims=True))).astype(jnp.bfloat16)
            att[:, at] = jnp.dot(probs, vals[:, at], preferred_element_type=jnp.float32).astype(att.dtype)

    def raw_copy(k, src, j):
        source = att.at[:, cols(j)] if k == 0 else line.at[src, :, cols(j)]
        return remote(source, line.at[src, :, cols(j)], out_send.at[k, 0, j], line_recv.at[src, j], inner_device)

    def outer_copy(k, src, j):
        there = device(src, y, c)
        return remote(
            stage.at[src, :, cols(j)],
            tokens.at[there, :, cols(j)],
            out_send.at[k, 1, j],
            token_recv.at[there, j],
            outer_device,
        )

    def plane_copy(k, src, j, index):
        ref = tokens.at[device(src, y, c), :, cols(j)]
        return remote(
            ref, ref, out_send.at[k, 2 + index, j], token_recv.at[device(src, y, c), j], (beside, twin)[index]
        )

    def twin_copy(k, src, j):
        there = device(src, 1 - y, c)
        ref = tokens.at[there, :, cols(j)]
        return remote(ref, ref, out_send.at[k, 4, j], token_recv.at[there, j], twin)

    far = jnp.where(at_end, p + 3 * toward, p + 2 * toward)
    second_plane = jnp.where(at_end, p + 2 * toward, outer)
    sources = [
        (p, 1, True, middle),
        (inner, 2, False, middle),
        (second_plane, jnp.where(at_end, 3, 2), middle, False),
        (far, jnp.where(at_end, 4, 3), False, middle),
    ]

    def relay(k, j):
        src, behind, whole, out = sources[k]
        jj = j - behind

        def go():
            there = device(src, y, c)
            if k > 0:
                pl.when(at_end)(
                    lambda: landed(tokens.at[there, :, cols(jj)], token_recv.at[there, jj])
                )
                pl.when(middle)(lambda: landed(line.at[src, :, cols(jj)], line_recv.at[src, jj]))
            if whole is not False:
                when(whole, raw_copy(k, src, jj).start)

            def pick():
                rows_here = att[:, cols(jj)] if k == 0 else line[src, :, cols(jj)]
                picked = jnp.dot(chooser[src], rows_here, preferred_element_type=jnp.float32).astype(
                    tokens.dtype
                )
                tokens[there, :, cols(jj)] = picked[:cap]
                stage[src, :, cols(jj)] = picked[cap:]

            when(True if k == 0 else middle, pick)
            if out is not False:
                when(out, outer_copy(k, src, jj).start)
            for index in (0, 1):
                plane_copy(k, src, jj, index).start()

        pl.when(jnp.logical_and(jj >= 0, jj < chunks))(go)

    def pass_on(k, j):
        src, behind, _, _ = sources[k]
        jj = j - behind - 1

        def go():
            there = device(src, 1 - y, c)
            landed(tokens.at[there, :, cols(jj)], token_recv.at[there, jj])
            twin_copy(k, src, jj).start()

        pl.when(jnp.logical_and(jj >= 0, jj < chunks))(go)

    def move(j):
        for k in range(planes):
            relay(k, j)
        for k in range(planes):
            pass_on(k, j)

    def stream(j, carry):
        pl.when(j + 2 < chunks)(lambda: send_own(j + 2))
        pl.when(j < chunks)(lambda: send_vertical(j))
        pl.when(j >= 1)(lambda: attend(j - 1))
        move(j)
        return carry

    lax.fori_loop(0, chunks + 1, stream, 0)

    token = lax.broadcasted_iota(jnp.int32, (16, rows), 1)
    line_of = lax.broadcasted_iota(jnp.int32, (16, rows), 0)
    mean_row = jnp.zeros((1, rows), jnp.float32)
    rate_row = jnp.zeros((1, rows), jnp.float32)
    for step in range(rows // 16):
        some = att[step * 16 : (step + 1) * 16, :].astype(jnp.float32)
        mean = jnp.mean(some, axis=-1, keepdims=True)
        some = some - mean
        rate = lax.rsqrt(jnp.mean(some * some, axis=-1, keepdims=True) + EPSILON)
        same = token == line_of + step * 16
        mean_row = mean_row + jnp.sum(jnp.where(same, mean, 0.0), axis=0, keepdims=True)
        rate_row = rate_row + jnp.sum(jnp.where(same, rate, 0.0), axis=0, keepdims=True)
    stats[me] = jnp.where(lax.broadcasted_iota(jnp.int32, (8, rows), 0) == 0, mean_row, rate_row)
    for copy in tell(stats, stat_send, stat_recv):
        copy.start()

    def drain(j, carry):
        move(j)
        return carry

    lax.fori_loop(chunks + 1, chunks + 5, drain, 0)
    for target in others:
        landed(stats.at[target], stat_recv.at[target])
    for load in loads[2:]:
        load.wait()

    order = [
        jnp.where(at_end, p + 3 * toward, p + 2 * toward),
        jnp.where(at_end, p + 2 * toward, inner),
        jnp.where(at_end, inner, outer),
        p,
    ]
    group = SPLIT * cap
    chunk = min(width, 256)
    chunk_out = 512

    def block(buf, index):
        return buf.at[pl.ds(pl.multiple_of(index * cap, 16), cap), :]

    def picked_column(tile_there, row):
        return jnp.sum(jnp.where(chosen(tile_there, p), row, 0.0), axis=1, keepdims=True)

    def compute(i):
        plane = order[i]

        def arrive(j, carry):
            for yy in (0, 1):
                there = device(plane, yy, 1 - c)
                landed(tokens.at[there, :, cols(j)], token_recv.at[there, j])
            return carry

        lax.fori_loop(0, chunks, arrive, 0)

        def normalise(t, carry):
            there = plane * SPLIT + t
            mean = picked_column(there, stats[there, 0:1, :])
            rate = picked_column(there, stats[there, 1:2, :])
            at = pl.ds(pl.multiple_of(t * cap, 16), cap)
            for step in range(D // chunk_out):
                some = slice(step * chunk_out, (step + 1) * chunk_out)
                value = (tokens[there, :, some].astype(jnp.float32) - mean) * rate
                normed[at, some] = (value * (1.0 + mod_ref[1:2, some]) + mod_ref[0:1, some]).astype(
                    normed.dtype
                )
            return carry

        lax.fori_loop(0, SPLIT, normalise, 0)

        def one(step, carry):
            at = pl.ds(pl.multiple_of(step * chunk, chunk), chunk)
            raw = jnp.dot(normed[...], first[:, at], preferred_element_type=jnp.float32)
            hidden[:, at] = jax.nn.gelu(raw, approximate=True).astype(hidden.dtype)
            return carry

        lax.fori_loop(0, width // chunk, one, 0)
        mine = pl.ds(pl.multiple_of(plane * group, 16), group)

        def two(step, carry):
            at = pl.ds(pl.multiple_of(step * chunk_out, chunk_out), chunk_out)
            raw = jnp.dot(hidden[...], second[:, at], preferred_element_type=jnp.float32)
            part[mine, at] = raw.astype(part.dtype)
            return carry

        lax.fori_loop(0, D // chunk_out, two, 0)
        for yy in (0, 1):
            to_twin(i, yy).start()

    def to_twin(i, yy):
        plane = order[i]
        return remote(
            block(part, device(plane, yy, 1 - c)),
            block(r1, plane * 2 + yy),
            back_send.at[i, yy],
            s1_recv.at[plane, yy],
            twin,
        )

    def to_beside(i):
        plane = order[i]
        return remote(
            block(part, device(plane, 1 - y, c)), block(r2, plane), back_send.at[i, 2], s2_recv.at[plane], beside
        )

    def fold_twin(i):
        plane = order[i]
        for yy in (1 - y, y):
            landed(block(r1, plane * 2 + yy), s1_recv.at[plane, yy])
            base = device(plane, yy, c) * cap
            from_there = (plane * 2 + yy) * cap

            def body(step, carry):
                at = pl.ds(pl.multiple_of(base + step * 16, 16), 16)
                extra = r1[pl.ds(pl.multiple_of(from_there + step * 16, 16), 16), :]
                part[at, :] = (part[at, :].astype(jnp.float32) + extra.astype(jnp.float32)).astype(part.dtype)
                return carry

            lax.fori_loop(0, cap // 16, body, 0)
            if yy is not y:
                to_beside(i).start()

    def fold_beside(i):
        plane = order[i]
        there = device(plane, y, c)
        landed(block(r2, plane), s2_recv.at[plane])
        weight = picked_column(there, tables[there, pl.ds(8 + p, 1), :])
        ours = pl.ds(pl.multiple_of(there * cap, 16), cap)
        theirs = pl.ds(pl.multiple_of(plane * cap, 16), cap)
        for step in range(D // chunk_out):
            some = slice(step * chunk_out, (step + 1) * chunk_out)
            total = part[ours, some].astype(jnp.float32) + r2[theirs, some].astype(jnp.float32)
            pair[plane, :cap, some] = (total * weight).astype(pair.dtype)

    def slots_home(i):
        plane = order[i]
        return remote(
            pair.at[plane, pl.ds(0, cap), :],
            pair.at[plane, pl.ds(cap, cap), :],
            back_send.at[i, 3],
            pair_recv.at[plane],
            inner_device,
        )

    def rows_home(i):
        plane = order[i]
        return remote(
            acc_out.at[plane],
            acc_in.at[plane],
            back_send.at[i, 3],
            acc_recv.at[plane],
            outer_device if i == 2 else inner_device,
        )

    def spread_out(plane, both, at):
        amount = 2 * cap if both else cap
        return lax.dot_general(
            chooser[plane, :amount, :],
            pair[plane, :amount, at],
            (((0,), (0,)), ((), ())),
            preferred_element_type=jnp.float32,
        )

    def fold_home(i):
        plane = order[i]

        def fold(both, extra, last):
            if both:
                landed(pair.at[plane, pl.ds(cap, cap), :], pair_recv.at[plane])
            if extra:
                landed(acc_in.at[plane], acc_recv.at[plane])

            def body(step, carry):
                at = pl.ds(pl.multiple_of(step * chunk_out, chunk_out), chunk_out)
                total = spread_out(plane, both, at)
                if extra:
                    total = total + acc_in[plane, :, at].astype(jnp.float32)
                if last:
                    out_ref[:, at] = (att[:, at].astype(jnp.float32) + mod_ref[2:3, at] * total).astype(
                        out_ref.dtype
                    )
                else:
                    acc_out[plane, :, at] = total.astype(acc_out.dtype)
                return carry

            lax.fori_loop(0, D // chunk_out, body, 0)
            if not last:
                rows_home(i).start()

        if i == 3:
            pl.when(at_end)(lambda: fold(False, True, True))
            pl.when(middle)(lambda: fold(True, True, True))
        else:
            pl.when(at_end)(slots_home(i).start)
            pl.when(middle)(lambda: fold(i < 2, i == 2, False))

    for i in range(planes):
        compute(i)
        fold_twin(i)
        if i > 0:
            fold_beside(i - 1)
            fold_home(i - 1)
    fold_beside(planes - 1)
    fold_home(planes - 1)

    def left(j, carry):
        for i in (0, 1):
            over_vertical(i, j).wait_send()
            for level in (0, 1):
                for index, (_, exists) in enumerate(sides):
                    when(exists, over_side(level, index, i, j).wait_send)
        for k, (src, _, whole, out) in enumerate(sources):
            if whole is not False:
                when(whole, raw_copy(k, src, j).wait_send)
            if out is not False:
                when(out, outer_copy(k, src, j).wait_send)
            for index in (0, 1):
                plane_copy(k, src, j, index).wait_send()
            twin_copy(k, src, j).wait_send()
        return carry

    lax.fori_loop(0, chunks, left, 0)
    for copy in tell(tables, table_send, table_recv) + tell(stats, stat_send, stat_recv):
        copy.wait_send()
    for i in range(planes):
        for yy in (0, 1):
            to_twin(i, yy).wait_send()
        to_beside(i).wait_send()
        if i < planes - 1:
            pl.when(at_end)(slots_home(i).wait_send)
            pl.when(middle)(rows_home(i).wait_send)


def kernel_bytes(n, rows, cap, width):
    planes = n // SPLIT
    lines = 2 * 6 * rows + 2 * n * cap + planes * (6 * cap + 3 * rows) + SPLIT * cap + 3 * rows
    return 2 * (lines * D + 2 * width * D)


def layer(queries, key_rows, values, modulation, expert_in, expert_out, routes, gate_fixed):
    n = lax.axis_size("tile")
    rows = queries.shape[0]
    width = expert_in.shape[1]
    planes = n // SPLIT
    cap = 3 * rows // planes
    chunks = 8
    vmem = pl.BlockSpec(memory_space=pltpu.VMEM)
    hbm = pl.BlockSpec(memory_space=pl.ANY)
    dma = pltpu.SemaphoreType.DMA
    bf = jnp.bfloat16
    return pl.pallas_call(
        functools.partial(layer_kernel, n, rows, cap, chunks),
        name="whole_layer",
        out_shape=jax.ShapeDtypeStruct((rows, D), bf),
        in_specs=[vmem, hbm, hbm, vmem, vmem, vmem, hbm, hbm],
        out_specs=vmem,
        scratch_shapes=[
            pltpu.VMEM((rows, D), bf),
            pltpu.VMEM((rows, 6 * rows), jnp.float32),
            pltpu.VMEM((6 * rows, D), bf),
            pltpu.VMEM((6 * rows, D), bf),
            pltpu.VMEM((planes, rows, D), bf),
            pltpu.VMEM((n, cap, D), bf),
            pltpu.VMEM((planes, cap, D), bf),
            pltpu.VMEM((planes, 2 * cap, rows), bf),
            pltpu.VMEM((n, 16, rows), jnp.float32),
            pltpu.VMEM((n, 8, rows), jnp.float32),
            pltpu.VMEM((SPLIT * cap, D), bf),
            pltpu.VMEM((D, width), bf),
            pltpu.VMEM((width, D), bf),
            pltpu.VMEM((SPLIT * cap, width), bf),
            pltpu.VMEM((n * cap, D), bf),
            pltpu.VMEM((planes * 2 * cap, D), bf),
            pltpu.VMEM((planes * cap, D), bf),
            pltpu.VMEM((planes, 2 * cap, D), bf),
            pltpu.VMEM((planes, rows, D), bf),
            pltpu.VMEM((planes, rows, D), bf),
            dma((4,)),
            dma((10, chunks)),
            dma((12, chunks)),
            dma((n - 1,)),
            dma((n,)),
            dma((n - 1,)),
            dma((n,)),
            dma((planes, 5, chunks)),
            dma((planes, chunks)),
            dma((n, chunks)),
            dma((planes, 4)),
            dma((planes, 2)),
            dma((planes,)),
            dma((planes,)),
            dma((planes,)),
        ],
        compiler_params=pltpu.CompilerParams(
            collective_id=1, has_side_effects=True, vmem_limit_bytes=VMEM_LIMIT
        ),
    )(queries, key_rows, values, modulation, routes.T, gate_fixed.T, expert_in, expert_out)


def slot_table(flat, experts_count):
    onehot = (flat[:, None] == jnp.arange(experts_count, dtype=jnp.int32)[None, :]).astype(
        jnp.int32
    )
    before = jnp.cumsum(onehot, axis=0) - onehot
    return jnp.sum(before * onehot, axis=1)


def expert_apply(rows, first_weight, second_weight):
    hidden = jax.nn.gelu(
        jnp.dot(rows, first_weight, preferred_element_type=jnp.float32), approximate=True
    ).astype(jnp.bfloat16)
    return jnp.dot(hidden, second_weight, preferred_element_type=jnp.float32).astype(jnp.bfloat16)


def experts_sparse(normed, attended, modulation, expert_in, expert_out, routes, gate_fixed):
    devices = lax.axis_size("tile")
    rows_dev = normed.shape[0]
    experts_count = devices // SPLIT
    capacity = 3 * rows_dev // experts_count
    flat = routes.reshape(-1)
    slots = slot_table(flat, experts_count)
    target = flat * capacity + slots
    chooser = (
        target[None, :] == jnp.arange(experts_count * capacity, dtype=jnp.int32)[:, None]
    ).astype(jnp.bfloat16)
    chooser = chooser.reshape(experts_count * capacity, rows_dev, 2).sum(axis=2)
    buffer = jnp.dot(chooser, normed, preferred_element_type=jnp.float32).astype(jnp.bfloat16)
    copies = jnp.broadcast_to(
        buffer.reshape(experts_count, 1, capacity, D), (experts_count, SPLIT, capacity, D)
    ).reshape(devices, capacity, D)
    received = lax.all_to_all(copies, "tile", split_axis=0, concat_axis=0, tiled=True)
    sources = received.shape[0]
    count = received.shape[1]
    partial_value = expert_apply(received.reshape(sources * count, D), expert_in, expert_out)
    returned = lax.all_to_all(
        partial_value.reshape(sources, count, D), "tile", split_axis=0, concat_axis=0, tiled=True
    )
    summed = jnp.sum(
        returned.reshape(experts_count, SPLIT, capacity, D).astype(jnp.float32), axis=1
    )
    expert_rows = summed.astype(jnp.bfloat16).reshape(experts_count * capacity, D)
    picked = jnp.take(expert_rows, target, axis=0).reshape(rows_dev, 2, D)
    gate_scale = gate_fixed.astype(jnp.float32) / 1024.0
    mixture = jnp.sum(picked.astype(jnp.float32) * gate_scale[:, :, None], axis=1)
    return (attended.astype(jnp.float32) + modulation[2] * mixture).astype(jnp.bfloat16)


def shards(queries, key_rows, values, modulation, expert_in, expert_out, routes, gate_fixed):
    n = lax.axis_size("tile")
    cap = 3 * queries.shape[0] // (n // SPLIT)
    if n == 2 * TILE_COLS and cap % 16 == 0 and kernel_bytes(n, queries.shape[0], cap, expert_in.shape[1]) < VMEM_LIMIT * 7 // 8:
        return layer(queries, key_rows, values, modulation, expert_in, expert_out, routes, gate_fixed)
    attended, normed = attention(queries, key_rows, values, modulation)
    return experts_sparse(normed, attended, modulation, expert_in, expert_out, routes, gate_fixed)


def solution(mesh):
    placed = (
        P(("groups", "tile"), None),
        P(("groups", "tile"), None),
        P(("groups", "tile"), None),
        P("groups", None),
        P(None, "tile"),
        P("tile", None),
        P(("groups", "tile"), None),
        P(("groups", "tile"), None),
    )
    return jax.shard_map(
        shards, mesh=mesh, in_specs=placed, out_specs=P(("groups", "tile"), None), check_vma=False
    )
```

```python
import functools
import math

import jax
import jax.numpy as jnp
from jax import lax
from jax.experimental import pallas as pl
from jax.experimental.pallas import tpu as pltpu
from jax.sharding import PartitionSpec as P

HEAD_DIM = 128
D = 4096
SPLIT = 4
TILE_COLS = 8

EPSILON = 1e-06
MASKED = -1e30
MESH = pl.DeviceIdType.MESH
VMEM_LIMIT = 60 * 1024 * 1024
CHUNKS = 8
AHEAD = 2
BEHIND = 1
HOP = 1


def when(cond, body):
    if cond is True:
        body()
    else:
        pl.when(cond)(body)


def both(a, b):
    if a is True:
        return b
    if b is True:
        return a
    return jnp.logical_and(a, b)


def remote(src, dst, send_sem, recv_sem, target):
    return pltpu.make_async_remote_copy(
        src_ref=src,
        dst_ref=dst,
        send_sem=send_sem,
        recv_sem=recv_sem,
        device_id={"tile": target},
        device_id_type=MESH,
    )


def halo_levels(n):
    grid_rows = n // TILE_COLS
    if grid_rows < 2:
        return 1
    return 2 if grid_rows == 2 else 3


def attention_kernel(
    n, rows, q_ref, k_ref, v_ref, mod_ref, att_ref, norm_ref, keys, vals, send_sem, recv_sem, own_sem,
):
    me = lax.axis_index("tile")
    grid_rows = n // TILE_COLS
    tile = lax.rem(me + TILE_COLS // 2, n)
    row = lax.div(tile, TILE_COLS)
    col = lax.rem(tile, TILE_COLS)
    if grid_rows < 2:
        verticals = []
    elif grid_rows == 2:
        verticals = [(1, TILE_COLS, True, 1)]
    else:
        verticals = [(1, n - TILE_COLS, row > 0, 2), (2, TILE_COLS, row < grid_rows - 1, 1)]
    sides = [(-1, col > 0), (1, col < TILE_COLS - 1)]
    here = {level: exists for level, _, exists, _ in verticals}
    here[0] = True

    def slot(level, side):
        return level * 3 + 1 + side

    def place(buf, s):
        return buf.at[pl.ds(s * rows, rows), :]

    def over(offset):
        return lax.rem(me + offset + n, n)

    half = rows // 2
    middle = TILE_COLS // 2
    crossing = {side: col == (middle if side < 0 else middle - 1) for side, _ in sides}
    two = grid_rows == 2

    def part_of(buf, s, h):
        return buf.at[pl.ds(pl.multiple_of(s * rows + h * half, half), half), :]

    own = [
        pltpu.make_async_copy(src, place(buf, slot(0, 0)), own_sem.at[i])
        for i, (src, buf) in enumerate(((k_ref, keys), (v_ref, vals)))
    ]
    for copy in own:
        copy.start()

    def beside(side):
        if not two:
            return over(side)
        return jnp.where(crossing[side], over(side + TILE_COLS), over(side))

    def level_there(level, side):
        return jnp.where(crossing[side], 1 - level, level) if two else level

    barrier = pltpu.get_barrier_semaphore()
    partners = [(over(offset), exists) for _, offset, exists, _ in verticals]
    partners += [(beside(side), exists) for side, exists in sides]
    for target, exists in partners:

        def greet(target=target):
            pl.semaphore_signal(barrier, inc=1, device_id={"tile": target}, device_id_type=MESH)

        when(exists, greet)
    expected = sum(1 if exists is True else jnp.where(exists, 1, 0) for _, exists in partners)
    pl.semaphore_wait(barrier, expected)

    sends = []
    pieces = [(i, h) for i in (0, 1) for h in (0, 1)]
    bufs = (keys, vals)

    def push(i, h, src, there, target, exists):
        copy = remote(
            src,
            part_of(bufs[i], there, h),
            send_sem.at[len(sends)],
            recv_sem.at[there, i * 2 + h],
            target,
        )
        when(exists, copy.start)
        sends.append((copy, exists))

    def arrived(s, exists, i, h):
        ref = part_of(bufs[i], s, h)
        when(exists, remote(ref, ref, send_sem.at[0], recv_sem.at[s, i * 2 + h], me).wait_recv)

    def own_part(i, h):
        return (k_ref, v_ref)[i].at[pl.ds(h * half, half), :]

    for i, h in pieces:
        for level, offset, exists, there in verticals:
            push(i, h, own_part(i, h), slot(there, 0), over(offset), exists)
    for i, h in pieces:
        for side, exists in sides:
            push(i, h, own_part(i, h), slot(level_there(0, side), -side), beside(side), exists)
    for s in range(3 * (1 + len(verticals))):
        level, side = s // 3, s % 3 - 1
        exists = here[level]
        for other, side_exists in sides:
            if other == side:
                exists = both(exists, side_exists)
        if exists is True:
            continue

        def clear(s=s):
            for buf in (keys, vals):
                buf[pl.ds(s * rows, rows), :] = jnp.zeros((rows, D), buf.dtype)

        pl.when(jnp.logical_not(exists))(clear)
    for i, h in pieces:
        for level, offset, exists, there in verticals:
            arrived(slot(level, 0), exists, i, h)
            for side, side_exists in sides:
                push(
                    i,
                    h,
                    part_of(bufs[i], slot(level, 0), h),
                    slot(level_there(level, side), -side),
                    beside(side),
                    both(exists, side_exists),
                )
    for copy in own:
        copy.wait()
    for i, h in pieces:
        for level, exists in sorted(here.items(), key=lambda item: item[0]):
            for side, side_exists in sides:
                arrived(slot(level, side), both(exists, side_exists), i, h)

    span = 3 * (1 + len(verticals)) * rows
    where = lax.broadcasted_iota(jnp.int32, (rows, span), 1)
    bias = jnp.zeros((rows, span), jnp.float32)
    for s in range(span // rows):
        level, side = s // 3, s % 3 - 1
        exists = here[level]
        for other, side_exists in sides:
            if other == side:
                exists = both(exists, side_exists)
        if exists is True:
            continue
        penalty = jnp.where(exists, 0.0, MASKED)
        bias = jnp.where((where >= s * rows) & (where < (s + 1) * rows), penalty, bias)
    scale = 1.0 / math.sqrt(HEAD_DIM)
    together = 8

    def heads(step, carry):
        for extra in range(together):
            at = pl.ds(pl.multiple_of((step * together + extra) * HEAD_DIM, HEAD_DIM), HEAD_DIM)
            scores = lax.dot_general(
                q_ref[:, at], keys[:, at], (((1,), (1,)), ((), ())), preferred_element_type=jnp.float32
            )
            scores = scores * scale + bias
            raised = jnp.exp(scores - jnp.max(scores, axis=-1, keepdims=True))
            probs = (raised * (1.0 / jnp.sum(raised, axis=-1, keepdims=True))).astype(jnp.bfloat16)
            att_ref[:, at] = jnp.dot(probs, vals[:, at], preferred_element_type=jnp.float32).astype(
                att_ref.dtype
            )
        return carry

    lax.fori_loop(0, D // HEAD_DIM // together, heads, 0)

    def normalise(step, carry):
        at = pl.ds(pl.multiple_of(step * 16, 16), 16)
        wide = att_ref[at, :].astype(jnp.float32)
        wide = wide - jnp.mean(wide, axis=-1, keepdims=True)
        spread = jnp.mean(wide * wide, axis=-1, keepdims=True)
        normed = wide * lax.rsqrt(spread + EPSILON)
        norm_ref[at, :] = (normed * (1.0 + mod_ref[1:2, :]) + mod_ref[0:1, :]).astype(norm_ref.dtype)
        return carry

    lax.fori_loop(0, rows // 16, normalise, 0)
    for copy, exists in sends:
        when(exists, copy.wait_send)


def attention(queries, key_rows, values, modulation):
    n = lax.axis_size("tile")
    rows = queries.shape[0]
    levels = halo_levels(n)
    slots = 3 * levels
    vmem = pl.BlockSpec(memory_space=pltpu.VMEM)
    hbm = pl.BlockSpec(memory_space=pl.ANY)
    return pl.pallas_call(
        functools.partial(attention_kernel, n, rows),
        name="halo_attention",
        out_shape=(
            jax.ShapeDtypeStruct((rows, D), jnp.bfloat16),
            jax.ShapeDtypeStruct((rows, D), jnp.bfloat16),
        ),
        in_specs=[vmem, hbm, hbm, vmem],
        out_specs=(vmem, vmem),
        scratch_shapes=[
            pltpu.VMEM((slots * rows, D), jnp.bfloat16),
            pltpu.VMEM((slots * rows, D), jnp.bfloat16),
            pltpu.SemaphoreType.DMA((4 * (2 + 3 * (levels - 1)),)),
            pltpu.SemaphoreType.DMA((slots, 4)),
            pltpu.SemaphoreType.DMA((2,)),
        ],
        compiler_params=pltpu.CompilerParams(
            collective_id=0, has_side_effects=True, vmem_limit_bytes=VMEM_LIMIT
        ),
    )(queries, key_rows, values, modulation)


def device(plane, yy, cc):
    return plane * SPLIT + yy * 2 + cc


def layer_kernel(
    n, rows, cap, chunks, q_ref, k_ref, v_ref, mod_ref, routes_ref, gates_ref, first_ref, second_ref,
    out_ref, att, asked, bias, keys, vals, line, tokens, stage, chooser, spreader, tables, stats, normed,
    first, second, hidden, part, r1, r2, pair, acc_in, acc_out,
    own_sem, kv_send, kv_recv, table_send, table_recv, stat_send, stat_recv, out_send, line_recv,
    token_recv, rest_send, back_send, s1_recv, s2_recv, pair_recv, acc_recv,
):
    planes = n // SPLIT
    width = first.shape[1]
    half = D // 2
    wide = half // chunks
    me = lax.axis_index("tile")
    p = lax.div(me, SPLIT)
    y = lax.div(lax.rem(me, SPLIT), 2)
    c = lax.rem(me, 2)
    beside = device(p, 1 - y, c)
    twin = device(p, y, 1 - c)
    low_half = p < planes // 2
    toward = jnp.where(low_half, 1, -1)
    inner = p + toward
    outer = p - toward
    at_end = jnp.logical_or(p == 0, p == planes - 1)
    middle = jnp.logical_not(at_end)
    outer_expert = jnp.where(low_half, 0, planes - 1)
    inner_device = device(inner, y, c)
    outer_device = device(jnp.where(at_end, p, outer), y, c)

    tile = lax.rem(me + TILE_COLS // 2, n)
    column = lax.rem(tile, TILE_COLS)
    partner = lax.rem(me + TILE_COLS, n)
    sides = [(-1, column > 0), (1, column < TILE_COLS - 1)]
    half_way = TILE_COLS // 2
    crossing = {-1: column == half_way, 1: column == half_way - 1}

    def part_of_plane(plane):
        return jnp.where(plane < planes // 2, half, 0)

    mine_from = part_of_plane(p)
    other_from = half - mine_from
    partner_plane = lax.rem(p + planes // 2, planes)

    def cols(j, base=0):
        return pl.ds(pl.multiple_of(base + j * wide, wide), wide)

    def halves(base):
        return pl.ds(pl.multiple_of(base, half), half)

    def lines(buf, s):
        return buf.at[pl.ds(pl.multiple_of(s * rows, rows), rows), :]

    loads = [
        pltpu.make_async_copy(q_ref.at[:, halves(mine_from)], lines(asked, 0), own_sem.at[0]),
        pltpu.make_async_copy(k_ref.at[:, halves(mine_from)], lines(keys, 1), own_sem.at[1]),
        pltpu.make_async_copy(v_ref.at[:, halves(mine_from)], lines(vals, 1), own_sem.at[2]),
        pltpu.make_async_copy(first_ref, first, own_sem.at[3]),
        pltpu.make_async_copy(second_ref, second, own_sem.at[4]),
    ]
    for load in loads:
        load.start()

    barrier = pltpu.get_barrier_semaphore()
    others = [lax.rem(me + step, n) for step in range(1, n)]
    for target in others:
        pl.semaphore_signal(barrier, inc=1, device_id={"tile": target}, device_id_type=MESH)
    pl.semaphore_wait(barrier, n - 1)

    def beside_tile(side):
        return lax.rem(me + side + jnp.where(crossing[side], TILE_COLS, 0) + n, n)

    def slot_there(level, side):
        return jnp.where(crossing[side], 1 - level, level) * 3 + 1 - side

    bufs = (keys, vals, asked)
    given = (k_ref, v_ref, q_ref)

    def place(i, s, j):
        return bufs[i].at[pl.ds(pl.multiple_of(s * rows, rows), rows), cols(j)]

    def over_vertical(i, j):
        return remote(
            given[i].at[:, cols(j, other_from)],
            place(i, 4 if i < 2 else 1, j),
            kv_send.at[i, j],
            kv_recv.at[8 + i if i < 2 else 12, j],
            partner,
        )

    def over_side(level, index, i, j):
        side = sides[index][0]
        there = slot_there(level, side)
        source = given[i].at[:, cols(j, mine_from)] if level == 0 else place(i, 4, j)
        return remote(
            source,
            place(i, there, j),
            kv_send.at[3 + level * 4 + index * 2 + i, j],
            kv_recv.at[there * 2 + i, j],
            beside_tile(side),
        )

    def landed(ref, sem):
        remote(ref, ref, own_sem.at[0], sem, me).wait_recv()

    def send_own(j):
        for i in range(3):
            over_vertical(i, j).start()

    def send_side(j):
        for i in (0, 1):
            for index, (_, exists) in enumerate(sides):
                when(exists, over_side(0, index, i, j).start)

    def send_vertical(j):
        for i in (0, 1):
            landed(place(i, 4, j), kv_recv.at[8 + i, j])
            for index, (_, exists) in enumerate(sides):
                when(exists, over_side(1, index, i, j).start)

    for j in range(min(AHEAD, chunks)):
        send_own(j)
        send_side(j)

    expert = lax.broadcasted_iota(jnp.int32, (8, rows), 0)
    named = [routes_ref[k : k + 1, :] == expert for k in (0, 1)]
    member = jnp.logical_or(named[0], named[1])
    upto = (
        lax.broadcasted_iota(jnp.int32, (rows, rows), 0) <= lax.broadcasted_iota(jnp.int32, (rows, rows), 1)
    ).astype(jnp.float32).astype(jnp.bfloat16)
    count = jnp.dot(
        member.astype(jnp.float32).astype(jnp.bfloat16), upto, preferred_element_type=jnp.float32
    )
    gate = sum(
        jnp.where(named[k], gates_ref[k : k + 1, :].astype(jnp.float32), 0.0) for k in (0, 1)
    )
    tables[me, 0:8, :] = jnp.where(member, count - 1.0, -1.0)
    tables[me, 8:16, :] = gate / 1024.0

    def tell(ref, send, recv):
        return [
            remote(ref.at[me], ref.at[me], send.at[step], recv.at[me], target)
            for step, target in enumerate(others)
        ]

    for copy in tell(tables, table_send, table_recv):
        copy.start()

    span = 6 * rows
    where = lax.broadcasted_iota(jnp.int32, (8, span), 1)
    penalty = jnp.zeros((8, span), jnp.float32)
    for s in range(6):
        for side, exists in sides:
            if side != s % 3 - 1:
                continue
            here = (where >= s * rows) & (where < (s + 1) * rows)
            penalty = jnp.where(here, jnp.where(exists, 0.0, MASKED), penalty)

            def clear(s=s):
                for buf in (keys, vals):
                    buf[s * rows : (s + 1) * rows, :] = jnp.zeros((rows, half), buf.dtype)

            pl.when(jnp.logical_not(exists))(clear)
    bias[...] = penalty
    for load in loads[:3]:
        load.wait()

    slot_line = lax.broadcasted_iota(jnp.int32, (cap, rows), 0).astype(jnp.float32)

    def chosen(tile_there, e):
        return tables[tile_there, pl.ds(e, 1), :] == slot_line

    def choose():
        for target in others:
            landed(tables.at[target], table_recv.at[target])
        chooser[...] = jnp.zeros(chooser.shape, chooser.dtype)
        for plane in range(planes):
            for place_in, e in ((0, p), (1, outer_expert)):
                found = chosen(device(plane, y, c), e).astype(jnp.float32).astype(jnp.bfloat16)
                at = place_in * 2 * cap
                spreader[plane, place_in * cap : (place_in + 1) * cap, :] = found
                chooser[plane, at : at + cap, :rows] = found
                chooser[(plane + planes // 2) % planes, at + cap : at + 2 * cap, rows:] = found

    scale = 1.0 / math.sqrt(HEAD_DIM)

    def attend(j):
        for level in (0, 1):
            for side, exists in sides:
                s = level * 3 + 1 + side
                for i in (0, 1):
                    when(exists, functools.partial(landed, place(i, s, j), kv_recv.at[s * 2 + i, j]))
        landed(place(2, 1, j), kv_recv.at[12, j])
        for extra in range(wide // HEAD_DIM):
            at = pl.ds(pl.multiple_of(j * wide + extra * HEAD_DIM, HEAD_DIM), HEAD_DIM)
            scores = lax.dot_general(
                asked[:, at], keys[:, at], (((1,), (1,)), ((), ())), preferred_element_type=jnp.float32
            )
            scores = scores * scale + bias[0:1, :]
            raised = jnp.exp(scores - jnp.max(scores, axis=-1, keepdims=True))
            probs = (raised * (1.0 / jnp.sum(raised, axis=-1, keepdims=True))).astype(jnp.bfloat16)
            att[:, at] = jnp.dot(probs, vals[:, at], preferred_element_type=jnp.float32).astype(att.dtype)

    def raw_copy(k, src, j):
        source = att.at[:, cols(j)] if k == 0 else line.at[src, :, cols(j)]
        return remote(source, line.at[src, :, cols(j)], out_send.at[k, 0, j], line_recv.at[src, j], inner_device)

    def outer_copy(k, src, j):
        there = device(src, y, c)
        return remote(
            stage.at[src, :, cols(j)],
            tokens.at[there, :, cols(j)],
            out_send.at[k, 1, j],
            token_recv.at[there, j],
            outer_device,
        )

    def rest_copy(src, j):
        ref = line.at[src, pl.ds(rows, rows), cols(j)]
        return remote(ref, ref, rest_send.at[j], line_recv.at[src, j], outer_device)

    def rest_landed(j):
        landed(line.at[partner_plane, pl.ds(rows, rows), cols(j)], line_recv.at[partner_plane, j])

    def plane_copy(k, src, j, index):
        ref = tokens.at[device(src, y, c), :, cols(j)]
        return remote(
            ref, ref, out_send.at[k, 2 + index, j], token_recv.at[device(src, y, c), j], (beside, twin)[index]
        )

    def twin_copy(k, src, j):
        there = device(src, 1 - y, c)
        ref = tokens.at[there, :, cols(j)]
        return remote(ref, ref, out_send.at[k, 4, j], token_recv.at[there, j], twin)

    far = jnp.where(at_end, p + 3 * toward, p + 2 * toward)
    second_plane = jnp.where(at_end, p + 2 * toward, outer)
    sources = [
        (p, BEHIND, True, middle),
        (inner, BEHIND + HOP, False, middle),
        (second_plane, BEHIND + HOP * jnp.where(at_end, 2, 1), middle, False),
        (far, BEHIND + HOP * jnp.where(at_end, 3, 2), False, middle),
    ]

    def relay(k, j):
        src, behind, whole, out = sources[k]
        jj = j - behind

        def go():
            there = device(src, y, c)
            if k > 0:
                pl.when(at_end)(
                    lambda: landed(tokens.at[there, :, cols(jj)], token_recv.at[there, jj])
                )
                pl.when(middle)(lambda: landed(line.at[src, :, cols(jj)], line_recv.at[src, jj]))
            if whole is not False:
                when(whole, raw_copy(k, src, jj).start)
            if k == 1:
                pl.when(middle)(rest_copy(src, jj).start)

            def pick():
                rows_here = att[:, cols(jj)] if k == 0 else line[src, :, cols(jj)]
                picked = jnp.dot(chooser[src], rows_here, preferred_element_type=jnp.float32).astype(
                    tokens.dtype
                )
                tokens[there, :, cols(jj)] = picked[: 2 * cap]
                stage[src, :, cols(jj)] = picked[2 * cap :]

            when(True if k == 0 else middle, pick)
            if out is not False:
                when(out, outer_copy(k, src, jj).start)
            for index in (0, 1):
                plane_copy(k, src, jj, index).start()

        pl.when(jnp.logical_and(jj >= 0, jj < chunks))(go)

    def pass_on(k, j):
        src, behind, _, _ = sources[k]
        jj = j - behind - HOP

        def go():
            there = device(src, 1 - y, c)
            landed(tokens.at[there, :, cols(jj)], token_recv.at[there, jj])
            twin_copy(k, src, jj).start()

        pl.when(jnp.logical_and(jj >= 0, jj < chunks))(go)

    def move(j):
        for k in range(planes):
            relay(k, j)
        for k in range(planes):
            pass_on(k, j)

    def stream(j, carry):
        pl.when(j < chunks)(lambda: send_vertical(j))

        def more():
            send_own(j + AHEAD)
            send_side(j + AHEAD)

        pl.when(j + AHEAD < chunks)(more)
        pl.when(j == BEHIND)(choose)
        pl.when(j >= BEHIND)(lambda: attend(j - BEHIND))
        move(j)
        return carry

    lax.fori_loop(0, chunks + BEHIND, stream, 0)

    token = lax.broadcasted_iota(jnp.int32, (16, rows), 1)
    line_of = lax.broadcasted_iota(jnp.int32, (16, rows), 0)
    row_number = lax.broadcasted_iota(jnp.int32, (8, rows), 0)
    found = jnp.zeros((8, rows), jnp.float32)
    for step in range(2 * rows // 16):
        some = att[step * 16 : (step + 1) * 16, :].astype(jnp.float32)
        mean = jnp.mean(some, axis=-1, keepdims=True)
        some = some - mean
        spread = jnp.mean(some * some, axis=-1, keepdims=True)
        which, at = divmod(step * 16, rows)
        for kind, value in enumerate((mean, spread)):
            row = jnp.sum(jnp.where(token == line_of + at, value, 0.0), axis=0, keepdims=True)
            found = found + jnp.where(row_number == 2 * which + kind, row, 0.0)
    stats[me] = found
    for copy in tell(stats, stat_send, stat_recv):
        copy.start()

    def drain(j, carry):
        move(j)
        return carry

    lax.fori_loop(chunks + BEHIND, chunks + BEHIND + 4 * HOP, drain, 0)
    for target in others:
        landed(stats.at[target], stat_recv.at[target])
    for load in loads[3:]:
        load.wait()

    order = [
        jnp.where(at_end, p + 3 * toward, p + 2 * toward),
        jnp.where(at_end, p + 2 * toward, inner),
        jnp.where(at_end, inner, outer),
        p,
    ]
    def arrive(j, carry):
        for plane in range(planes):
            for yy in (0, 1):
                there = device(plane, yy, 1 - c)
                landed(tokens.at[there, :, cols(j)], token_recv.at[there, j])
        pl.when(at_end)(lambda: rest_landed(j))
        return carry

    lax.fori_loop(0, chunks, arrive, 0)
    group = SPLIT * cap
    chunk = min(width, 256)
    chunk_out = 512

    def block(buf, index):
        return buf.at[pl.ds(pl.multiple_of(index * cap, 16), cap), :]

    def picked_column(tile_there, row):
        return jnp.sum(jnp.where(chosen(tile_there, p), row, 0.0), axis=1, keepdims=True)

    def compute(i):
        plane = order[i]

        def normalise(t, carry):
            there = plane * SPLIT + t
            across = lax.rem(there + TILE_COLS, n)
            mean_here, mean_there = stats[there, 0:1, :], stats[across, 2:3, :]
            apart = 0.5 * (mean_here - mean_there)
            spread = 0.5 * (stats[there, 1:2, :] + stats[across, 3:4, :]) + apart * apart
            mean = picked_column(there, 0.5 * (mean_here + mean_there))
            rate = picked_column(there, lax.rsqrt(spread + EPSILON))
            at = pl.ds(pl.multiple_of(t * cap, 16), cap)
            base = part_of_plane(plane)
            for source, lower, start in ((there, 0, base), (across, cap, half - base)):
                for step in range(half // chunk_out):
                    some = slice(step * chunk_out, (step + 1) * chunk_out)
                    to = pl.ds(pl.multiple_of(start + step * chunk_out, chunk_out), chunk_out)
                    value = (tokens[source, lower : lower + cap, some].astype(jnp.float32) - mean) * rate
                    normed[at, to] = (value * (1.0 + mod_ref[1:2, to]) + mod_ref[0:1, to]).astype(
                        normed.dtype
                    )
            return carry

        lax.fori_loop(0, SPLIT, normalise, 0)

        def one(step, carry):
            at = pl.ds(pl.multiple_of(step * chunk, chunk), chunk)
            raw = jnp.dot(normed[...], first[:, at], preferred_element_type=jnp.float32)
            hidden[:, at] = jax.nn.gelu(raw, approximate=True).astype(hidden.dtype)
            return carry

        lax.fori_loop(0, width // chunk, one, 0)
        mine = pl.ds(pl.multiple_of(plane * group, 16), group)

        def two(step, carry):
            at = pl.ds(pl.multiple_of(step * chunk_out, chunk_out), chunk_out)
            raw = jnp.dot(hidden[...], second[:, at], preferred_element_type=jnp.float32)
            part[mine, at] = raw.astype(part.dtype)
            return carry

        lax.fori_loop(0, D // chunk_out, two, 0)
        for yy in (0, 1):
            to_twin(i, yy).start()

    def to_twin(i, yy):
        plane = order[i]
        return remote(
            block(part, device(plane, yy, 1 - c)),
            block(r1, plane * 2 + yy),
            back_send.at[i, yy],
            s1_recv.at[plane, yy],
            twin,
        )

    def to_beside(i):
        plane = order[i]
        return remote(
            block(part, device(plane, 1 - y, c)), block(r2, plane), back_send.at[i, 2], s2_recv.at[plane], beside
        )

    def fold_twin(i):
        plane = order[i]
        for yy in (1 - y, y):
            landed(block(r1, plane * 2 + yy), s1_recv.at[plane, yy])
            base = device(plane, yy, c) * cap
            from_there = (plane * 2 + yy) * cap

            def body(step, carry):
                at = pl.ds(pl.multiple_of(base + step * 16, 16), 16)
                extra = r1[pl.ds(pl.multiple_of(from_there + step * 16, 16), 16), :]
                part[at, :] = (part[at, :].astype(jnp.float32) + extra.astype(jnp.float32)).astype(part.dtype)
                return carry

            lax.fori_loop(0, cap // 16, body, 0)
            if yy is not y:
                to_beside(i).start()

    def fold_beside(i):
        plane = order[i]
        there = device(plane, y, c)
        landed(block(r2, plane), s2_recv.at[plane])
        weight = picked_column(there, tables[there, pl.ds(8 + p, 1), :])
        ours = pl.ds(pl.multiple_of(there * cap, 16), cap)
        theirs = pl.ds(pl.multiple_of(plane * cap, 16), cap)
        for step in range(D // chunk_out):
            some = slice(step * chunk_out, (step + 1) * chunk_out)
            total = part[ours, some].astype(jnp.float32) + r2[theirs, some].astype(jnp.float32)
            pair[plane, :cap, some] = (total * weight).astype(pair.dtype)

    def slots_home(i):
        plane = order[i]
        return remote(
            pair.at[plane, pl.ds(0, cap), :],
            pair.at[plane, pl.ds(cap, cap), :],
            back_send.at[i, 3],
            pair_recv.at[plane],
            inner_device,
        )

    def rows_home(i):
        plane = order[i]
        return remote(
            acc_out.at[plane],
            acc_in.at[plane],
            back_send.at[i, 3],
            acc_recv.at[plane],
            outer_device if i == 2 else inner_device,
        )

    def spread_out(plane, both, at):
        amount = 2 * cap if both else cap
        return lax.dot_general(
            spreader[plane, :amount, :],
            pair[plane, :amount, at],
            (((0,), (0,)), ((), ())),
            preferred_element_type=jnp.float32,
        )

    def fold_home(i):
        plane = order[i]

        def fold(both, extra, last):
            if both:
                landed(pair.at[plane, pl.ds(cap, cap), :], pair_recv.at[plane])
            if extra:
                landed(acc_in.at[plane], acc_recv.at[plane])

            def body(step, carry):
                at = pl.ds(pl.multiple_of(step * chunk_out, chunk_out), chunk_out)
                total = spread_out(plane, both, at)
                if extra:
                    total = total + acc_in[plane, :, at].astype(jnp.float32)
                if last:
                    out_ref[:, at] = (mod_ref[2:3, at] * total + out_ref[:, at].astype(jnp.float32)).astype(
                        out_ref.dtype
                    )
                else:
                    acc_out[plane, :, at] = total.astype(acc_out.dtype)
                return carry

            if last:
                out_ref[:, halves(mine_from)] = att[:rows, :]
                out_ref[:, halves(other_from)] = line[partner_plane, rows:, :]
            lax.fori_loop(0, D // chunk_out, body, 0)
            if not last:
                rows_home(i).start()

        if i == 3:
            pl.when(at_end)(lambda: fold(False, True, True))
            pl.when(middle)(lambda: fold(True, True, True))
        else:
            pl.when(at_end)(slots_home(i).start)
            pl.when(middle)(lambda: fold(i < 2, i == 2, False))

    for i in range(planes):
        compute(i)
        fold_twin(i)
        if i > 0:
            fold_beside(i - 1)
            fold_home(i - 1)
    fold_beside(planes - 1)
    fold_home(planes - 1)

    def left(j, carry):
        for i in range(3):
            over_vertical(i, j).wait_send()
        pl.when(middle)(rest_copy(inner, j).wait_send)
        for i in (0, 1):
            for level in (0, 1):
                for index, (_, exists) in enumerate(sides):
                    when(exists, over_side(level, index, i, j).wait_send)
        for k, (src, _, whole, out) in enumerate(sources):
            if whole is not False:
                when(whole, raw_copy(k, src, j).wait_send)
            if out is not False:
                when(out, outer_copy(k, src, j).wait_send)
            for index in (0, 1):
                plane_copy(k, src, j, index).wait_send()
            twin_copy(k, src, j).wait_send()
        return carry

    lax.fori_loop(0, chunks, left, 0)
    for copy in tell(tables, table_send, table_recv) + tell(stats, stat_send, stat_recv):
        copy.wait_send()
    for i in range(planes):
        for yy in (0, 1):
            to_twin(i, yy).wait_send()
        to_beside(i).wait_send()
        if i < planes - 1:
            pl.when(at_end)(slots_home(i).wait_send)
            pl.when(middle)(rows_home(i).wait_send)


def kernel_bytes(n, rows, cap, width):
    planes = n // SPLIT
    lines = 2 * 6 * rows + 2 * n * cap + planes * (6 * cap + 3 * rows) + SPLIT * cap + 3 * rows
    return 2 * (lines * D + 2 * width * D)


def layer(queries, key_rows, values, modulation, expert_in, expert_out, routes, gate_fixed):
    n = lax.axis_size("tile")
    rows = queries.shape[0]
    width = expert_in.shape[1]
    planes = n // SPLIT
    cap = 3 * rows // planes
    chunks = CHUNKS
    vmem = pl.BlockSpec(memory_space=pltpu.VMEM)
    hbm = pl.BlockSpec(memory_space=pl.ANY)
    dma = pltpu.SemaphoreType.DMA
    bf = jnp.bfloat16
    return pl.pallas_call(
        functools.partial(layer_kernel, n, rows, cap, chunks),
        name="whole_layer",
        out_shape=jax.ShapeDtypeStruct((rows, D), bf),
        in_specs=[hbm, hbm, hbm, vmem, vmem, vmem, hbm, hbm],
        out_specs=vmem,
        scratch_shapes=[
            pltpu.VMEM((2 * rows, D // 2), bf),
            pltpu.VMEM((2 * rows, D // 2), bf),
            pltpu.VMEM((8, 6 * rows), jnp.float32),
            pltpu.VMEM((6 * rows, D // 2), bf),
            pltpu.VMEM((6 * rows, D // 2), bf),
            pltpu.VMEM((planes, 2 * rows, D // 2), bf),
            pltpu.VMEM((n, 2 * cap, D // 2), bf),
            pltpu.VMEM((planes, 2 * cap, D // 2), bf),
            pltpu.VMEM((planes, 4 * cap, 2 * rows), bf),
            pltpu.VMEM((planes, 2 * cap, rows), bf),
            pltpu.VMEM((n, 16, rows), jnp.float32),
            pltpu.VMEM((n, 8, rows), jnp.float32),
            pltpu.VMEM((SPLIT * cap, D), bf),
            pltpu.VMEM((D, width), bf),
            pltpu.VMEM((width, D), bf),
            pltpu.VMEM((SPLIT * cap, width), bf),
            pltpu.VMEM((n * cap, D), bf),
            pltpu.VMEM((planes * 2 * cap, D), bf),
            pltpu.VMEM((planes * cap, D), bf),
            pltpu.VMEM((planes, 2 * cap, D), bf),
            pltpu.VMEM((planes, rows, D), bf),
            pltpu.VMEM((planes, rows, D), bf),
            dma((5,)),
            dma((11, chunks)),
            dma((13, chunks)),
            dma((n - 1,)),
            dma((n,)),
            dma((n - 1,)),
            dma((n,)),
            dma((planes, 5, chunks)),
            dma((planes, chunks)),
            dma((n, chunks)),
            dma((chunks,)),
            dma((planes, 4)),
            dma((planes, 2)),
            dma((planes,)),
            dma((planes,)),
            dma((planes,)),
        ],
        compiler_params=pltpu.CompilerParams(
            collective_id=1, has_side_effects=True, vmem_limit_bytes=VMEM_LIMIT
        ),
    )(queries, key_rows, values, modulation, routes.T, gate_fixed.T, expert_in, expert_out)


def slot_table(flat, experts_count):
    onehot = (flat[:, None] == jnp.arange(experts_count, dtype=jnp.int32)[None, :]).astype(
        jnp.int32
    )
    before = jnp.cumsum(onehot, axis=0) - onehot
    return jnp.sum(before * onehot, axis=1)


def expert_apply(rows, first_weight, second_weight):
    hidden = jax.nn.gelu(
        jnp.dot(rows, first_weight, preferred_element_type=jnp.float32), approximate=True
    ).astype(jnp.bfloat16)
    return jnp.dot(hidden, second_weight, preferred_element_type=jnp.float32).astype(jnp.bfloat16)


def experts_sparse(normed, attended, modulation, expert_in, expert_out, routes, gate_fixed):
    devices = lax.axis_size("tile")
    rows_dev = normed.shape[0]
    experts_count = devices // SPLIT
    capacity = 3 * rows_dev // experts_count
    flat = routes.reshape(-1)
    slots = slot_table(flat, experts_count)
    target = flat * capacity + slots
    chooser = (
        target[None, :] == jnp.arange(experts_count * capacity, dtype=jnp.int32)[:, None]
    ).astype(jnp.bfloat16)
    chooser = chooser.reshape(experts_count * capacity, rows_dev, 2).sum(axis=2)
    buffer = jnp.dot(chooser, normed, preferred_element_type=jnp.float32).astype(jnp.bfloat16)
    copies = jnp.broadcast_to(
        buffer.reshape(experts_count, 1, capacity, D), (experts_count, SPLIT, capacity, D)
    ).reshape(devices, capacity, D)
    received = lax.all_to_all(copies, "tile", split_axis=0, concat_axis=0, tiled=True)
    sources = received.shape[0]
    count = received.shape[1]
    partial_value = expert_apply(received.reshape(sources * count, D), expert_in, expert_out)
    returned = lax.all_to_all(
        partial_value.reshape(sources, count, D), "tile", split_axis=0, concat_axis=0, tiled=True
    )
    summed = jnp.sum(
        returned.reshape(experts_count, SPLIT, capacity, D).astype(jnp.float32), axis=1
    )
    expert_rows = summed.astype(jnp.bfloat16).reshape(experts_count * capacity, D)
    picked = jnp.take(expert_rows, target, axis=0).reshape(rows_dev, 2, D)
    gate_scale = gate_fixed.astype(jnp.float32) / 1024.0
    mixture = jnp.sum(picked.astype(jnp.float32) * gate_scale[:, :, None], axis=1)
    return (attended.astype(jnp.float32) + modulation[2] * mixture).astype(jnp.bfloat16)


def shards(queries, key_rows, values, modulation, expert_in, expert_out, routes, gate_fixed):
    n = lax.axis_size("tile")
    cap = 3 * queries.shape[0] // (n // SPLIT)
    if n == 2 * TILE_COLS and cap % 16 == 0 and kernel_bytes(n, queries.shape[0], cap, expert_in.shape[1]) < VMEM_LIMIT * 7 // 8:
        return layer(queries, key_rows, values, modulation, expert_in, expert_out, routes, gate_fixed)
    attended, normed = attention(queries, key_rows, values, modulation)
    return experts_sparse(normed, attended, modulation, expert_in, expert_out, routes, gate_fixed)


def solution(mesh):
    placed = (
        P(("groups", "tile"), None),
        P(("groups", "tile"), None),
        P(("groups", "tile"), None),
        P("groups", None),
        P(None, "tile"),
        P("tile", None),
        P(("groups", "tile"), None),
        P(("groups", "tile"), None),
    )
    return jax.shard_map(
        shards, mesh=mesh, in_specs=placed, out_specs=P(("groups", "tile"), None), check_vma=False
    )
```

```python
import functools
import math

import jax
import jax.numpy as jnp
from jax import lax
from jax.experimental import pallas as pl
from jax.experimental.pallas import tpu as pltpu
from jax.sharding import PartitionSpec as P

HEAD_DIM = 128
D = 4096
SPLIT = 4
TILE_COLS = 8

EPSILON = 1e-06
MASKED = -1e30
MESH = pl.DeviceIdType.MESH
VMEM_LIMIT = 60 * 1024 * 1024
CHUNKS = 8
AHEAD = 2
BEHIND = 2
HOP = 2
BACK_CHUNKS = 4
BACK_LAGS = (1, 4, 6)


def when(cond, body):
    if cond is True:
        body()
    else:
        pl.when(cond)(body)


def both(a, b):
    if a is True:
        return b
    if b is True:
        return a
    return jnp.logical_and(a, b)


def remote(src, dst, send_sem, recv_sem, target):
    return pltpu.make_async_remote_copy(
        src_ref=src,
        dst_ref=dst,
        send_sem=send_sem,
        recv_sem=recv_sem,
        device_id={"tile": target},
        device_id_type=MESH,
    )


def halo_levels(n):
    grid_rows = n // TILE_COLS
    if grid_rows < 2:
        return 1
    return 2 if grid_rows == 2 else 3


def attention_kernel(
    n, rows, q_ref, k_ref, v_ref, mod_ref, att_ref, norm_ref, keys, vals, send_sem, recv_sem, own_sem,
):
    me = lax.axis_index("tile")
    grid_rows = n // TILE_COLS
    tile = lax.rem(me + TILE_COLS // 2, n)
    row = lax.div(tile, TILE_COLS)
    col = lax.rem(tile, TILE_COLS)
    if grid_rows < 2:
        verticals = []
    elif grid_rows == 2:
        verticals = [(1, TILE_COLS, True, 1)]
    else:
        verticals = [(1, n - TILE_COLS, row > 0, 2), (2, TILE_COLS, row < grid_rows - 1, 1)]
    sides = [(-1, col > 0), (1, col < TILE_COLS - 1)]
    here = {level: exists for level, _, exists, _ in verticals}
    here[0] = True

    def slot(level, side):
        return level * 3 + 1 + side

    def place(buf, s):
        return buf.at[pl.ds(s * rows, rows), :]

    def over(offset):
        return lax.rem(me + offset + n, n)

    half = rows // 2
    middle = TILE_COLS // 2
    crossing = {side: col == (middle if side < 0 else middle - 1) for side, _ in sides}
    two = grid_rows == 2

    def part_of(buf, s, h):
        return buf.at[pl.ds(pl.multiple_of(s * rows + h * half, half), half), :]

    own = [
        pltpu.make_async_copy(src, place(buf, slot(0, 0)), own_sem.at[i])
        for i, (src, buf) in enumerate(((k_ref, keys), (v_ref, vals)))
    ]
    for copy in own:
        copy.start()

    def beside(side):
        if not two:
            return over(side)
        return jnp.where(crossing[side], over(side + TILE_COLS), over(side))

    def level_there(level, side):
        return jnp.where(crossing[side], 1 - level, level) if two else level

    barrier = pltpu.get_barrier_semaphore()
    partners = [(over(offset), exists) for _, offset, exists, _ in verticals]
    partners += [(beside(side), exists) for side, exists in sides]
    for target, exists in partners:

        def greet(target=target):
            pl.semaphore_signal(barrier, inc=1, device_id={"tile": target}, device_id_type=MESH)

        when(exists, greet)
    expected = sum(1 if exists is True else jnp.where(exists, 1, 0) for _, exists in partners)
    pl.semaphore_wait(barrier, expected)

    sends = []
    pieces = [(i, h) for i in (0, 1) for h in (0, 1)]
    bufs = (keys, vals)

    def push(i, h, src, there, target, exists):
        copy = remote(
            src,
            part_of(bufs[i], there, h),
            send_sem.at[len(sends)],
            recv_sem.at[there, i * 2 + h],
            target,
        )
        when(exists, copy.start)
        sends.append((copy, exists))

    def arrived(s, exists, i, h):
        ref = part_of(bufs[i], s, h)
        when(exists, remote(ref, ref, send_sem.at[0], recv_sem.at[s, i * 2 + h], me).wait_recv)

    def own_part(i, h):
        return (k_ref, v_ref)[i].at[pl.ds(h * half, half), :]

    for i, h in pieces:
        for level, offset, exists, there in verticals:
            push(i, h, own_part(i, h), slot(there, 0), over(offset), exists)
    for i, h in pieces:
        for side, exists in sides:
            push(i, h, own_part(i, h), slot(level_there(0, side), -side), beside(side), exists)
    for s in range(3 * (1 + len(verticals))):
        level, side = s // 3, s % 3 - 1
        exists = here[level]
        for other, side_exists in sides:
            if other == side:
                exists = both(exists, side_exists)
        if exists is True:
            continue

        def clear(s=s):
            for buf in (keys, vals):
                buf[pl.ds(s * rows, rows), :] = jnp.zeros((rows, D), buf.dtype)

        pl.when(jnp.logical_not(exists))(clear)
    for i, h in pieces:
        for level, offset, exists, there in verticals:
            arrived(slot(level, 0), exists, i, h)
            for side, side_exists in sides:
                push(
                    i,
                    h,
                    part_of(bufs[i], slot(level, 0), h),
                    slot(level_there(level, side), -side),
                    beside(side),
                    both(exists, side_exists),
                )
    for copy in own:
        copy.wait()
    for i, h in pieces:
        for level, exists in sorted(here.items(), key=lambda item: item[0]):
            for side, side_exists in sides:
                arrived(slot(level, side), both(exists, side_exists), i, h)

    span = 3 * (1 + len(verticals)) * rows
    where = lax.broadcasted_iota(jnp.int32, (rows, span), 1)
    bias = jnp.zeros((rows, span), jnp.float32)
    for s in range(span // rows):
        level, side = s // 3, s % 3 - 1
        exists = here[level]
        for other, side_exists in sides:
            if other == side:
                exists = both(exists, side_exists)
        if exists is True:
            continue
        penalty = jnp.where(exists, 0.0, MASKED)
        bias = jnp.where((where >= s * rows) & (where < (s + 1) * rows), penalty, bias)
    scale = 1.0 / math.sqrt(HEAD_DIM)
    together = 8

    def heads(step, carry):
        for extra in range(together):
            at = pl.ds(pl.multiple_of((step * together + extra) * HEAD_DIM, HEAD_DIM), HEAD_DIM)
            scores = lax.dot_general(
                q_ref[:, at], keys[:, at], (((1,), (1,)), ((), ())), preferred_element_type=jnp.float32
            )
            scores = scores * scale + bias
            raised = jnp.exp(scores - jnp.max(scores, axis=-1, keepdims=True))
            probs = (raised * (1.0 / jnp.sum(raised, axis=-1, keepdims=True))).astype(jnp.bfloat16)
            att_ref[:, at] = jnp.dot(probs, vals[:, at], preferred_element_type=jnp.float32).astype(
                att_ref.dtype
            )
        return carry

    lax.fori_loop(0, D // HEAD_DIM // together, heads, 0)

    def normalise(step, carry):
        at = pl.ds(pl.multiple_of(step * 16, 16), 16)
        wide = att_ref[at, :].astype(jnp.float32)
        wide = wide - jnp.mean(wide, axis=-1, keepdims=True)
        spread = jnp.mean(wide * wide, axis=-1, keepdims=True)
        normed = wide * lax.rsqrt(spread + EPSILON)
        norm_ref[at, :] = (normed * (1.0 + mod_ref[1:2, :]) + mod_ref[0:1, :]).astype(norm_ref.dtype)
        return carry

    lax.fori_loop(0, rows // 16, normalise, 0)
    for copy, exists in sends:
        when(exists, copy.wait_send)


def attention(queries, key_rows, values, modulation):
    n = lax.axis_size("tile")
    rows = queries.shape[0]
    levels = halo_levels(n)
    slots = 3 * levels
    vmem = pl.BlockSpec(memory_space=pltpu.VMEM)
    hbm = pl.BlockSpec(memory_space=pl.ANY)
    return pl.pallas_call(
        functools.partial(attention_kernel, n, rows),
        name="halo_attention",
        out_shape=(
            jax.ShapeDtypeStruct((rows, D), jnp.bfloat16),
            jax.ShapeDtypeStruct((rows, D), jnp.bfloat16),
        ),
        in_specs=[vmem, hbm, hbm, vmem],
        out_specs=(vmem, vmem),
        scratch_shapes=[
            pltpu.VMEM((slots * rows, D), jnp.bfloat16),
            pltpu.VMEM((slots * rows, D), jnp.bfloat16),
            pltpu.SemaphoreType.DMA((4 * (2 + 3 * (levels - 1)),)),
            pltpu.SemaphoreType.DMA((slots, 4)),
            pltpu.SemaphoreType.DMA((2,)),
        ],
        compiler_params=pltpu.CompilerParams(
            collective_id=0, has_side_effects=True, vmem_limit_bytes=VMEM_LIMIT
        ),
    )(queries, key_rows, values, modulation)


def device(plane, yy, cc):
    return plane * SPLIT + yy * 2 + cc


def layer_kernel(
    n, rows, cap, chunks, backs, q_ref, k_ref, v_ref, mod_ref, routes_ref, gates_ref, first_ref, second_ref,
    out_ref, att, asked, bias, keys, vals, line, tokens, stage, chooser, spreader, tables, stats, normed,
    first, second, hidden, part, r1, r2, pair, acc_in, acc_out,
    own_sem, kv_send, kv_recv, table_send, table_recv, stat_send, stat_recv, out_send, line_recv,
    token_recv, rest_send, back_send, s1_recv, s2_recv, pair_recv, acc_recv,
):
    planes = n // SPLIT
    width = first.shape[1]
    half = D // 2
    wide = half // chunks
    me = lax.axis_index("tile")
    p = lax.div(me, SPLIT)
    y = lax.div(lax.rem(me, SPLIT), 2)
    c = lax.rem(me, 2)
    beside = device(p, 1 - y, c)
    twin = device(p, y, 1 - c)
    low_half = p < planes // 2
    toward = jnp.where(low_half, 1, -1)
    inner = p + toward
    outer = p - toward
    at_end = jnp.logical_or(p == 0, p == planes - 1)
    middle = jnp.logical_not(at_end)
    outer_expert = jnp.where(low_half, 0, planes - 1)
    inner_device = device(inner, y, c)
    outer_device = device(jnp.where(at_end, p, outer), y, c)

    tile = lax.rem(me + TILE_COLS // 2, n)
    column = lax.rem(tile, TILE_COLS)
    partner = lax.rem(me + TILE_COLS, n)
    sides = [(-1, column > 0), (1, column < TILE_COLS - 1)]
    half_way = TILE_COLS // 2
    crossing = {-1: column == half_way, 1: column == half_way - 1}

    def part_of_plane(plane):
        return jnp.where(plane < planes // 2, half, 0)

    mine_from = part_of_plane(p)
    other_from = half - mine_from
    partner_plane = lax.rem(p + planes // 2, planes)

    def cols(j, base=0):
        return pl.ds(pl.multiple_of(base + j * wide, wide), wide)

    def halves(base):
        return pl.ds(pl.multiple_of(base, half), half)

    def lines(buf, s):
        return buf.at[pl.ds(pl.multiple_of(s * rows, rows), rows), :]

    loads = [
        pltpu.make_async_copy(q_ref.at[:, halves(mine_from)], lines(asked, 0), own_sem.at[0]),
        pltpu.make_async_copy(k_ref.at[:, halves(mine_from)], lines(keys, 1), own_sem.at[1]),
        pltpu.make_async_copy(v_ref.at[:, halves(mine_from)], lines(vals, 1), own_sem.at[2]),
        pltpu.make_async_copy(first_ref, first, own_sem.at[3]),
        pltpu.make_async_copy(second_ref, second, own_sem.at[4]),
    ]
    for load in loads:
        load.start()

    barrier = pltpu.get_barrier_semaphore()
    others = [lax.rem(me + step, n) for step in range(1, n)]
    for target in others:
        pl.semaphore_signal(barrier, inc=1, device_id={"tile": target}, device_id_type=MESH)
    pl.semaphore_wait(barrier, n - 1)

    def beside_tile(side):
        return lax.rem(me + side + jnp.where(crossing[side], TILE_COLS, 0) + n, n)

    def slot_there(level, side):
        return jnp.where(crossing[side], 1 - level, level) * 3 + 1 - side

    bufs = (keys, vals, asked)
    given = (k_ref, v_ref, q_ref)

    def place(i, s, j):
        return bufs[i].at[pl.ds(pl.multiple_of(s * rows, rows), rows), cols(j)]

    def over_vertical(i, j):
        return remote(
            given[i].at[:, cols(j, other_from)],
            place(i, 4 if i < 2 else 1, j),
            kv_send.at[i, j],
            kv_recv.at[8 + i if i < 2 else 12, j],
            partner,
        )

    def over_side(level, index, i, j):
        side = sides[index][0]
        there = slot_there(level, side)
        source = given[i].at[:, cols(j, mine_from)] if level == 0 else place(i, 4, j)
        return remote(
            source,
            place(i, there, j),
            kv_send.at[3 + level * 4 + index * 2 + i, j],
            kv_recv.at[there * 2 + i, j],
            beside_tile(side),
        )

    def landed(ref, sem):
        remote(ref, ref, own_sem.at[0], sem, me).wait_recv()

    def send_own(j):
        for i in range(3):
            over_vertical(i, j).start()

    def send_side(j):
        for i in (0, 1):
            for index, (_, exists) in enumerate(sides):
                when(exists, over_side(0, index, i, j).start)

    def send_vertical(j):
        for i in (0, 1):
            landed(place(i, 4, j), kv_recv.at[8 + i, j])
            for index, (_, exists) in enumerate(sides):
                when(exists, over_side(1, index, i, j).start)

    for j in range(min(AHEAD, chunks)):
        send_own(j)
        send_side(j)

    expert = lax.broadcasted_iota(jnp.int32, (8, rows), 0)
    named = [routes_ref[k : k + 1, :] == expert for k in (0, 1)]
    member = jnp.logical_or(named[0], named[1])
    upto = (
        lax.broadcasted_iota(jnp.int32, (rows, rows), 0) <= lax.broadcasted_iota(jnp.int32, (rows, rows), 1)
    ).astype(jnp.float32).astype(jnp.bfloat16)
    count = jnp.dot(
        member.astype(jnp.float32).astype(jnp.bfloat16), upto, preferred_element_type=jnp.float32
    )
    gate = sum(
        jnp.where(named[k], gates_ref[k : k + 1, :].astype(jnp.float32), 0.0) for k in (0, 1)
    )
    tables[me, 0:8, :] = jnp.where(member, count - 1.0, -1.0)
    tables[me, 8:16, :] = gate / 1024.0

    def tell(ref, send, recv):
        return [
            remote(ref.at[me], ref.at[me], send.at[step], recv.at[me], target)
            for step, target in enumerate(others)
        ]

    for copy in tell(tables, table_send, table_recv):
        copy.start()

    span = 6 * rows
    where = lax.broadcasted_iota(jnp.int32, (8, span), 1)
    penalty = jnp.zeros((8, span), jnp.float32)
    for s in range(6):
        for side, exists in sides:
            if side != s % 3 - 1:
                continue
            here = (where >= s * rows) & (where < (s + 1) * rows)
            penalty = jnp.where(here, jnp.where(exists, 0.0, MASKED), penalty)

            def clear(s=s):
                for buf in (keys, vals):
                    buf[s * rows : (s + 1) * rows, :] = jnp.zeros((rows, half), buf.dtype)

            pl.when(jnp.logical_not(exists))(clear)
    bias[...] = penalty
    for load in loads[:3]:
        load.wait()

    slot_line = lax.broadcasted_iota(jnp.int32, (cap, rows), 0).astype(jnp.float32)

    def chosen(tile_there, e):
        return tables[tile_there, pl.ds(e, 1), :] == slot_line

    def choose():
        for target in others:
            landed(tables.at[target], table_recv.at[target])
        chooser[...] = jnp.zeros(chooser.shape, chooser.dtype)
        for plane in range(planes):
            for place_in, e in ((0, p), (1, outer_expert)):
                found = chosen(device(plane, y, c), e).astype(jnp.float32).astype(jnp.bfloat16)
                at = place_in * 2 * cap
                spreader[plane, place_in * cap : (place_in + 1) * cap, :] = found
                chooser[plane, at : at + cap, :rows] = found
                chooser[(plane + planes // 2) % planes, at + cap : at + 2 * cap, rows:] = found

    scale = 1.0 / math.sqrt(HEAD_DIM)

    def attend(j):
        for level in (0, 1):
            for side, exists in sides:
                s = level * 3 + 1 + side
                for i in (0, 1):
                    when(exists, functools.partial(landed, place(i, s, j), kv_recv.at[s * 2 + i, j]))
        landed(place(2, 1, j), kv_recv.at[12, j])
        for extra in range(wide // HEAD_DIM):
            at = pl.ds(pl.multiple_of(j * wide + extra * HEAD_DIM, HEAD_DIM), HEAD_DIM)
            scores = lax.dot_general(
                asked[:, at], keys[:, at], (((1,), (1,)), ((), ())), preferred_element_type=jnp.float32
            )
            scores = scores * scale + bias[0:1, :]
            raised = jnp.exp(scores - jnp.max(scores, axis=-1, keepdims=True))
            probs = (raised * (1.0 / jnp.sum(raised, axis=-1, keepdims=True))).astype(jnp.bfloat16)
            att[:, at] = jnp.dot(probs, vals[:, at], preferred_element_type=jnp.float32).astype(att.dtype)

    def raw_copy(k, src, j):
        source = att.at[:, cols(j)] if k == 0 else line.at[src, :, cols(j)]
        return remote(source, line.at[src, :, cols(j)], out_send.at[k, 0, j], line_recv.at[src, j], inner_device)

    def outer_copy(k, src, j):
        there = device(src, y, c)
        return remote(
            stage.at[src, :, cols(j)],
            tokens.at[there, :, cols(j)],
            out_send.at[k, 1, j],
            token_recv.at[there, j],
            outer_device,
        )

    def rest_copy(src, j):
        ref = line.at[src, pl.ds(rows, rows), cols(j)]
        return remote(ref, ref, rest_send.at[j], line_recv.at[src, j], outer_device)

    def rest_landed(j):
        landed(line.at[partner_plane, pl.ds(rows, rows), cols(j)], line_recv.at[partner_plane, j])

    def plane_copy(k, src, j, index):
        ref = tokens.at[device(src, y, c), :, cols(j)]
        return remote(
            ref, ref, out_send.at[k, 2 + index, j], token_recv.at[device(src, y, c), j], (beside, twin)[index]
        )

    def twin_copy(k, src, j):
        there = device(src, 1 - y, c)
        ref = tokens.at[there, :, cols(j)]
        return remote(ref, ref, out_send.at[k, 4, j], token_recv.at[there, j], twin)

    far = jnp.where(at_end, p + 3 * toward, p + 2 * toward)
    second_plane = jnp.where(at_end, p + 2 * toward, outer)
    sources = [
        (p, BEHIND, True, middle),
        (inner, BEHIND + HOP, False, middle),
        (second_plane, BEHIND + HOP * jnp.where(at_end, 2, 1), middle, False),
        (far, BEHIND + HOP * jnp.where(at_end, 3, 2), False, middle),
    ]

    def relay(k, j):
        src, behind, whole, out = sources[k]
        jj = j - behind

        def go():
            there = device(src, y, c)
            if k > 0:
                pl.when(at_end)(
                    lambda: landed(tokens.at[there, :, cols(jj)], token_recv.at[there, jj])
                )
                pl.when(middle)(lambda: landed(line.at[src, :, cols(jj)], line_recv.at[src, jj]))
            if whole is not False:
                when(whole, raw_copy(k, src, jj).start)
            if k == 1:
                pl.when(middle)(rest_copy(src, jj).start)

            def pick():
                rows_here = att[:, cols(jj)] if k == 0 else line[src, :, cols(jj)]
                picked = jnp.dot(chooser[src], rows_here, preferred_element_type=jnp.float32).astype(
                    tokens.dtype
                )
                tokens[there, :, cols(jj)] = picked[: 2 * cap]
                stage[src, :, cols(jj)] = picked[2 * cap :]

            when(True if k == 0 else middle, pick)
            if out is not False:
                when(out, outer_copy(k, src, jj).start)
            for index in (0, 1):
                plane_copy(k, src, jj, index).start()

        pl.when(jnp.logical_and(jj >= 0, jj < chunks))(go)

    def pass_on(k, j):
        src, behind, _, _ = sources[k]
        jj = j - behind - HOP

        def go():
            there = device(src, 1 - y, c)
            landed(tokens.at[there, :, cols(jj)], token_recv.at[there, jj])
            twin_copy(k, src, jj).start()

        pl.when(jnp.logical_and(jj >= 0, jj < chunks))(go)

    def move(j):
        for k in range(planes):
            relay(k, j)
        for k in range(planes):
            pass_on(k, j)

    def stream(j, carry):
        pl.when(j < chunks)(lambda: send_vertical(j))

        def more():
            send_own(j + AHEAD)
            send_side(j + AHEAD)

        pl.when(j + AHEAD < chunks)(more)
        pl.when(j == BEHIND)(choose)
        pl.when(j >= BEHIND)(lambda: attend(j - BEHIND))
        move(j)
        return carry

    lax.fori_loop(0, chunks + BEHIND, stream, 0)

    token = lax.broadcasted_iota(jnp.int32, (16, rows), 1)
    line_of = lax.broadcasted_iota(jnp.int32, (16, rows), 0)
    row_number = lax.broadcasted_iota(jnp.int32, (8, rows), 0)
    found = jnp.zeros((8, rows), jnp.float32)
    for step in range(2 * rows // 16):
        some = att[step * 16 : (step + 1) * 16, :].astype(jnp.float32)
        mean = jnp.mean(some, axis=-1, keepdims=True)
        some = some - mean
        spread = jnp.mean(some * some, axis=-1, keepdims=True)
        which, at = divmod(step * 16, rows)
        for kind, value in enumerate((mean, spread)):
            row = jnp.sum(jnp.where(token == line_of + at, value, 0.0), axis=0, keepdims=True)
            found = found + jnp.where(row_number == 2 * which + kind, row, 0.0)
    stats[me] = found
    for copy in tell(stats, stat_send, stat_recv):
        copy.start()

    def drain(j, carry):
        move(j)
        return carry

    lax.fori_loop(chunks + BEHIND, chunks + BEHIND + 4 * HOP, drain, 0)
    for target in others:
        landed(stats.at[target], stat_recv.at[target])
    for load in loads[3:]:
        load.wait()

    order = [
        jnp.where(at_end, p + 3 * toward, p + 2 * toward),
        jnp.where(at_end, p + 2 * toward, inner),
        jnp.where(at_end, inner, outer),
        p,
    ]
    def arrive(j, carry):
        for plane in range(planes):
            for yy in (0, 1):
                there = device(plane, yy, 1 - c)
                landed(tokens.at[there, :, cols(j)], token_recv.at[there, j])
        pl.when(at_end)(lambda: rest_landed(j))
        return carry

    lax.fori_loop(0, chunks, arrive, 0)
    group = SPLIT * cap
    chunk = 512
    span_back = D // backs

    def home_of(i):
        return jnp.where(i == 0, order[0], jnp.where(i == 1, order[1], jnp.where(i == 2, order[2], order[3])))

    def block(buf, index, count, j):
        return buf.at[pl.ds(pl.multiple_of(index * cap, 16), count * cap), back_cols(j)]

    def back_cols(j):
        return pl.ds(pl.multiple_of(j * span_back, span_back), span_back)

    def picked_column(tile_there, row):
        return jnp.sum(jnp.where(chosen(tile_there, p), row, 0.0), axis=1, keepdims=True)

    def start_group(plane):
        def normalise(t, carry):
            yy, cc = lax.rem(t, 2), lax.div(t, 2)
            there = device(plane, yy, cc)
            across = lax.rem(there + TILE_COLS, n)
            mean_here, mean_there = stats[there, 0:1, :], stats[across, 2:3, :]
            apart = 0.5 * (mean_here - mean_there)
            spread = 0.5 * (stats[there, 1:2, :] + stats[across, 3:4, :]) + apart * apart
            mean = picked_column(there, 0.5 * (mean_here + mean_there))
            rate = picked_column(there, lax.rsqrt(spread + EPSILON))
            at = pl.ds(pl.multiple_of(t * cap, 16), cap)
            base = part_of_plane(plane)
            for source, lower, start in ((there, 0, base), (across, cap, half - base)):
                for step in range(half // chunk):
                    some = slice(step * chunk, (step + 1) * chunk)
                    to = pl.ds(pl.multiple_of(start + step * chunk, chunk), chunk)
                    value = (tokens[source, lower : lower + cap, some].astype(jnp.float32) - mean) * rate
                    normed[at, to] = (value * (1.0 + mod_ref[1:2, to]) + mod_ref[0:1, to]).astype(
                        normed.dtype
                    )
            return carry

        lax.fori_loop(0, SPLIT, normalise, 0)
        raw = jnp.dot(normed[...], first[...], preferred_element_type=jnp.float32)
        hidden[...] = jax.nn.gelu(raw, approximate=True).astype(hidden.dtype)

    def to_twin(plane, j):
        return remote(
            block(part, plane * SPLIT + (1 - c) * 2, 2, j),
            block(r1, plane * 2, 2, j),
            back_send.at[plane, 0, j],
            s1_recv.at[plane, j],
            twin,
        )

    def to_beside(plane, j):
        return remote(
            block(part, plane * SPLIT + c * 2 + 1 - y, 1, j),
            block(r2, plane, 1, j),
            back_send.at[plane, 1, j],
            s2_recv.at[plane, j],
            beside,
        )

    def slots_home(plane, j):
        return remote(
            pair.at[plane, pl.ds(0, cap), back_cols(j)],
            pair.at[plane, pl.ds(cap, cap), back_cols(j)],
            back_send.at[plane, 2, j],
            pair_recv.at[plane, j],
            inner_device,
        )

    def rows_home(plane, j):
        return remote(
            acc_out.at[plane, :, back_cols(j)],
            acc_in.at[plane, :, back_cols(j)],
            back_send.at[plane, 3, j],
            acc_recv.at[plane, j],
            device(jnp.where(plane == outer, outer, inner), y, c),
        )

    def produce(i, j):
        plane = home_of(i)
        pl.when(j == 0)(lambda: start_group(plane))
        raw = jnp.dot(hidden[...], second[:, back_cols(j)], preferred_element_type=jnp.float32)
        mine = pl.ds(pl.multiple_of(plane * group, 16), group)
        part[mine, back_cols(j)] = raw.astype(part.dtype)
        to_twin(plane, j).start()

    def fold_twin(i, j):
        plane = home_of(i)
        landed(block(r1, plane * 2, 2, j), s1_recv.at[plane, j])
        for yy in (1 - y, y):
            at = pl.ds(pl.multiple_of((plane * SPLIT + c * 2 + yy) * cap, 16), cap)
            there = pl.ds(pl.multiple_of((plane * 2 + yy) * cap, 16), cap)
            total = part[at, back_cols(j)].astype(jnp.float32) + r1[there, back_cols(j)].astype(jnp.float32)
            part[at, back_cols(j)] = total.astype(part.dtype)
            if yy is not y:
                to_beside(plane, j).start()

    def fold_beside(i, j):
        plane = home_of(i)
        there = device(plane, y, c)
        landed(block(r2, plane, 1, j), s2_recv.at[plane, j])
        weight = picked_column(there, tables[there, pl.ds(8 + p, 1), :])
        ours = pl.ds(pl.multiple_of((plane * SPLIT + c * 2 + y) * cap, 16), cap)
        theirs = pl.ds(pl.multiple_of(plane * cap, 16), cap)
        total = part[ours, back_cols(j)].astype(jnp.float32) + r2[theirs, back_cols(j)].astype(jnp.float32)
        pair[plane, :cap, back_cols(j)] = (total * weight).astype(pair.dtype)
        pl.when(jnp.logical_and(at_end, plane != p))(slots_home(plane, j).start)

    def spread_out(plane, both, at):
        amount = 2 * cap if both else cap
        return lax.dot_general(
            spreader[plane, :amount, :],
            pair[plane, :amount, at],
            (((0,), (0,)), ((), ())),
            preferred_element_type=jnp.float32,
        )

    def fold_home(i, j):
        plane = home_of(i)
        at = back_cols(j)

        def fold(both, extra, last):
            if both:
                landed(pair.at[plane, pl.ds(cap, cap), at], pair_recv.at[plane, j])
            if extra:
                landed(acc_in.at[plane, :, at], acc_recv.at[plane, j])
            total = spread_out(plane, both, at)
            if extra:
                total = total + acc_in[plane, :, at].astype(jnp.float32)
            if last:
                out_ref[:, at] = (mod_ref[2:3, at] * total + out_ref[:, at].astype(jnp.float32)).astype(
                    out_ref.dtype
                )
            else:
                acc_out[plane, :, at] = total.astype(acc_out.dtype)
                rows_home(plane, j).start()

        pl.when(jnp.logical_and(at_end, i == 3))(lambda: fold(False, True, True))
        pl.when(jnp.logical_and(middle, i == 3))(lambda: fold(True, True, True))
        pl.when(jnp.logical_and(middle, i == 2))(lambda: fold(False, True, False))
        pl.when(jnp.logical_and(middle, i < 2))(lambda: fold(True, False, False))

    out_ref[:, halves(mine_from)] = att[:rows, :]
    out_ref[:, halves(other_from)] = line[partner_plane, rows:, :]
    units = planes * backs

    def give_back(u, carry):
        for behind, act in ((0, produce), (BACK_LAGS[0], fold_twin), (BACK_LAGS[1], fold_beside), (BACK_LAGS[2], fold_home)):
            at = u - behind
            i, j = lax.div(at, backs), lax.rem(at, backs)
            pl.when(jnp.logical_and(at >= 0, at < units))(functools.partial(act, i, j))
        return carry

    lax.fori_loop(0, units + BACK_LAGS[2], give_back, 0)

    def left(j, carry):
        for i in range(3):
            over_vertical(i, j).wait_send()
        pl.when(middle)(rest_copy(inner, j).wait_send)
        for i in (0, 1):
            for level in (0, 1):
                for index, (_, exists) in enumerate(sides):
                    when(exists, over_side(level, index, i, j).wait_send)
        for k, (src, _, whole, out) in enumerate(sources):
            if whole is not False:
                when(whole, raw_copy(k, src, j).wait_send)
            if out is not False:
                when(out, outer_copy(k, src, j).wait_send)
            for index in (0, 1):
                plane_copy(k, src, j, index).wait_send()
            twin_copy(k, src, j).wait_send()
        return carry

    lax.fori_loop(0, chunks, left, 0)
    for copy in tell(tables, table_send, table_recv) + tell(stats, stat_send, stat_recv):
        copy.wait_send()

    def returned(j, carry):
        for plane in range(planes):
            to_twin(plane, j).wait_send()
            to_beside(plane, j).wait_send()
            away = p != plane
            pl.when(jnp.logical_and(at_end, away))(slots_home(plane, j).wait_send)
            pl.when(jnp.logical_and(middle, away))(rows_home(plane, j).wait_send)
        return carry

    lax.fori_loop(0, backs, returned, 0)


def kernel_bytes(n, rows, cap, width):
    planes = n // SPLIT
    lines = 2 * 6 * rows + 2 * n * cap + planes * (6 * cap + 3 * rows) + SPLIT * cap + 3 * rows
    return 2 * (lines * D + 2 * width * D)


def layer(queries, key_rows, values, modulation, expert_in, expert_out, routes, gate_fixed):
    n = lax.axis_size("tile")
    rows = queries.shape[0]
    width = expert_in.shape[1]
    planes = n // SPLIT
    cap = 3 * rows // planes
    chunks, backs = CHUNKS, BACK_CHUNKS
    vmem = pl.BlockSpec(memory_space=pltpu.VMEM)
    hbm = pl.BlockSpec(memory_space=pl.ANY)
    dma = pltpu.SemaphoreType.DMA
    bf = jnp.bfloat16
    return pl.pallas_call(
        functools.partial(layer_kernel, n, rows, cap, CHUNKS, BACK_CHUNKS),
        name="whole_layer",
        out_shape=jax.ShapeDtypeStruct((rows, D), bf),
        in_specs=[hbm, hbm, hbm, vmem, vmem, vmem, hbm, hbm],
        out_specs=vmem,
        scratch_shapes=[
            pltpu.VMEM((2 * rows, D // 2), bf),
            pltpu.VMEM((2 * rows, D // 2), bf),
            pltpu.VMEM((8, 6 * rows), jnp.float32),
            pltpu.VMEM((6 * rows, D // 2), bf),
            pltpu.VMEM((6 * rows, D // 2), bf),
            pltpu.VMEM((planes, 2 * rows, D // 2), bf),
            pltpu.VMEM((n, 2 * cap, D // 2), bf),
            pltpu.VMEM((planes, 2 * cap, D // 2), bf),
            pltpu.VMEM((planes, 4 * cap, 2 * rows), bf),
            pltpu.VMEM((planes, 2 * cap, rows), bf),
            pltpu.VMEM((n, 16, rows), jnp.float32),
            pltpu.VMEM((n, 8, rows), jnp.float32),
            pltpu.VMEM((SPLIT * cap, D), bf),
            pltpu.VMEM((D, width), bf),
            pltpu.VMEM((width, D), bf),
            pltpu.VMEM((SPLIT * cap, width), bf),
            pltpu.VMEM((n * cap, D), bf),
            pltpu.VMEM((planes * 2 * cap, D), bf),
            pltpu.VMEM((planes * cap, D), bf),
            pltpu.VMEM((planes, 2 * cap, D), bf),
            pltpu.VMEM((planes, rows, D), bf),
            pltpu.VMEM((planes, rows, D), bf),
            dma((5,)),
            dma((11, chunks)),
            dma((13, chunks)),
            dma((n - 1,)),
            dma((n,)),
            dma((n - 1,)),
            dma((n,)),
            dma((planes, 5, chunks)),
            dma((planes, chunks)),
            dma((n, chunks)),
            dma((chunks,)),
            dma((planes, 4, backs)),
            dma((planes, backs)),
            dma((planes, backs)),
            dma((planes, backs)),
            dma((planes, backs)),
        ],
        compiler_params=pltpu.CompilerParams(
            collective_id=1, has_side_effects=True, vmem_limit_bytes=VMEM_LIMIT
        ),
    )(queries, key_rows, values, modulation, routes.T, gate_fixed.T, expert_in, expert_out)


def slot_table(flat, experts_count):
    onehot = (flat[:, None] == jnp.arange(experts_count, dtype=jnp.int32)[None, :]).astype(
        jnp.int32
    )
    before = jnp.cumsum(onehot, axis=0) - onehot
    return jnp.sum(before * onehot, axis=1)


def expert_apply(rows, first_weight, second_weight):
    hidden = jax.nn.gelu(
        jnp.dot(rows, first_weight, preferred_element_type=jnp.float32), approximate=True
    ).astype(jnp.bfloat16)
    return jnp.dot(hidden, second_weight, preferred_element_type=jnp.float32).astype(jnp.bfloat16)


def experts_sparse(normed, attended, modulation, expert_in, expert_out, routes, gate_fixed):
    devices = lax.axis_size("tile")
    rows_dev = normed.shape[0]
    experts_count = devices // SPLIT
    capacity = 3 * rows_dev // experts_count
    flat = routes.reshape(-1)
    slots = slot_table(flat, experts_count)
    target = flat * capacity + slots
    chooser = (
        target[None, :] == jnp.arange(experts_count * capacity, dtype=jnp.int32)[:, None]
    ).astype(jnp.bfloat16)
    chooser = chooser.reshape(experts_count * capacity, rows_dev, 2).sum(axis=2)
    buffer = jnp.dot(chooser, normed, preferred_element_type=jnp.float32).astype(jnp.bfloat16)
    copies = jnp.broadcast_to(
        buffer.reshape(experts_count, 1, capacity, D), (experts_count, SPLIT, capacity, D)
    ).reshape(devices, capacity, D)
    received = lax.all_to_all(copies, "tile", split_axis=0, concat_axis=0, tiled=True)
    sources = received.shape[0]
    count = received.shape[1]
    partial_value = expert_apply(received.reshape(sources * count, D), expert_in, expert_out)
    returned = lax.all_to_all(
        partial_value.reshape(sources, count, D), "tile", split_axis=0, concat_axis=0, tiled=True
    )
    summed = jnp.sum(
        returned.reshape(experts_count, SPLIT, capacity, D).astype(jnp.float32), axis=1
    )
    expert_rows = summed.astype(jnp.bfloat16).reshape(experts_count * capacity, D)
    picked = jnp.take(expert_rows, target, axis=0).reshape(rows_dev, 2, D)
    gate_scale = gate_fixed.astype(jnp.float32) / 1024.0
    mixture = jnp.sum(picked.astype(jnp.float32) * gate_scale[:, :, None], axis=1)
    return (attended.astype(jnp.float32) + modulation[2] * mixture).astype(jnp.bfloat16)


def shards(queries, key_rows, values, modulation, expert_in, expert_out, routes, gate_fixed):
    n = lax.axis_size("tile")
    cap = 3 * queries.shape[0] // (n // SPLIT)
    if n == 2 * TILE_COLS and cap % 16 == 0 and kernel_bytes(n, queries.shape[0], cap, expert_in.shape[1]) < VMEM_LIMIT * 7 // 8:
        return layer(queries, key_rows, values, modulation, expert_in, expert_out, routes, gate_fixed)
    attended, normed = attention(queries, key_rows, values, modulation)
    return experts_sparse(normed, attended, modulation, expert_in, expert_out, routes, gate_fixed)


def solution(mesh):
    placed = (
        P(("groups", "tile"), None),
        P(("groups", "tile"), None),
        P(("groups", "tile"), None),
        P("groups", None),
        P(None, "tile"),
        P("tile", None),
        P(("groups", "tile"), None),
        P(("groups", "tile"), None),
    )
    return jax.shard_map(
        shards, mesh=mesh, in_specs=placed, out_specs=P(("groups", "tile"), None), check_vma=False
    )
```

```python
import functools
import math

import jax
import jax.numpy as jnp
from jax import lax
from jax.experimental import pallas as pl
from jax.experimental.pallas import tpu as pltpu
from jax.sharding import PartitionSpec as P

HEAD_DIM = 128
D = 4096
SPLIT = 4
TILE_COLS = 8

EPSILON = 1e-06
MASKED = -1e30
MESH = pl.DeviceIdType.MESH
VMEM_LIMIT = 60 * 1024 * 1024
CHUNKS = 8
AHEAD = 2
ASIDE = 2
BEHIND = 2
HOP = 2
BACK_CHUNKS = 4
BACK_LAGS = (1, 4, 6)


def when(cond, body):
    if cond is True:
        body()
    else:
        pl.when(cond)(body)


def both(a, b):
    if a is True:
        return b
    if b is True:
        return a
    return jnp.logical_and(a, b)


def remote(src, dst, send_sem, recv_sem, target):
    return pltpu.make_async_remote_copy(
        src_ref=src,
        dst_ref=dst,
        send_sem=send_sem,
        recv_sem=recv_sem,
        device_id={"tile": target},
        device_id_type=MESH,
    )


def halo_levels(n):
    grid_rows = n // TILE_COLS
    if grid_rows < 2:
        return 1
    return 2 if grid_rows == 2 else 3


def attention_kernel(
    n, rows, q_ref, k_ref, v_ref, mod_ref, att_ref, norm_ref, keys, vals, send_sem, recv_sem, own_sem,
):
    me = lax.axis_index("tile")
    grid_rows = n // TILE_COLS
    tile = lax.rem(me + TILE_COLS // 2, n)
    row = lax.div(tile, TILE_COLS)
    col = lax.rem(tile, TILE_COLS)
    if grid_rows < 2:
        verticals = []
    elif grid_rows == 2:
        verticals = [(1, TILE_COLS, True, 1)]
    else:
        verticals = [(1, n - TILE_COLS, row > 0, 2), (2, TILE_COLS, row < grid_rows - 1, 1)]
    sides = [(-1, col > 0), (1, col < TILE_COLS - 1)]
    here = {level: exists for level, _, exists, _ in verticals}
    here[0] = True

    def slot(level, side):
        return level * 3 + 1 + side

    def place(buf, s):
        return buf.at[pl.ds(s * rows, rows), :]

    def over(offset):
        return lax.rem(me + offset + n, n)

    half = rows // 2
    middle = TILE_COLS // 2
    crossing = {side: col == (middle if side < 0 else middle - 1) for side, _ in sides}
    two = grid_rows == 2

    def part_of(buf, s, h):
        return buf.at[pl.ds(pl.multiple_of(s * rows + h * half, half), half), :]

    own = [
        pltpu.make_async_copy(src, place(buf, slot(0, 0)), own_sem.at[i])
        for i, (src, buf) in enumerate(((k_ref, keys), (v_ref, vals)))
    ]
    for copy in own:
        copy.start()

    def beside(side):
        if not two:
            return over(side)
        return jnp.where(crossing[side], over(side + TILE_COLS), over(side))

    def level_there(level, side):
        return jnp.where(crossing[side], 1 - level, level) if two else level

    barrier = pltpu.get_barrier_semaphore()
    partners = [(over(offset), exists) for _, offset, exists, _ in verticals]
    partners += [(beside(side), exists) for side, exists in sides]
    for target, exists in partners:

        def greet(target=target):
            pl.semaphore_signal(barrier, inc=1, device_id={"tile": target}, device_id_type=MESH)

        when(exists, greet)
    expected = sum(1 if exists is True else jnp.where(exists, 1, 0) for _, exists in partners)
    pl.semaphore_wait(barrier, expected)

    sends = []
    pieces = [(i, h) for i in (0, 1) for h in (0, 1)]
    bufs = (keys, vals)

    def push(i, h, src, there, target, exists):
        copy = remote(
            src,
            part_of(bufs[i], there, h),
            send_sem.at[len(sends)],
            recv_sem.at[there, i * 2 + h],
            target,
        )
        when(exists, copy.start)
        sends.append((copy, exists))

    def arrived(s, exists, i, h):
        ref = part_of(bufs[i], s, h)
        when(exists, remote(ref, ref, send_sem.at[0], recv_sem.at[s, i * 2 + h], me).wait_recv)

    def own_part(i, h):
        return (k_ref, v_ref)[i].at[pl.ds(h * half, half), :]

    for i, h in pieces:
        for level, offset, exists, there in verticals:
            push(i, h, own_part(i, h), slot(there, 0), over(offset), exists)
    for i, h in pieces:
        for side, exists in sides:
            push(i, h, own_part(i, h), slot(level_there(0, side), -side), beside(side), exists)
    for s in range(3 * (1 + len(verticals))):
        level, side = s // 3, s % 3 - 1
        exists = here[level]
        for other, side_exists in sides:
            if other == side:
                exists = both(exists, side_exists)
        if exists is True:
            continue

        def clear(s=s):
            for buf in (keys, vals):
                buf[pl.ds(s * rows, rows), :] = jnp.zeros((rows, D), buf.dtype)

        pl.when(jnp.logical_not(exists))(clear)
    for i, h in pieces:
        for level, offset, exists, there in verticals:
            arrived(slot(level, 0), exists, i, h)
            for side, side_exists in sides:
                push(
                    i,
                    h,
                    part_of(bufs[i], slot(level, 0), h),
                    slot(level_there(level, side), -side),
                    beside(side),
                    both(exists, side_exists),
                )
    for copy in own:
        copy.wait()
    for i, h in pieces:
        for level, exists in sorted(here.items(), key=lambda item: item[0]):
            for side, side_exists in sides:
                arrived(slot(level, side), both(exists, side_exists), i, h)

    span = 3 * (1 + len(verticals)) * rows
    where = lax.broadcasted_iota(jnp.int32, (rows, span), 1)
    bias = jnp.zeros((rows, span), jnp.float32)
    for s in range(span // rows):
        level, side = s // 3, s % 3 - 1
        exists = here[level]
        for other, side_exists in sides:
            if other == side:
                exists = both(exists, side_exists)
        if exists is True:
            continue
        penalty = jnp.where(exists, 0.0, MASKED)
        bias = jnp.where((where >= s * rows) & (where < (s + 1) * rows), penalty, bias)
    scale = 1.0 / math.sqrt(HEAD_DIM)
    together = 8

    def heads(step, carry):
        for extra in range(together):
            at = pl.ds(pl.multiple_of((step * together + extra) * HEAD_DIM, HEAD_DIM), HEAD_DIM)
            scores = lax.dot_general(
                q_ref[:, at], keys[:, at], (((1,), (1,)), ((), ())), preferred_element_type=jnp.float32
            )
            scores = scores * scale + bias
            raised = jnp.exp(scores - jnp.max(scores, axis=-1, keepdims=True))
            probs = (raised * (1.0 / jnp.sum(raised, axis=-1, keepdims=True))).astype(jnp.bfloat16)
            att_ref[:, at] = jnp.dot(probs, vals[:, at], preferred_element_type=jnp.float32).astype(
                att_ref.dtype
            )
        return carry

    lax.fori_loop(0, D // HEAD_DIM // together, heads, 0)

    def normalise(step, carry):
        at = pl.ds(pl.multiple_of(step * 16, 16), 16)
        wide = att_ref[at, :].astype(jnp.float32)
        wide = wide - jnp.mean(wide, axis=-1, keepdims=True)
        spread = jnp.mean(wide * wide, axis=-1, keepdims=True)
        normed = wide * lax.rsqrt(spread + EPSILON)
        norm_ref[at, :] = (normed * (1.0 + mod_ref[1:2, :]) + mod_ref[0:1, :]).astype(norm_ref.dtype)
        return carry

    lax.fori_loop(0, rows // 16, normalise, 0)
    for copy, exists in sends:
        when(exists, copy.wait_send)


def attention(queries, key_rows, values, modulation):
    n = lax.axis_size("tile")
    rows = queries.shape[0]
    levels = halo_levels(n)
    slots = 3 * levels
    vmem = pl.BlockSpec(memory_space=pltpu.VMEM)
    hbm = pl.BlockSpec(memory_space=pl.ANY)
    return pl.pallas_call(
        functools.partial(attention_kernel, n, rows),
        name="halo_attention",
        out_shape=(
            jax.ShapeDtypeStruct((rows, D), jnp.bfloat16),
            jax.ShapeDtypeStruct((rows, D), jnp.bfloat16),
        ),
        in_specs=[vmem, hbm, hbm, vmem],
        out_specs=(vmem, vmem),
        scratch_shapes=[
            pltpu.VMEM((slots * rows, D), jnp.bfloat16),
            pltpu.VMEM((slots * rows, D), jnp.bfloat16),
            pltpu.SemaphoreType.DMA((4 * (2 + 3 * (levels - 1)),)),
            pltpu.SemaphoreType.DMA((slots, 4)),
            pltpu.SemaphoreType.DMA((2,)),
        ],
        compiler_params=pltpu.CompilerParams(
            collective_id=0, has_side_effects=True, vmem_limit_bytes=VMEM_LIMIT
        ),
    )(queries, key_rows, values, modulation)


def device(plane, yy, cc):
    return plane * SPLIT + yy * 2 + cc


def layer_kernel(
    n, rows, cap, chunks, backs, q_ref, k_ref, v_ref, mod_ref, routes_ref, gates_ref, first_ref, second_ref,
    out_ref, att, asked, bias, keys, vals, line, tokens, stage, chooser, spreader, tables, stats, normed,
    first, second, hidden, part, r1, r2, pair, acc_in, acc_out,
    own_sem, kv_send, kv_recv, table_send, table_recv, stat_send, stat_recv, out_send, line_recv,
    token_recv, rest_send, back_send, s1_recv, s2_recv, pair_recv, acc_recv,
):
    planes = n // SPLIT
    width = first.shape[1]
    half = D // 2
    wide = half // chunks
    me = lax.axis_index("tile")
    p = lax.div(me, SPLIT)
    y = lax.div(lax.rem(me, SPLIT), 2)
    c = lax.rem(me, 2)
    beside = device(p, 1 - y, c)
    twin = device(p, y, 1 - c)
    low_half = p < planes // 2
    toward = jnp.where(low_half, 1, -1)
    inner = p + toward
    outer = p - toward
    at_end = jnp.logical_or(p == 0, p == planes - 1)
    middle = jnp.logical_not(at_end)
    outer_expert = jnp.where(low_half, 0, planes - 1)
    inner_device = device(inner, y, c)
    outer_device = device(jnp.where(at_end, p, outer), y, c)

    tile = lax.rem(me + TILE_COLS // 2, n)
    column = lax.rem(tile, TILE_COLS)
    partner = lax.rem(me + TILE_COLS, n)
    sides = [(-1, column > 0), (1, column < TILE_COLS - 1)]
    half_way = TILE_COLS // 2
    crossing = {-1: column == half_way, 1: column == half_way - 1}

    def part_of_plane(plane):
        return jnp.where(plane < planes // 2, half, 0)

    mine_from = part_of_plane(p)
    other_from = half - mine_from
    partner_plane = lax.rem(p + planes // 2, planes)

    def cols(j, base=0):
        return pl.ds(pl.multiple_of(base + j * wide, wide), wide)

    def halves(base):
        return pl.ds(pl.multiple_of(base, half), half)

    def lines(buf, s):
        return buf.at[pl.ds(pl.multiple_of(s * rows, rows), rows), :]

    loads = [
        pltpu.make_async_copy(q_ref.at[:, halves(mine_from)], lines(asked, 0), own_sem.at[0]),
        pltpu.make_async_copy(k_ref.at[:, halves(mine_from)], lines(keys, 1), own_sem.at[1]),
        pltpu.make_async_copy(v_ref.at[:, halves(mine_from)], lines(vals, 1), own_sem.at[2]),
        pltpu.make_async_copy(first_ref, first, own_sem.at[3]),
        pltpu.make_async_copy(second_ref, second, own_sem.at[4]),
    ]

    barrier = pltpu.get_barrier_semaphore()
    others = [lax.rem(me + step, n) for step in range(1, n)]
    for target in others:
        pl.semaphore_signal(barrier, inc=1, device_id={"tile": target}, device_id_type=MESH)

    def beside_tile(side):
        return lax.rem(me + side + jnp.where(crossing[side], TILE_COLS, 0) + n, n)

    def slot_there(level, side):
        return jnp.where(crossing[side], 1 - level, level) * 3 + 1 - side

    bufs = (keys, vals, asked)
    given = (k_ref, v_ref, q_ref)

    def place(i, s, j):
        return bufs[i].at[pl.ds(pl.multiple_of(s * rows, rows), rows), cols(j)]

    def over_vertical(i, j):
        return remote(
            given[i].at[:, cols(j, other_from)],
            place(i, 4 if i < 2 else 1, j),
            kv_send.at[i, j],
            kv_recv.at[8 + i if i < 2 else 12, j],
            partner,
        )

    def over_side(level, index, i, j):
        side = sides[index][0]
        there = slot_there(level, side)
        source = given[i].at[:, cols(j, mine_from)] if level == 0 else place(i, 4, j)
        return remote(
            source,
            place(i, there, j),
            kv_send.at[3 + level * 4 + index * 2 + i, j],
            kv_recv.at[there * 2 + i, j],
            beside_tile(side),
        )

    def landed(ref, sem):
        remote(ref, ref, own_sem.at[0], sem, me).wait_recv()

    def send_own(j):
        for i in range(3):
            over_vertical(i, j).start()

    def send_side(j):
        for i in (0, 1):
            for index, (_, exists) in enumerate(sides):
                when(exists, over_side(0, index, i, j).start)

    def send_vertical(j):
        for i in (0, 1):
            landed(place(i, 4, j), kv_recv.at[8 + i, j])
            for index, (_, exists) in enumerate(sides):
                when(exists, over_side(1, index, i, j).start)

    expert = lax.broadcasted_iota(jnp.int32, (8, rows), 0)
    named = [routes_ref[k : k + 1, :] == expert for k in (0, 1)]
    member = jnp.logical_or(named[0], named[1])
    upto = (
        lax.broadcasted_iota(jnp.int32, (rows, rows), 0) <= lax.broadcasted_iota(jnp.int32, (rows, rows), 1)
    ).astype(jnp.float32).astype(jnp.bfloat16)
    count = jnp.dot(
        member.astype(jnp.float32).astype(jnp.bfloat16), upto, preferred_element_type=jnp.float32
    )
    gate = sum(
        jnp.where(named[k], gates_ref[k : k + 1, :].astype(jnp.float32), 0.0) for k in (0, 1)
    )
    tables[me, 0:8, :] = jnp.where(member, count - 1.0, -1.0)
    stats[me, 8:16, :] = jnp.where(member, count - 1.0, -1.0)
    tables[me, 8:16, :] = gate / 1024.0

    span = 6 * rows
    where = lax.broadcasted_iota(jnp.int32, (8, span), 1)
    penalty = jnp.zeros((8, span), jnp.float32)
    for s in range(6):
        for side, exists in sides:
            if side != s % 3 - 1:
                continue
            here = (where >= s * rows) & (where < (s + 1) * rows)
            penalty = jnp.where(here, jnp.where(exists, 0.0, MASKED), penalty)

            def clear(s=s):
                for buf in (keys, vals):
                    buf[s * rows : (s + 1) * rows, :] = jnp.zeros((rows, half), buf.dtype)

            pl.when(jnp.logical_not(exists))(clear)
    bias[...] = penalty

    column_planes = [lax.rem(p + step, planes) for step in range(1, planes)]

    def tell_column(step):
        there = device(column_planes[step], y, c)
        return remote(tables.at[me], tables.at[me], table_send.at[step], table_recv.at[p], there)

    def tell_all():
        return [
            remote(stats.at[me], stats.at[me], stat_send.at[step], stat_recv.at[me], target)
            for step, target in enumerate(others)
        ]

    pl.semaphore_wait(barrier, n - 1)
    send_own(0)
    for step in range(planes - 1):
        tell_column(step).start()
    send_side(0)
    for load in loads[:3]:
        load.start()
    for j in range(1, max(AHEAD, ASIDE)):
        if j < min(AHEAD, chunks):
            send_own(j)
        if j < min(ASIDE, chunks):
            send_side(j)
    for load in loads[:3]:
        load.wait()
    for load in loads[3:]:
        load.start()

    slot_line = lax.broadcasted_iota(jnp.int32, (cap, rows), 0).astype(jnp.float32)

    def chosen(tile_there, e):
        return tables[tile_there, pl.ds(e, 1), :] == slot_line

    def picked_column(which, row):
        return jnp.sum(jnp.where(which, row, 0.0), axis=1, keepdims=True)

    def choose():
        for plane in column_planes:
            landed(tables.at[device(plane, y, c)], table_recv.at[plane])
        chooser[...] = jnp.zeros(chooser.shape, chooser.dtype)
        for plane in range(planes):
            for place_in, e in ((0, p), (1, outer_expert)):
                found = chosen(device(plane, y, c), e).astype(jnp.float32).astype(jnp.bfloat16)
                at = place_in * 2 * cap
                spreader[plane, place_in * cap : (place_in + 1) * cap, :] = found
                chooser[plane, at : at + cap, :rows] = found
                chooser[(plane + planes // 2) % planes, at + cap : at + 2 * cap, rows:] = found

    scale = 1.0 / math.sqrt(HEAD_DIM)

    def attend(j):
        for level in (0, 1):
            for side, exists in sides:
                s = level * 3 + 1 + side
                for i in (0, 1):
                    when(exists, functools.partial(landed, place(i, s, j), kv_recv.at[s * 2 + i, j]))
        landed(place(2, 1, j), kv_recv.at[12, j])
        for extra in range(wide // HEAD_DIM):
            at = pl.ds(pl.multiple_of(j * wide + extra * HEAD_DIM, HEAD_DIM), HEAD_DIM)
            scores = lax.dot_general(
                asked[:, at], keys[:, at], (((1,), (1,)), ((), ())), preferred_element_type=jnp.float32
            )
            scores = scores * scale + bias[0:1, :]
            raised = jnp.exp(scores - jnp.max(scores, axis=-1, keepdims=True))
            probs = (raised * (1.0 / jnp.sum(raised, axis=-1, keepdims=True))).astype(jnp.bfloat16)
            att[:, at] = jnp.dot(probs, vals[:, at], preferred_element_type=jnp.float32).astype(att.dtype)

    def raw_copy(k, src, j):
        source = att.at[:, cols(j)] if k == 0 else line.at[src, :, cols(j)]
        return remote(source, line.at[src, :, cols(j)], out_send.at[k, 0, j], line_recv.at[src, j], inner_device)

    def outer_copy(k, src, j):
        there = device(src, y, c)
        return remote(
            stage.at[src, :, cols(j)],
            tokens.at[there, :, cols(j)],
            out_send.at[k, 1, j],
            token_recv.at[there, j],
            outer_device,
        )

    def rest_copy(src, j):
        ref = line.at[src, pl.ds(rows, rows), cols(j)]
        return remote(ref, ref, rest_send.at[j], line_recv.at[src, j], outer_device)

    def rest_landed(j):
        landed(line.at[partner_plane, pl.ds(rows, rows), cols(j)], line_recv.at[partner_plane, j])

    def plane_copy(k, src, j, index):
        ref = tokens.at[device(src, y, c), :, cols(j)]
        return remote(
            ref, ref, out_send.at[k, 2 + index, j], token_recv.at[device(src, y, c), j], (beside, twin)[index]
        )

    def twin_copy(k, src, j):
        there = device(src, 1 - y, c)
        ref = tokens.at[there, :, cols(j)]
        return remote(ref, ref, out_send.at[k, 4, j], token_recv.at[there, j], twin)

    far = jnp.where(at_end, p + 3 * toward, p + 2 * toward)
    second_plane = jnp.where(at_end, p + 2 * toward, outer)
    sources = [
        (p, BEHIND, True, middle),
        (inner, BEHIND + HOP, False, middle),
        (second_plane, BEHIND + HOP * jnp.where(at_end, 2, 1), middle, False),
        (far, BEHIND + HOP * jnp.where(at_end, 3, 2), False, middle),
    ]

    def relay(k, j):
        src, behind, whole, out = sources[k]
        jj = j - behind

        def go():
            there = device(src, y, c)
            if k > 0:
                pl.when(at_end)(
                    lambda: landed(tokens.at[there, :, cols(jj)], token_recv.at[there, jj])
                )
                pl.when(middle)(lambda: landed(line.at[src, :, cols(jj)], line_recv.at[src, jj]))
            if whole is not False:
                when(whole, raw_copy(k, src, jj).start)
            if k == 1:
                pl.when(middle)(rest_copy(src, jj).start)

            def pick():
                rows_here = att[:, cols(jj)] if k == 0 else line[src, :, cols(jj)]
                picked = jnp.dot(chooser[src], rows_here, preferred_element_type=jnp.float32).astype(
                    tokens.dtype
                )
                tokens[there, :, cols(jj)] = picked[: 2 * cap]
                stage[src, :, cols(jj)] = picked[2 * cap :]

            when(True if k == 0 else middle, pick)
            if out is not False:
                when(out, outer_copy(k, src, jj).start)
            for index in (0, 1):
                plane_copy(k, src, jj, index).start()

        pl.when(jnp.logical_and(jj >= 0, jj < chunks))(go)

    def pass_on(k, j):
        src, behind, _, _ = sources[k]
        jj = j - behind - HOP

        def go():
            there = device(src, 1 - y, c)
            landed(tokens.at[there, :, cols(jj)], token_recv.at[there, jj])
            twin_copy(k, src, jj).start()

        pl.when(jnp.logical_and(jj >= 0, jj < chunks))(go)

    def move(j):
        for k in range(planes):
            relay(k, j)
        for k in range(planes):
            pass_on(k, j)

    def stream(j, carry):
        pl.when(j < chunks)(lambda: send_vertical(j))

        pl.when(j + AHEAD < chunks)(lambda: send_own(j + AHEAD))
        pl.when(j + ASIDE < chunks)(lambda: send_side(j + ASIDE))
        pl.when(j == BEHIND)(choose)
        pl.when(j >= BEHIND)(lambda: attend(j - BEHIND))
        move(j)
        return carry

    lax.fori_loop(0, chunks + BEHIND, stream, 0)

    token = lax.broadcasted_iota(jnp.int32, (16, rows), 1)
    line_of = lax.broadcasted_iota(jnp.int32, (16, rows), 0)
    row_number = lax.broadcasted_iota(jnp.int32, (8, rows), 0)
    found = jnp.zeros((8, rows), jnp.float32)
    for step in range(2 * rows // 16):
        some = att[step * 16 : (step + 1) * 16, :].astype(jnp.float32)
        mean = jnp.mean(some, axis=-1, keepdims=True)
        some = some - mean
        spread = jnp.mean(some * some, axis=-1, keepdims=True)
        which, at = divmod(step * 16, rows)
        for kind, value in enumerate((mean, spread)):
            row = jnp.sum(jnp.where(token == line_of + at, value, 0.0), axis=0, keepdims=True)
            found = found + jnp.where(row_number == 2 * which + kind, row, 0.0)
    stats[me, 0:8, :] = found
    for copy in tell_all():
        copy.start()

    def drain(j, carry):
        move(j)
        return carry

    lax.fori_loop(chunks + BEHIND, chunks + BEHIND + 4 * HOP, drain, 0)
    for target in others:
        landed(stats.at[target], stat_recv.at[target])
    for load in loads[3:]:
        load.wait()

    order = [
        jnp.where(at_end, p + 3 * toward, p + 2 * toward),
        jnp.where(at_end, p + 2 * toward, inner),
        jnp.where(at_end, inner, outer),
        p,
    ]
    def arrive(j, carry):
        for plane in range(planes):
            for yy in (0, 1):
                there = device(plane, yy, 1 - c)
                landed(tokens.at[there, :, cols(j)], token_recv.at[there, j])
        pl.when(at_end)(lambda: rest_landed(j))
        return carry

    lax.fori_loop(0, chunks, arrive, 0)
    group = SPLIT * cap
    chunk = 512
    span_back = D // backs

    def home_of(i):
        return jnp.where(i == 0, order[0], jnp.where(i == 1, order[1], jnp.where(i == 2, order[2], order[3])))

    def block(buf, index, count, j):
        return buf.at[pl.ds(pl.multiple_of(index * cap, 16), count * cap), back_cols(j)]

    def back_cols(j):
        return pl.ds(pl.multiple_of(j * span_back, span_back), span_back)

    def start_group(plane):
        def normalise(t, carry):
            yy, cc = lax.rem(t, 2), lax.div(t, 2)
            there = device(plane, yy, cc)
            across = lax.rem(there + TILE_COLS, n)
            mean_here, mean_there = stats[there, 0:1, :], stats[across, 2:3, :]
            apart = 0.5 * (mean_here - mean_there)
            spread = 0.5 * (stats[there, 1:2, :] + stats[across, 3:4, :]) + apart * apart
            which = stats[there, pl.ds(8 + p, 1), :] == slot_line
            mean = picked_column(which, 0.5 * (mean_here + mean_there))
            rate = picked_column(which, lax.rsqrt(spread + EPSILON))
            at = pl.ds(pl.multiple_of(t * cap, 16), cap)
            base = part_of_plane(plane)
            for source, lower, start in ((there, 0, base), (across, cap, half - base)):
                for step in range(half // chunk):
                    some = slice(step * chunk, (step + 1) * chunk)
                    to = pl.ds(pl.multiple_of(start + step * chunk, chunk), chunk)
                    value = (tokens[source, lower : lower + cap, some].astype(jnp.float32) - mean) * rate
                    normed[at, to] = (value * (1.0 + mod_ref[1:2, to]) + mod_ref[0:1, to]).astype(
                        normed.dtype
                    )
            return carry

        lax.fori_loop(0, SPLIT, normalise, 0)
        raw = jnp.dot(normed[...], first[...], preferred_element_type=jnp.float32)
        hidden[...] = jax.nn.gelu(raw, approximate=True).astype(hidden.dtype)

    def to_twin(plane, j):
        return remote(
            block(part, plane * SPLIT + (1 - c) * 2, 2, j),
            block(r1, plane * 2, 2, j),
            back_send.at[plane, 0, j],
            s1_recv.at[plane, j],
            twin,
        )

    def to_beside(plane, j):
        return remote(
            block(part, plane * SPLIT + c * 2 + 1 - y, 1, j),
            block(r2, plane, 1, j),
            back_send.at[plane, 1, j],
            s2_recv.at[plane, j],
            beside,
        )

    def slots_home(plane, j):
        return remote(
            pair.at[plane, pl.ds(0, cap), back_cols(j)],
            pair.at[plane, pl.ds(cap, cap), back_cols(j)],
            back_send.at[plane, 2, j],
            pair_recv.at[plane, j],
            inner_device,
        )

    def rows_home(plane, j):
        return remote(
            acc_out.at[plane, :, back_cols(j)],
            acc_in.at[plane, :, back_cols(j)],
            back_send.at[plane, 3, j],
            acc_recv.at[plane, j],
            device(jnp.where(plane == outer, outer, inner), y, c),
        )

    def produce(i, j):
        plane = home_of(i)
        pl.when(j == 0)(lambda: start_group(plane))
        raw = jnp.dot(hidden[...], second[:, back_cols(j)], preferred_element_type=jnp.float32)
        mine = pl.ds(pl.multiple_of(plane * group, 16), group)
        part[mine, back_cols(j)] = raw.astype(part.dtype)
        to_twin(plane, j).start()

    def fold_twin(i, j):
        plane = home_of(i)
        landed(block(r1, plane * 2, 2, j), s1_recv.at[plane, j])
        for yy in (1 - y, y):
            at = pl.ds(pl.multiple_of((plane * SPLIT + c * 2 + yy) * cap, 16), cap)
            there = pl.ds(pl.multiple_of((plane * 2 + yy) * cap, 16), cap)
            total = part[at, back_cols(j)].astype(jnp.float32) + r1[there, back_cols(j)].astype(jnp.float32)
            part[at, back_cols(j)] = total.astype(part.dtype)
            if yy is not y:
                to_beside(plane, j).start()

    def fold_beside(i, j):
        plane = home_of(i)
        there = device(plane, y, c)
        landed(block(r2, plane, 1, j), s2_recv.at[plane, j])
        weight = picked_column(chosen(there, p), tables[there, pl.ds(8 + p, 1), :])
        ours = pl.ds(pl.multiple_of((plane * SPLIT + c * 2 + y) * cap, 16), cap)
        theirs = pl.ds(pl.multiple_of(plane * cap, 16), cap)
        total = part[ours, back_cols(j)].astype(jnp.float32) + r2[theirs, back_cols(j)].astype(jnp.float32)
        pair[plane, :cap, back_cols(j)] = (total * weight).astype(pair.dtype)
        pl.when(jnp.logical_and(at_end, plane != p))(slots_home(plane, j).start)

    def spread_out(plane, both, at):
        amount = 2 * cap if both else cap
        return lax.dot_general(
            spreader[plane, :amount, :],
            pair[plane, :amount, at],
            (((0,), (0,)), ((), ())),
            preferred_element_type=jnp.float32,
        )

    def fold_home(i, j):
        plane = home_of(i)
        at = back_cols(j)

        def fold(both, extra, last):
            if both:
                landed(pair.at[plane, pl.ds(cap, cap), at], pair_recv.at[plane, j])
            if extra:
                landed(acc_in.at[plane, :, at], acc_recv.at[plane, j])
            total = spread_out(plane, both, at)
            if extra:
                total = total + acc_in[plane, :, at].astype(jnp.float32)
            if last:
                out_ref[:, at] = (mod_ref[2:3, at] * total + out_ref[:, at].astype(jnp.float32)).astype(
                    out_ref.dtype
                )
            else:
                acc_out[plane, :, at] = total.astype(acc_out.dtype)
                rows_home(plane, j).start()

        pl.when(jnp.logical_and(at_end, i == 3))(lambda: fold(False, True, True))
        pl.when(jnp.logical_and(middle, i == 3))(lambda: fold(True, True, True))
        pl.when(jnp.logical_and(middle, i == 2))(lambda: fold(False, True, False))
        pl.when(jnp.logical_and(middle, i < 2))(lambda: fold(True, False, False))

    out_ref[:, halves(mine_from)] = att[:rows, :]
    out_ref[:, halves(other_from)] = line[partner_plane, rows:, :]
    units = planes * backs

    def give_back(u, carry):
        for behind, act in ((0, produce), (BACK_LAGS[0], fold_twin), (BACK_LAGS[1], fold_beside), (BACK_LAGS[2], fold_home)):
            at = u - behind
            i, j = lax.div(at, backs), lax.rem(at, backs)
            pl.when(jnp.logical_and(at >= 0, at < units))(functools.partial(act, i, j))
        return carry

    lax.fori_loop(0, units + BACK_LAGS[2], give_back, 0)

    def left(j, carry):
        for i in range(3):
            over_vertical(i, j).wait_send()
        pl.when(middle)(rest_copy(inner, j).wait_send)
        for i in (0, 1):
            for level in (0, 1):
                for index, (_, exists) in enumerate(sides):
                    when(exists, over_side(level, index, i, j).wait_send)
        for k, (src, _, whole, out) in enumerate(sources):
            if whole is not False:
                when(whole, raw_copy(k, src, j).wait_send)
            if out is not False:
                when(out, outer_copy(k, src, j).wait_send)
            for index in (0, 1):
                plane_copy(k, src, j, index).wait_send()
            twin_copy(k, src, j).wait_send()
        return carry

    lax.fori_loop(0, chunks, left, 0)
    for copy in [tell_column(step) for step in range(planes - 1)] + tell_all():
        copy.wait_send()

    def returned(j, carry):
        for plane in range(planes):
            to_twin(plane, j).wait_send()
            to_beside(plane, j).wait_send()
            away = p != plane
            pl.when(jnp.logical_and(at_end, away))(slots_home(plane, j).wait_send)
            pl.when(jnp.logical_and(middle, away))(rows_home(plane, j).wait_send)
        return carry

    lax.fori_loop(0, backs, returned, 0)


def kernel_bytes(n, rows, cap, width):
    planes = n // SPLIT
    lines = 2 * 6 * rows + 2 * n * cap + planes * (6 * cap + 3 * rows) + SPLIT * cap + 3 * rows
    return 2 * (lines * D + 2 * width * D)


def layer(queries, key_rows, values, modulation, expert_in, expert_out, routes, gate_fixed):
    n = lax.axis_size("tile")
    rows = queries.shape[0]
    width = expert_in.shape[1]
    planes = n // SPLIT
    cap = 3 * rows // planes
    chunks, backs = CHUNKS, BACK_CHUNKS
    vmem = pl.BlockSpec(memory_space=pltpu.VMEM)
    hbm = pl.BlockSpec(memory_space=pl.ANY)
    dma = pltpu.SemaphoreType.DMA
    bf = jnp.bfloat16
    return pl.pallas_call(
        functools.partial(layer_kernel, n, rows, cap, CHUNKS, BACK_CHUNKS),
        name="whole_layer",
        out_shape=pltpu.VMEM((rows, D), bf),
        in_specs=[hbm, hbm, hbm, vmem, vmem, vmem, hbm, hbm],
        out_specs=vmem,
        scratch_shapes=[
            pltpu.VMEM((2 * rows, D // 2), bf),
            pltpu.VMEM((2 * rows, D // 2), bf),
            pltpu.VMEM((8, 6 * rows), jnp.float32),
            pltpu.VMEM((6 * rows, D // 2), bf),
            pltpu.VMEM((6 * rows, D // 2), bf),
            pltpu.VMEM((planes, 2 * rows, D // 2), bf),
            pltpu.VMEM((n, 2 * cap, D // 2), bf),
            pltpu.VMEM((planes, 2 * cap, D // 2), bf),
            pltpu.VMEM((planes, 4 * cap, 2 * rows), bf),
            pltpu.VMEM((planes, 2 * cap, rows), bf),
            pltpu.VMEM((n, 16, rows), jnp.float32),
            pltpu.VMEM((n, 16, rows), jnp.float32),
            pltpu.VMEM((SPLIT * cap, D), bf),
            pltpu.VMEM((D, width), bf),
            pltpu.VMEM((width, D), bf),
            pltpu.VMEM((SPLIT * cap, width), bf),
            pltpu.VMEM((n * cap, D), bf),
            pltpu.VMEM((planes * 2 * cap, D), bf),
            pltpu.VMEM((planes * cap, D), bf),
            pltpu.VMEM((planes, 2 * cap, D), bf),
            pltpu.VMEM((planes, rows, D), bf),
            pltpu.VMEM((planes, rows, D), bf),
            dma((5,)),
            dma((11, chunks)),
            dma((13, chunks)),
            dma((planes - 1,)),
            dma((planes,)),
            dma((n - 1,)),
            dma((n,)),
            dma((planes, 5, chunks)),
            dma((planes, chunks)),
            dma((n, chunks)),
            dma((chunks,)),
            dma((planes, 4, backs)),
            dma((planes, backs)),
            dma((planes, backs)),
            dma((planes, backs)),
            dma((planes, backs)),
        ],
        compiler_params=pltpu.CompilerParams(
            collective_id=1, has_side_effects=True, vmem_limit_bytes=VMEM_LIMIT
        ),
    )(queries, key_rows, values, modulation, routes.T, gate_fixed.T, expert_in, expert_out)


def slot_table(flat, experts_count):
    onehot = (flat[:, None] == jnp.arange(experts_count, dtype=jnp.int32)[None, :]).astype(
        jnp.int32
    )
    before = jnp.cumsum(onehot, axis=0) - onehot
    return jnp.sum(before * onehot, axis=1)


def expert_apply(rows, first_weight, second_weight):
    hidden = jax.nn.gelu(
        jnp.dot(rows, first_weight, preferred_element_type=jnp.float32), approximate=True
    ).astype(jnp.bfloat16)
    return jnp.dot(hidden, second_weight, preferred_element_type=jnp.float32).astype(jnp.bfloat16)


def experts_sparse(normed, attended, modulation, expert_in, expert_out, routes, gate_fixed):
    devices = lax.axis_size("tile")
    rows_dev = normed.shape[0]
    experts_count = devices // SPLIT
    capacity = 3 * rows_dev // experts_count
    flat = routes.reshape(-1)
    slots = slot_table(flat, experts_count)
    target = flat * capacity + slots
    chooser = (
        target[None, :] == jnp.arange(experts_count * capacity, dtype=jnp.int32)[:, None]
    ).astype(jnp.bfloat16)
    chooser = chooser.reshape(experts_count * capacity, rows_dev, 2).sum(axis=2)
    buffer = jnp.dot(chooser, normed, preferred_element_type=jnp.float32).astype(jnp.bfloat16)
    copies = jnp.broadcast_to(
        buffer.reshape(experts_count, 1, capacity, D), (experts_count, SPLIT, capacity, D)
    ).reshape(devices, capacity, D)
    received = lax.all_to_all(copies, "tile", split_axis=0, concat_axis=0, tiled=True)
    sources = received.shape[0]
    count = received.shape[1]
    partial_value = expert_apply(received.reshape(sources * count, D), expert_in, expert_out)
    returned = lax.all_to_all(
        partial_value.reshape(sources, count, D), "tile", split_axis=0, concat_axis=0, tiled=True
    )
    summed = jnp.sum(
        returned.reshape(experts_count, SPLIT, capacity, D).astype(jnp.float32), axis=1
    )
    expert_rows = summed.astype(jnp.bfloat16).reshape(experts_count * capacity, D)
    picked = jnp.take(expert_rows, target, axis=0).reshape(rows_dev, 2, D)
    gate_scale = gate_fixed.astype(jnp.float32) / 1024.0
    mixture = jnp.sum(picked.astype(jnp.float32) * gate_scale[:, :, None], axis=1)
    return (attended.astype(jnp.float32) + modulation[2] * mixture).astype(jnp.bfloat16)


def shards(queries, key_rows, values, modulation, expert_in, expert_out, routes, gate_fixed):
    n = lax.axis_size("tile")
    cap = 3 * queries.shape[0] // (n // SPLIT)
    if n == 2 * TILE_COLS and cap % 16 == 0 and kernel_bytes(n, queries.shape[0], cap, expert_in.shape[1]) < VMEM_LIMIT * 7 // 8:
        return layer(queries, key_rows, values, modulation, expert_in, expert_out, routes, gate_fixed)
    attended, normed = attention(queries, key_rows, values, modulation)
    return experts_sparse(normed, attended, modulation, expert_in, expert_out, routes, gate_fixed)


def solution(mesh):
    placed = (
        P(("groups", "tile"), None),
        P(("groups", "tile"), None),
        P(("groups", "tile"), None),
        P("groups", None),
        P(None, "tile"),
        P("tile", None),
        P(("groups", "tile"), None),
        P(("groups", "tile"), None),
    )
    return jax.shard_map(
        shards, mesh=mesh, in_specs=placed, out_specs=P(("groups", "tile"), None), check_vma=False
    )
```

```python
import functools
import math

import jax
import jax.numpy as jnp
from jax import lax
from jax.experimental import pallas as pl
from jax.experimental.pallas import tpu as pltpu
from jax.sharding import PartitionSpec as P

HEAD_DIM = 128
D = 4096
SPLIT = 4
TILE_COLS = 8

EPSILON = 1e-06
MASKED = -1e30
MESH = pl.DeviceIdType.MESH
VMEM_LIMIT = 60 * 1024 * 1024
CHUNKS = 8
AHEAD = 2
ASIDE = 2
BEHIND = 2
HOP = 2
BACK_CHUNKS = 4
BACK_LAGS = (1, 4, 6)


def when(cond, body):
    if cond is True:
        body()
    else:
        pl.when(cond)(body)


def both(a, b):
    if a is True:
        return b
    if b is True:
        return a
    return jnp.logical_and(a, b)


def remote(src, dst, send_sem, recv_sem, target):
    return pltpu.make_async_remote_copy(
        src_ref=src,
        dst_ref=dst,
        send_sem=send_sem,
        recv_sem=recv_sem,
        device_id={"tile": target},
        device_id_type=MESH,
    )


def halo_levels(n):
    grid_rows = n // TILE_COLS
    if grid_rows < 2:
        return 1
    return 2 if grid_rows == 2 else 3


def attention_kernel(
    n, rows, q_ref, k_ref, v_ref, mod_ref, att_ref, norm_ref, keys, vals, send_sem, recv_sem, own_sem,
):
    me = lax.axis_index("tile")
    grid_rows = n // TILE_COLS
    tile = lax.rem(me + TILE_COLS // 2, n)
    row = lax.div(tile, TILE_COLS)
    col = lax.rem(tile, TILE_COLS)
    if grid_rows < 2:
        verticals = []
    elif grid_rows == 2:
        verticals = [(1, TILE_COLS, True, 1)]
    else:
        verticals = [(1, n - TILE_COLS, row > 0, 2), (2, TILE_COLS, row < grid_rows - 1, 1)]
    sides = [(-1, col > 0), (1, col < TILE_COLS - 1)]
    here = {level: exists for level, _, exists, _ in verticals}
    here[0] = True

    def slot(level, side):
        return level * 3 + 1 + side

    def place(buf, s):
        return buf.at[pl.ds(s * rows, rows), :]

    def over(offset):
        return lax.rem(me + offset + n, n)

    half = rows // 2
    middle = TILE_COLS // 2
    crossing = {side: col == (middle if side < 0 else middle - 1) for side, _ in sides}
    two = grid_rows == 2

    def part_of(buf, s, h):
        return buf.at[pl.ds(pl.multiple_of(s * rows + h * half, half), half), :]

    own = [
        pltpu.make_async_copy(src, place(buf, slot(0, 0)), own_sem.at[i])
        for i, (src, buf) in enumerate(((k_ref, keys), (v_ref, vals)))
    ]
    for copy in own:
        copy.start()

    def beside(side):
        if not two:
            return over(side)
        return jnp.where(crossing[side], over(side + TILE_COLS), over(side))

    def level_there(level, side):
        return jnp.where(crossing[side], 1 - level, level) if two else level

    barrier = pltpu.get_barrier_semaphore()
    partners = [(over(offset), exists) for _, offset, exists, _ in verticals]
    partners += [(beside(side), exists) for side, exists in sides]
    for target, exists in partners:

        def greet(target=target):
            pl.semaphore_signal(barrier, inc=1, device_id={"tile": target}, device_id_type=MESH)

        when(exists, greet)
    expected = sum(1 if exists is True else jnp.where(exists, 1, 0) for _, exists in partners)
    pl.semaphore_wait(barrier, expected)

    sends = []
    pieces = [(i, h) for i in (0, 1) for h in (0, 1)]
    bufs = (keys, vals)

    def push(i, h, src, there, target, exists):
        copy = remote(
            src,
            part_of(bufs[i], there, h),
            send_sem.at[len(sends)],
            recv_sem.at[there, i * 2 + h],
            target,
        )
        when(exists, copy.start)
        sends.append((copy, exists))

    def arrived(s, exists, i, h):
        ref = part_of(bufs[i], s, h)
        when(exists, remote(ref, ref, send_sem.at[0], recv_sem.at[s, i * 2 + h], me).wait_recv)

    def own_part(i, h):
        return (k_ref, v_ref)[i].at[pl.ds(h * half, half), :]

    for i, h in pieces:
        for level, offset, exists, there in verticals:
            push(i, h, own_part(i, h), slot(there, 0), over(offset), exists)
    for i, h in pieces:
        for side, exists in sides:
            push(i, h, own_part(i, h), slot(level_there(0, side), -side), beside(side), exists)
    for s in range(3 * (1 + len(verticals))):
        level, side = s // 3, s % 3 - 1
        exists = here[level]
        for other, side_exists in sides:
            if other == side:
                exists = both(exists, side_exists)
        if exists is True:
            continue

        def clear(s=s):
            for buf in (keys, vals):
                buf[pl.ds(s * rows, rows), :] = jnp.zeros((rows, D), buf.dtype)

        pl.when(jnp.logical_not(exists))(clear)
    for i, h in pieces:
        for level, offset, exists, there in verticals:
            arrived(slot(level, 0), exists, i, h)
            for side, side_exists in sides:
                push(
                    i,
                    h,
                    part_of(bufs[i], slot(level, 0), h),
                    slot(level_there(level, side), -side),
                    beside(side),
                    both(exists, side_exists),
                )
    for copy in own:
        copy.wait()
    for i, h in pieces:
        for level, exists in sorted(here.items(), key=lambda item: item[0]):
            for side, side_exists in sides:
                arrived(slot(level, side), both(exists, side_exists), i, h)

    span = 3 * (1 + len(verticals)) * rows
    where = lax.broadcasted_iota(jnp.int32, (rows, span), 1)
    bias = jnp.zeros((rows, span), jnp.float32)
    for s in range(span // rows):
        level, side = s // 3, s % 3 - 1
        exists = here[level]
        for other, side_exists in sides:
            if other == side:
                exists = both(exists, side_exists)
        if exists is True:
            continue
        penalty = jnp.where(exists, 0.0, MASKED)
        bias = jnp.where((where >= s * rows) & (where < (s + 1) * rows), penalty, bias)
    scale = 1.0 / math.sqrt(HEAD_DIM)
    together = 8

    def heads(step, carry):
        for extra in range(together):
            at = pl.ds(pl.multiple_of((step * together + extra) * HEAD_DIM, HEAD_DIM), HEAD_DIM)
            scores = lax.dot_general(
                q_ref[:, at], keys[:, at], (((1,), (1,)), ((), ())), preferred_element_type=jnp.float32
            )
            scores = scores * scale + bias
            raised = jnp.exp(scores - jnp.max(scores, axis=-1, keepdims=True))
            probs = (raised * (1.0 / jnp.sum(raised, axis=-1, keepdims=True))).astype(jnp.bfloat16)
            att_ref[:, at] = jnp.dot(probs, vals[:, at], preferred_element_type=jnp.float32).astype(
                att_ref.dtype
            )
        return carry

    lax.fori_loop(0, D // HEAD_DIM // together, heads, 0)

    def normalise(step, carry):
        at = pl.ds(pl.multiple_of(step * 16, 16), 16)
        wide = att_ref[at, :].astype(jnp.float32)
        wide = wide - jnp.mean(wide, axis=-1, keepdims=True)
        spread = jnp.mean(wide * wide, axis=-1, keepdims=True)
        normed = wide * lax.rsqrt(spread + EPSILON)
        norm_ref[at, :] = (normed * (1.0 + mod_ref[1:2, :]) + mod_ref[0:1, :]).astype(norm_ref.dtype)
        return carry

    lax.fori_loop(0, rows // 16, normalise, 0)
    for copy, exists in sends:
        when(exists, copy.wait_send)


def attention(queries, key_rows, values, modulation):
    n = lax.axis_size("tile")
    rows = queries.shape[0]
    levels = halo_levels(n)
    slots = 3 * levels
    vmem = pl.BlockSpec(memory_space=pltpu.VMEM)
    hbm = pl.BlockSpec(memory_space=pl.ANY)
    return pl.pallas_call(
        functools.partial(attention_kernel, n, rows),
        name="halo_attention",
        out_shape=(
            jax.ShapeDtypeStruct((rows, D), jnp.bfloat16),
            jax.ShapeDtypeStruct((rows, D), jnp.bfloat16),
        ),
        in_specs=[vmem, hbm, hbm, vmem],
        out_specs=(vmem, vmem),
        scratch_shapes=[
            pltpu.VMEM((slots * rows, D), jnp.bfloat16),
            pltpu.VMEM((slots * rows, D), jnp.bfloat16),
            pltpu.SemaphoreType.DMA((4 * (2 + 3 * (levels - 1)),)),
            pltpu.SemaphoreType.DMA((slots, 4)),
            pltpu.SemaphoreType.DMA((2,)),
        ],
        compiler_params=pltpu.CompilerParams(
            collective_id=0, has_side_effects=True, vmem_limit_bytes=VMEM_LIMIT
        ),
    )(queries, key_rows, values, modulation)


def device(plane, yy, cc):
    return plane * SPLIT + yy * 2 + cc


def layer_kernel(
    n, rows, cap, chunks, backs, q_ref, k_ref, v_ref, mod_ref, routes_ref, gates_ref, first_ref, second_ref,
    out_ref, att, asked, bias, keys, vals, line, tokens, stage, chooser, spreader, tables, stats, normed,
    first, second, hidden, part, r1, r2, pair, acc_in, acc_out,
    own_sem, kv_send, kv_recv, table_send, table_recv, out_send, line_recv, beside_recv, twin_recv,
    rest_sem, back_send, s1_recv, s2_recv, pair_recv, acc_recv,
):
    planes = n // SPLIT
    width = first.shape[1]
    half = D // 2
    wide = half // chunks
    me = lax.axis_index("tile")
    p = lax.div(me, SPLIT)
    y = lax.div(lax.rem(me, SPLIT), 2)
    c = lax.rem(me, 2)
    beside = device(p, 1 - y, c)
    twin = device(p, y, 1 - c)
    low_half = p < planes // 2
    toward = jnp.where(low_half, 1, -1)
    inner = p + toward
    outer = p - toward
    at_end = jnp.logical_or(p == 0, p == planes - 1)
    middle = jnp.logical_not(at_end)
    outer_expert = jnp.where(low_half, 0, planes - 1)
    inner_device = device(inner, y, c)
    outer_device = device(jnp.where(at_end, p, outer), y, c)

    tile = lax.rem(me + TILE_COLS // 2, n)
    column = lax.rem(tile, TILE_COLS)
    partner = lax.rem(me + TILE_COLS, n)
    sides = [(-1, column > 0), (1, column < TILE_COLS - 1)]
    half_way = TILE_COLS // 2
    crossing = {-1: column == half_way, 1: column == half_way - 1}

    def part_of_plane(plane):
        return jnp.where(plane < planes // 2, half, 0)

    mine_from = part_of_plane(p)
    other_from = half - mine_from
    partner_plane = lax.rem(p + planes // 2, planes)

    def cols(j, base=0):
        return pl.ds(pl.multiple_of(base + j * wide, wide), wide)

    def halves(base):
        return pl.ds(pl.multiple_of(base, half), half)

    def lines(buf, s):
        return buf.at[pl.ds(pl.multiple_of(s * rows, rows), rows), :]

    loads = [
        pltpu.make_async_copy(q_ref.at[:, halves(mine_from)], lines(asked, 0), own_sem.at[0]),
        pltpu.make_async_copy(k_ref.at[:, halves(mine_from)], lines(keys, 1), own_sem.at[1]),
        pltpu.make_async_copy(v_ref.at[:, halves(mine_from)], lines(vals, 1), own_sem.at[2]),
        pltpu.make_async_copy(first_ref, first, own_sem.at[3]),
        pltpu.make_async_copy(second_ref, second, own_sem.at[4]),
    ]

    barrier = pltpu.get_barrier_semaphore()
    others = [lax.rem(me + step, n) for step in range(1, n)]
    for target in others:
        pl.semaphore_signal(barrier, inc=1, device_id={"tile": target}, device_id_type=MESH)

    def beside_tile(side):
        return lax.rem(me + side + jnp.where(crossing[side], TILE_COLS, 0) + n, n)

    def slot_there(level, side):
        return jnp.where(crossing[side], 1 - level, level) * 3 + 1 - side

    bufs = (keys, vals, asked)
    given = (k_ref, v_ref, q_ref)

    def place(i, s, j):
        return bufs[i].at[pl.ds(pl.multiple_of(s * rows, rows), rows), cols(j)]

    def over_vertical(i, j):
        return remote(
            given[i].at[:, cols(j, other_from)],
            place(i, 4 if i < 2 else 1, j),
            kv_send.at[0],
            kv_recv.at[4, j],
            partner,
        )

    def over_side(level, index, i, j):
        side = sides[index][0]
        there = slot_there(level, side)
        source = given[i].at[:, cols(j, mine_from)] if level == 0 else place(i, 4, j)
        return remote(
            source,
            place(i, there, j),
            kv_send.at[1 + level * 2 + index],
            kv_recv.at[there, j],
            beside_tile(side),
        )

    def landed(ref, sem):
        remote(ref, ref, own_sem.at[0], sem, me).wait_recv()

    def send_own(j):
        for i in range(3):
            over_vertical(i, j).start()

    def send_side(j):
        for i in (0, 1):
            for index, (_, exists) in enumerate(sides):
                when(exists, over_side(0, index, i, j).start)

    def bytes_of(count, at):
        return keys.at[pl.ds(0, count * rows), at]

    def send_vertical(j):
        landed(bytes_of(3, cols(j)), kv_recv.at[4, j])
        for i in (0, 1):
            for index, (_, exists) in enumerate(sides):
                when(exists, over_side(1, index, i, j).start)

    expert = lax.broadcasted_iota(jnp.int32, (8, rows), 0)
    named = [routes_ref[k : k + 1, :] == expert for k in (0, 1)]
    member = jnp.logical_or(named[0], named[1])
    upto = (
        lax.broadcasted_iota(jnp.int32, (rows, rows), 0) <= lax.broadcasted_iota(jnp.int32, (rows, rows), 1)
    ).astype(jnp.float32).astype(jnp.bfloat16)
    count = jnp.dot(
        member.astype(jnp.float32).astype(jnp.bfloat16), upto, preferred_element_type=jnp.float32
    )
    gate = sum(
        jnp.where(named[k], gates_ref[k : k + 1, :].astype(jnp.float32), 0.0) for k in (0, 1)
    )
    tables[me, 0:8, :] = jnp.where(member, count - 1.0, -1.0)
    stats[me, 8:16, :] = jnp.where(member, count - 1.0, -1.0)
    tables[me, 8:16, :] = gate / 1024.0

    span = 6 * rows
    where = lax.broadcasted_iota(jnp.int32, (8, span), 1)
    penalty = jnp.zeros((8, span), jnp.float32)
    for s in range(6):
        for side, exists in sides:
            if side != s % 3 - 1:
                continue
            here = (where >= s * rows) & (where < (s + 1) * rows)
            penalty = jnp.where(here, jnp.where(exists, 0.0, MASKED), penalty)

            def clear(s=s):
                for buf in (keys, vals):
                    buf[s * rows : (s + 1) * rows, :] = jnp.zeros((rows, half), buf.dtype)

            pl.when(jnp.logical_not(exists))(clear)
    bias[...] = penalty

    column_planes = [lax.rem(p + step, planes) for step in range(1, planes)]

    def tell_column(step):
        there = device(column_planes[step], y, c)
        return remote(tables.at[me], tables.at[me], table_send.at[0], table_recv.at[0], there)

    def tell_all():
        return [
            remote(stats.at[me], stats.at[me], table_send.at[1], table_recv.at[1], target)
            for target in others
        ]

    pl.semaphore_wait(barrier, n - 1)
    send_own(0)
    for step in range(planes - 1):
        tell_column(step).start()
    send_side(0)
    for load in loads[:3]:
        load.start()
    for j in range(1, max(AHEAD, ASIDE)):
        if j < min(AHEAD, chunks):
            send_own(j)
        if j < min(ASIDE, chunks):
            send_side(j)
    for load in loads[:3]:
        load.wait()
    for load in loads[3:]:
        load.start()

    slot_line = lax.broadcasted_iota(jnp.int32, (cap, rows), 0).astype(jnp.float32)

    def chosen(tile_there, e):
        return tables[tile_there, pl.ds(e, 1), :] == slot_line

    def picked_column(which, row):
        return jnp.sum(jnp.where(which, row, 0.0), axis=1, keepdims=True)

    def choose():
        landed(tables.at[pl.ds(0, planes - 1)], table_recv.at[0])
        chooser[...] = jnp.zeros(chooser.shape, chooser.dtype)
        for plane in range(planes):
            for place_in, e in ((0, p), (1, outer_expert)):
                found = chosen(device(plane, y, c), e).astype(jnp.float32).astype(jnp.bfloat16)
                at = place_in * 2 * cap
                spreader[plane, place_in * cap : (place_in + 1) * cap, :] = found
                chooser[plane, at : at + cap, :rows] = found
                chooser[(plane + planes // 2) % planes, at + cap : at + 2 * cap, rows:] = found

    scale = 1.0 / math.sqrt(HEAD_DIM)

    def attend(j):
        for level in (0, 1):
            for side, exists in sides:
                s = level * 3 + 1 + side
                when(exists, functools.partial(landed, bytes_of(2, cols(j)), kv_recv.at[s, j]))
        for extra in range(wide // HEAD_DIM):
            at = pl.ds(pl.multiple_of(j * wide + extra * HEAD_DIM, HEAD_DIM), HEAD_DIM)
            scores = lax.dot_general(
                asked[:, at], keys[:, at], (((1,), (1,)), ((), ())), preferred_element_type=jnp.float32
            )
            scores = scores * scale + bias[0:1, :]
            raised = jnp.exp(scores - jnp.max(scores, axis=-1, keepdims=True))
            probs = (raised * (1.0 / jnp.sum(raised, axis=-1, keepdims=True))).astype(jnp.bfloat16)
            att[:, at] = jnp.dot(probs, vals[:, at], preferred_element_type=jnp.float32).astype(att.dtype)

    def raw_copy(k, src, j):
        source = att.at[:, cols(j)] if k == 0 else line.at[src, :, cols(j)]
        return remote(source, line.at[src, :, cols(j)], out_send.at[k, 0], line_recv.at[src, j], inner_device)

    def outer_copy(k, src, j):
        there = device(src, y, c)
        return remote(
            stage.at[src, :, cols(j)],
            tokens.at[there, :, cols(j)],
            out_send.at[k, 1],
            line_recv.at[src, j],
            outer_device,
        )

    def rest_copy(src, j):
        ref = line.at[src, pl.ds(rows, rows), cols(j)]
        return remote(ref, ref, rest_sem.at[0], rest_sem.at[1], outer_device)

    def plane_copy(k, src, j, index):
        ref = tokens.at[device(src, y, c), :, cols(j)]
        recv = beside_recv.at[src, j] if index == 0 else twin_recv.at[device(src, y, c)]
        return remote(ref, ref, out_send.at[k, 2 + index], recv, (beside, twin)[index])

    def twin_copy(k, src, j):
        there = device(src, 1 - y, c)
        ref = tokens.at[there, :, cols(j)]
        return remote(ref, ref, out_send.at[k, 4], twin_recv.at[there], twin)

    far = jnp.where(at_end, p + 3 * toward, p + 2 * toward)
    second_plane = jnp.where(at_end, p + 2 * toward, outer)
    sources = [
        (p, BEHIND, True, middle),
        (inner, BEHIND + HOP, False, middle),
        (second_plane, BEHIND + HOP * jnp.where(at_end, 2, 1), middle, False),
        (far, BEHIND + HOP * jnp.where(at_end, 3, 2), False, middle),
    ]

    def relay(k, j):
        src, behind, whole, out = sources[k]
        jj = j - behind

        def go():
            there = device(src, y, c)
            if k > 0:
                pl.when(at_end)(
                    lambda: landed(tokens.at[there, :, cols(jj)], line_recv.at[src, jj])
                )
                pl.when(middle)(lambda: landed(line.at[src, :, cols(jj)], line_recv.at[src, jj]))
            if whole is not False:
                when(whole, raw_copy(k, src, jj).start)
            if k == 1:
                pl.when(middle)(rest_copy(src, jj).start)

            def pick():
                rows_here = att[:, cols(jj)] if k == 0 else line[src, :, cols(jj)]
                picked = jnp.dot(chooser[src], rows_here, preferred_element_type=jnp.float32).astype(
                    tokens.dtype
                )
                tokens[there, :, cols(jj)] = picked[: 2 * cap]
                stage[src, :, cols(jj)] = picked[2 * cap :]

            when(True if k == 0 else middle, pick)
            if out is not False:
                when(out, outer_copy(k, src, jj).start)
            for index in (0, 1):
                plane_copy(k, src, jj, index).start()

        pl.when(jnp.logical_and(jj >= 0, jj < chunks))(go)

    def pass_on(k, j):
        src, behind, _, _ = sources[k]
        jj = j - behind - HOP

        def go():
            there = device(src, 1 - y, c)
            landed(tokens.at[there, :, cols(jj)], beside_recv.at[src, jj])
            twin_copy(k, src, jj).start()

        pl.when(jnp.logical_and(jj >= 0, jj < chunks))(go)

    def move(j):
        for k in range(planes):
            relay(k, j)
        for k in range(planes):
            pass_on(k, j)

    def stream(j, carry):
        pl.when(j < chunks)(lambda: send_vertical(j))

        pl.when(j + AHEAD < chunks)(lambda: send_own(j + AHEAD))
        pl.when(j + ASIDE < chunks)(lambda: send_side(j + ASIDE))
        pl.when(j == BEHIND)(choose)
        pl.when(j >= BEHIND)(lambda: attend(j - BEHIND))
        move(j)
        return carry

    lax.fori_loop(0, chunks + BEHIND, stream, 0)

    token = lax.broadcasted_iota(jnp.int32, (16, rows), 1)
    line_of = lax.broadcasted_iota(jnp.int32, (16, rows), 0)
    row_number = lax.broadcasted_iota(jnp.int32, (8, rows), 0)
    found = jnp.zeros((8, rows), jnp.float32)
    for step in range(2 * rows // 16):
        some = att[step * 16 : (step + 1) * 16, :].astype(jnp.float32)
        mean = jnp.mean(some, axis=-1, keepdims=True)
        some = some - mean
        spread = jnp.mean(some * some, axis=-1, keepdims=True)
        which, at = divmod(step * 16, rows)
        for kind, value in enumerate((mean, spread)):
            row = jnp.sum(jnp.where(token == line_of + at, value, 0.0), axis=0, keepdims=True)
            found = found + jnp.where(row_number == 2 * which + kind, row, 0.0)
    stats[me, 0:8, :] = found
    for copy in tell_all():
        copy.start()

    def drain(j, carry):
        move(j)
        return carry

    lax.fori_loop(chunks + BEHIND, chunks + BEHIND + 4 * HOP, drain, 0)
    landed(stats.at[pl.ds(0, n - 1)], table_recv.at[1])
    for load in loads[3:]:
        load.wait()

    order = [
        jnp.where(at_end, p + 3 * toward, p + 2 * toward),
        jnp.where(at_end, p + 2 * toward, inner),
        jnp.where(at_end, inner, outer),
        p,
    ]
    for plane in range(planes):
        for yy in (0, 1):
            there = device(plane, yy, 1 - c)
            landed(tokens.at[there], twin_recv.at[there])
    pl.when(at_end)(lambda: landed(line.at[partner_plane, pl.ds(rows, rows), :], rest_sem.at[1]))
    group = SPLIT * cap
    chunk = 512
    span_back = D // backs

    def home_of(i):
        return jnp.where(i == 0, order[0], jnp.where(i == 1, order[1], jnp.where(i == 2, order[2], order[3])))

    def block(buf, index, count, j):
        return buf.at[pl.ds(pl.multiple_of(index * cap, 16), count * cap), back_cols(j)]

    def back_cols(j):
        return pl.ds(pl.multiple_of(j * span_back, span_back), span_back)

    def start_group(plane):
        def normalise(t, carry):
            yy, cc = lax.rem(t, 2), lax.div(t, 2)
            there = device(plane, yy, cc)
            across = lax.rem(there + TILE_COLS, n)
            mean_here, mean_there = stats[there, 0:1, :], stats[across, 2:3, :]
            apart = 0.5 * (mean_here - mean_there)
            spread = 0.5 * (stats[there, 1:2, :] + stats[across, 3:4, :]) + apart * apart
            which = stats[there, pl.ds(8 + p, 1), :] == slot_line
            mean = picked_column(which, 0.5 * (mean_here + mean_there))
            rate = picked_column(which, lax.rsqrt(spread + EPSILON))
            at = pl.ds(pl.multiple_of(t * cap, 16), cap)
            base = part_of_plane(plane)
            for source, lower, start in ((there, 0, base), (across, cap, half - base)):
                for step in range(half // chunk):
                    some = slice(step * chunk, (step + 1) * chunk)
                    to = pl.ds(pl.multiple_of(start + step * chunk, chunk), chunk)
                    value = (tokens[source, lower : lower + cap, some].astype(jnp.float32) - mean) * rate
                    normed[at, to] = (value * (1.0 + mod_ref[1:2, to]) + mod_ref[0:1, to]).astype(
                        normed.dtype
                    )
            return carry

        lax.fori_loop(0, SPLIT, normalise, 0)
        raw = jnp.dot(normed[...], first[...], preferred_element_type=jnp.float32)
        hidden[...] = jax.nn.gelu(raw, approximate=True).astype(hidden.dtype)

    def to_twin(plane, j):
        return remote(
            block(part, plane * SPLIT + (1 - c) * 2, 2, j),
            block(r1, plane * 2, 2, j),
            back_send.at[plane, 0],
            s1_recv.at[plane, j],
            twin,
        )

    def to_beside(plane, j):
        return remote(
            block(part, plane * SPLIT + c * 2 + 1 - y, 1, j),
            block(r2, plane, 1, j),
            back_send.at[plane, 1],
            s2_recv.at[plane, j],
            beside,
        )

    def slots_home(plane, j):
        return remote(
            pair.at[plane, pl.ds(0, cap), back_cols(j)],
            pair.at[plane, pl.ds(cap, cap), back_cols(j)],
            back_send.at[plane, 2],
            pair_recv.at[plane, j],
            inner_device,
        )

    def rows_home(plane, j):
        return remote(
            acc_out.at[plane, :, back_cols(j)],
            acc_in.at[plane, :, back_cols(j)],
            back_send.at[plane, 3],
            acc_recv.at[plane, j],
            device(jnp.where(plane == outer, outer, inner), y, c),
        )

    def produce(i, j):
        plane = home_of(i)
        pl.when(j == 0)(lambda: start_group(plane))
        raw = jnp.dot(hidden[...], second[:, back_cols(j)], preferred_element_type=jnp.float32)
        mine = pl.ds(pl.multiple_of(plane * group, 16), group)
        part[mine, back_cols(j)] = raw.astype(part.dtype)
        to_twin(plane, j).start()

    def fold_twin(i, j):
        plane = home_of(i)
        landed(block(r1, plane * 2, 2, j), s1_recv.at[plane, j])
        for yy in (1 - y, y):
            at = pl.ds(pl.multiple_of((plane * SPLIT + c * 2 + yy) * cap, 16), cap)
            there = pl.ds(pl.multiple_of((plane * 2 + yy) * cap, 16), cap)
            total = part[at, back_cols(j)].astype(jnp.float32) + r1[there, back_cols(j)].astype(jnp.float32)
            part[at, back_cols(j)] = total.astype(part.dtype)
            if yy is not y:
                to_beside(plane, j).start()

    def fold_beside(i, j):
        plane = home_of(i)
        there = device(plane, y, c)
        landed(block(r2, plane, 1, j), s2_recv.at[plane, j])
        weight = picked_column(chosen(there, p), tables[there, pl.ds(8 + p, 1), :])
        ours = pl.ds(pl.multiple_of((plane * SPLIT + c * 2 + y) * cap, 16), cap)
        theirs = pl.ds(pl.multiple_of(plane * cap, 16), cap)
        total = part[ours, back_cols(j)].astype(jnp.float32) + r2[theirs, back_cols(j)].astype(jnp.float32)
        pair[plane, :cap, back_cols(j)] = (total * weight).astype(pair.dtype)
        pl.when(jnp.logical_and(at_end, plane != p))(slots_home(plane, j).start)

    def spread_out(plane, both, at):
        amount = 2 * cap if both else cap
        return lax.dot_general(
            spreader[plane, :amount, :],
            pair[plane, :amount, at],
            (((0,), (0,)), ((), ())),
            preferred_element_type=jnp.float32,
        )

    def fold_home(i, j):
        plane = home_of(i)
        at = back_cols(j)

        def fold(both, extra, last):
            if both:
                landed(pair.at[plane, pl.ds(cap, cap), at], pair_recv.at[plane, j])
            if extra:
                landed(acc_in.at[plane, :, at], acc_recv.at[plane, j])
            total = spread_out(plane, both, at)
            if extra:
                total = total + acc_in[plane, :, at].astype(jnp.float32)
            if last:
                out_ref[:, at] = (mod_ref[2:3, at] * total + out_ref[:, at].astype(jnp.float32)).astype(
                    out_ref.dtype
                )
            else:
                acc_out[plane, :, at] = total.astype(acc_out.dtype)
                rows_home(plane, j).start()

        pl.when(jnp.logical_and(at_end, i == 3))(lambda: fold(False, True, True))
        pl.when(jnp.logical_and(middle, i == 3))(lambda: fold(True, True, True))
        pl.when(jnp.logical_and(middle, i == 2))(lambda: fold(False, True, False))
        pl.when(jnp.logical_and(middle, i < 2))(lambda: fold(True, False, False))

    out_ref[:, halves(mine_from)] = att[:rows, :]
    out_ref[:, halves(other_from)] = line[partner_plane, rows:, :]
    units = planes * backs

    def give_back(u, carry):
        for behind, act in ((0, produce), (BACK_LAGS[0], fold_twin), (BACK_LAGS[1], fold_beside), (BACK_LAGS[2], fold_home)):
            at = u - behind
            i, j = lax.div(at, backs), lax.rem(at, backs)
            pl.when(jnp.logical_and(at >= 0, at < units))(functools.partial(act, i, j))
        return carry

    lax.fori_loop(0, units + BACK_LAGS[2], give_back, 0)

    def gone(ref, sem):
        remote(ref, ref, sem, own_sem.at[0], twin).wait_send()

    every = pl.ds(0, half)
    gone(bytes_of(3, every), kv_send.at[0])
    for level in (0, 1):
        for index, (_, exists) in enumerate(sides):
            when(exists, functools.partial(gone, bytes_of(2, every), kv_send.at[1 + level * 2 + index]))
    for k, (_, _, whole, out) in enumerate(sources):
        if whole is not False:
            when(whole, functools.partial(gone, line.at[0], out_send.at[k, 0]))
        if out is not False:
            when(out, functools.partial(gone, stage.at[0], out_send.at[k, 1]))
        for index in range(3):
            gone(tokens.at[0], out_send.at[k, 2 + index])
    pl.when(middle)(lambda: gone(line.at[0, pl.ds(0, rows), :], rest_sem.at[0]))
    gone(tables.at[pl.ds(0, planes - 1)], table_send.at[0])
    gone(stats.at[pl.ds(0, n - 1)], table_send.at[1])
    for plane in range(planes):
        gone(r1.at[pl.ds(0, 2 * cap), :], back_send.at[plane, 0])
        gone(r1.at[pl.ds(0, cap), :], back_send.at[plane, 1])
        away = p != plane
        pl.when(jnp.logical_and(at_end, away))(
            functools.partial(gone, r1.at[pl.ds(0, cap), :], back_send.at[plane, 2])
        )
        pl.when(jnp.logical_and(middle, away))(functools.partial(gone, acc_in.at[0], back_send.at[plane, 3]))


def kernel_bytes(n, rows, cap, width):
    planes = n // SPLIT
    lines = 2 * 6 * rows + 2 * n * cap + planes * (6 * cap + 3 * rows) + SPLIT * cap + 3 * rows
    return 2 * (lines * D + 2 * width * D)


def layer(queries, key_rows, values, modulation, expert_in, expert_out, routes, gate_fixed):
    n = lax.axis_size("tile")
    rows = queries.shape[0]
    width = expert_in.shape[1]
    planes = n // SPLIT
    cap = 3 * rows // planes
    chunks, backs = CHUNKS, BACK_CHUNKS
    vmem = pl.BlockSpec(memory_space=pltpu.VMEM)
    hbm = pl.BlockSpec(memory_space=pl.ANY)
    dma = pltpu.SemaphoreType.DMA
    bf = jnp.bfloat16
    return pl.pallas_call(
        functools.partial(layer_kernel, n, rows, cap, CHUNKS, BACK_CHUNKS),
        name="whole_layer",
        out_shape=pltpu.VMEM((rows, D), bf),
        in_specs=[hbm, hbm, hbm, vmem, vmem, vmem, hbm, hbm],
        out_specs=vmem,
        scratch_shapes=[
            pltpu.VMEM((2 * rows, D // 2), bf),
            pltpu.VMEM((2 * rows, D // 2), bf),
            pltpu.VMEM((8, 6 * rows), jnp.float32),
            pltpu.VMEM((6 * rows, D // 2), bf),
            pltpu.VMEM((6 * rows, D // 2), bf),
            pltpu.VMEM((planes, 2 * rows, D // 2), bf),
            pltpu.VMEM((n, 2 * cap, D // 2), bf),
            pltpu.VMEM((planes, 2 * cap, D // 2), bf),
            pltpu.VMEM((planes, 4 * cap, 2 * rows), bf),
            pltpu.VMEM((planes, 2 * cap, rows), bf),
            pltpu.VMEM((n, 16, rows), jnp.float32),
            pltpu.VMEM((n, 16, rows), jnp.float32),
            pltpu.VMEM((SPLIT * cap, D), bf),
            pltpu.VMEM((D, width), bf),
            pltpu.VMEM((width, D), bf),
            pltpu.VMEM((SPLIT * cap, width), bf),
            pltpu.VMEM((n * cap, D), bf),
            pltpu.VMEM((planes * 2 * cap, D), bf),
            pltpu.VMEM((planes * cap, D), bf),
            pltpu.VMEM((planes, 2 * cap, D), bf),
            pltpu.VMEM((planes, rows, D), bf),
            pltpu.VMEM((planes, rows, D), bf),
            dma((5,)),
            dma((5,)),
            dma((6, chunks)),
            dma((2,)),
            dma((2,)),
            dma((planes, 5)),
            dma((planes, chunks)),
            dma((planes, chunks)),
            dma((n,)),
            dma((2,)),
            dma((planes, 4)),
            dma((planes, backs)),
            dma((planes, backs)),
            dma((planes, backs)),
            dma((planes, backs)),
        ],
        compiler_params=pltpu.CompilerParams(
            collective_id=1, has_side_effects=True, vmem_limit_bytes=VMEM_LIMIT
        ),
    )(queries, key_rows, values, modulation, routes.T, gate_fixed.T, expert_in, expert_out)


def slot_table(flat, experts_count):
    onehot = (flat[:, None] == jnp.arange(experts_count, dtype=jnp.int32)[None, :]).astype(
        jnp.int32
    )
    before = jnp.cumsum(onehot, axis=0) - onehot
    return jnp.sum(before * onehot, axis=1)


def expert_apply(rows, first_weight, second_weight):
    hidden = jax.nn.gelu(
        jnp.dot(rows, first_weight, preferred_element_type=jnp.float32), approximate=True
    ).astype(jnp.bfloat16)
    return jnp.dot(hidden, second_weight, preferred_element_type=jnp.float32).astype(jnp.bfloat16)


def experts_sparse(normed, attended, modulation, expert_in, expert_out, routes, gate_fixed):
    devices = lax.axis_size("tile")
    rows_dev = normed.shape[0]
    experts_count = devices // SPLIT
    capacity = 3 * rows_dev // experts_count
    flat = routes.reshape(-1)
    slots = slot_table(flat, experts_count)
    target = flat * capacity + slots
    chooser = (
        target[None, :] == jnp.arange(experts_count * capacity, dtype=jnp.int32)[:, None]
    ).astype(jnp.bfloat16)
    chooser = chooser.reshape(experts_count * capacity, rows_dev, 2).sum(axis=2)
    buffer = jnp.dot(chooser, normed, preferred_element_type=jnp.float32).astype(jnp.bfloat16)
    copies = jnp.broadcast_to(
        buffer.reshape(experts_count, 1, capacity, D), (experts_count, SPLIT, capacity, D)
    ).reshape(devices, capacity, D)
    received = lax.all_to_all(copies, "tile", split_axis=0, concat_axis=0, tiled=True)
    sources = received.shape[0]
    count = received.shape[1]
    partial_value = expert_apply(received.reshape(sources * count, D), expert_in, expert_out)
    returned = lax.all_to_all(
        partial_value.reshape(sources, count, D), "tile", split_axis=0, concat_axis=0, tiled=True
    )
    summed = jnp.sum(
        returned.reshape(experts_count, SPLIT, capacity, D).astype(jnp.float32), axis=1
    )
    expert_rows = summed.astype(jnp.bfloat16).reshape(experts_count * capacity, D)
    picked = jnp.take(expert_rows, target, axis=0).reshape(rows_dev, 2, D)
    gate_scale = gate_fixed.astype(jnp.float32) / 1024.0
    mixture = jnp.sum(picked.astype(jnp.float32) * gate_scale[:, :, None], axis=1)
    return (attended.astype(jnp.float32) + modulation[2] * mixture).astype(jnp.bfloat16)


def shards(queries, key_rows, values, modulation, expert_in, expert_out, routes, gate_fixed):
    n = lax.axis_size("tile")
    cap = 3 * queries.shape[0] // (n // SPLIT)
    if n == 2 * TILE_COLS and cap % 16 == 0 and kernel_bytes(n, queries.shape[0], cap, expert_in.shape[1]) < VMEM_LIMIT * 7 // 8:
        return layer(queries, key_rows, values, modulation, expert_in, expert_out, routes, gate_fixed)
    attended, normed = attention(queries, key_rows, values, modulation)
    return experts_sparse(normed, attended, modulation, expert_in, expert_out, routes, gate_fixed)


def solution(mesh):
    placed = (
        P(("groups", "tile"), None),
        P(("groups", "tile"), None),
        P(("groups", "tile"), None),
        P("groups", None),
        P(None, "tile"),
        P("tile", None),
        P(("groups", "tile"), None),
        P(("groups", "tile"), None),
    )
    return jax.shard_map(
        shards, mesh=mesh, in_specs=placed, out_specs=P(("groups", "tile"), None), check_vma=False
    )
```

```python
import functools
import math

import jax
import jax.numpy as jnp
from jax import lax
from jax.experimental import pallas as pl
from jax.experimental.pallas import tpu as pltpu
from jax.sharding import PartitionSpec as P

HEAD_DIM = 128
D = 4096
SPLIT = 4
TILE_COLS = 8

EPSILON = 1e-06
MASKED = -1e30
MESH = pl.DeviceIdType.MESH
VMEM_LIMIT = 60 * 1024 * 1024
CHUNKS = 8
AHEAD = 2
ASIDE = 2
BEHIND = 2
HOP = 2
DRAIN = (2, 7)
EARLY = 2
BACK_CHUNKS = 4
BACK_LAGS = (1, 4, 6)


def when(cond, body):
    if cond is True:
        body()
    else:
        pl.when(cond)(body)


def both(a, b):
    if a is True:
        return b
    if b is True:
        return a
    return jnp.logical_and(a, b)


def remote(src, dst, send_sem, recv_sem, target):
    return pltpu.make_async_remote_copy(
        src_ref=src,
        dst_ref=dst,
        send_sem=send_sem,
        recv_sem=recv_sem,
        device_id={"tile": target},
        device_id_type=MESH,
    )


def halo_levels(n):
    grid_rows = n // TILE_COLS
    if grid_rows < 2:
        return 1
    return 2 if grid_rows == 2 else 3


def attention_kernel(
    n, rows, q_ref, k_ref, v_ref, mod_ref, att_ref, norm_ref, keys, vals, send_sem, recv_sem, own_sem,
):
    me = lax.axis_index("tile")
    grid_rows = n // TILE_COLS
    tile = lax.rem(me + TILE_COLS // 2, n)
    row = lax.div(tile, TILE_COLS)
    col = lax.rem(tile, TILE_COLS)
    if grid_rows < 2:
        verticals = []
    elif grid_rows == 2:
        verticals = [(1, TILE_COLS, True, 1)]
    else:
        verticals = [(1, n - TILE_COLS, row > 0, 2), (2, TILE_COLS, row < grid_rows - 1, 1)]
    sides = [(-1, col > 0), (1, col < TILE_COLS - 1)]
    here = {level: exists for level, _, exists, _ in verticals}
    here[0] = True

    def slot(level, side):
        return level * 3 + 1 + side

    def place(buf, s):
        return buf.at[pl.ds(s * rows, rows), :]

    def over(offset):
        return lax.rem(me + offset + n, n)

    half = rows // 2
    middle = TILE_COLS // 2
    crossing = {side: col == (middle if side < 0 else middle - 1) for side, _ in sides}
    two = grid_rows == 2

    def part_of(buf, s, h):
        return buf.at[pl.ds(pl.multiple_of(s * rows + h * half, half), half), :]

    own = [
        pltpu.make_async_copy(src, place(buf, slot(0, 0)), own_sem.at[i])
        for i, (src, buf) in enumerate(((k_ref, keys), (v_ref, vals)))
    ]
    for copy in own:
        copy.start()

    def beside(side):
        if not two:
            return over(side)
        return jnp.where(crossing[side], over(side + TILE_COLS), over(side))

    def level_there(level, side):
        return jnp.where(crossing[side], 1 - level, level) if two else level

    barrier = pltpu.get_barrier_semaphore()
    partners = [(over(offset), exists) for _, offset, exists, _ in verticals]
    partners += [(beside(side), exists) for side, exists in sides]
    for target, exists in partners:

        def greet(target=target):
            pl.semaphore_signal(barrier, inc=1, device_id={"tile": target}, device_id_type=MESH)

        when(exists, greet)
    expected = sum(1 if exists is True else jnp.where(exists, 1, 0) for _, exists in partners)
    pl.semaphore_wait(barrier, expected)

    sends = []
    pieces = [(i, h) for i in (0, 1) for h in (0, 1)]
    bufs = (keys, vals)

    def push(i, h, src, there, target, exists):
        copy = remote(
            src,
            part_of(bufs[i], there, h),
            send_sem.at[len(sends)],
            recv_sem.at[there, i * 2 + h],
            target,
        )
        when(exists, copy.start)
        sends.append((copy, exists))

    def arrived(s, exists, i, h):
        ref = part_of(bufs[i], s, h)
        when(exists, remote(ref, ref, send_sem.at[0], recv_sem.at[s, i * 2 + h], me).wait_recv)

    def own_part(i, h):
        return (k_ref, v_ref)[i].at[pl.ds(h * half, half), :]

    for i, h in pieces:
        for level, offset, exists, there in verticals:
            push(i, h, own_part(i, h), slot(there, 0), over(offset), exists)
    for i, h in pieces:
        for side, exists in sides:
            push(i, h, own_part(i, h), slot(level_there(0, side), -side), beside(side), exists)
    for s in range(3 * (1 + len(verticals))):
        level, side = s // 3, s % 3 - 1
        exists = here[level]
        for other, side_exists in sides:
            if other == side:
                exists = both(exists, side_exists)
        if exists is True:
            continue

        def clear(s=s):
            for buf in (keys, vals):
                buf[pl.ds(s * rows, rows), :] = jnp.zeros((rows, D), buf.dtype)

        pl.when(jnp.logical_not(exists))(clear)
    for i, h in pieces:
        for level, offset, exists, there in verticals:
            arrived(slot(level, 0), exists, i, h)
            for side, side_exists in sides:
                push(
                    i,
                    h,
                    part_of(bufs[i], slot(level, 0), h),
                    slot(level_there(level, side), -side),
                    beside(side),
                    both(exists, side_exists),
                )
    for copy in own:
        copy.wait()
    for i, h in pieces:
        for level, exists in sorted(here.items(), key=lambda item: item[0]):
            for side, side_exists in sides:
                arrived(slot(level, side), both(exists, side_exists), i, h)

    span = 3 * (1 + len(verticals)) * rows
    where = lax.broadcasted_iota(jnp.int32, (rows, span), 1)
    bias = jnp.zeros((rows, span), jnp.float32)
    for s in range(span // rows):
        level, side = s // 3, s % 3 - 1
        exists = here[level]
        for other, side_exists in sides:
            if other == side:
                exists = both(exists, side_exists)
        if exists is True:
            continue
        penalty = jnp.where(exists, 0.0, MASKED)
        bias = jnp.where((where >= s * rows) & (where < (s + 1) * rows), penalty, bias)
    scale = 1.0 / math.sqrt(HEAD_DIM)
    together = 8

    def heads(step, carry):
        for extra in range(together):
            at = pl.ds(pl.multiple_of((step * together + extra) * HEAD_DIM, HEAD_DIM), HEAD_DIM)
            scores = lax.dot_general(
                q_ref[:, at], keys[:, at], (((1,), (1,)), ((), ())), preferred_element_type=jnp.float32
            )
            scores = scores * scale + bias
            raised = jnp.exp(scores - jnp.max(scores, axis=-1, keepdims=True))
            probs = (raised * (1.0 / jnp.sum(raised, axis=-1, keepdims=True))).astype(jnp.bfloat16)
            att_ref[:, at] = jnp.dot(probs, vals[:, at], preferred_element_type=jnp.float32).astype(
                att_ref.dtype
            )
        return carry

    lax.fori_loop(0, D // HEAD_DIM // together, heads, 0)

    def normalise(step, carry):
        at = pl.ds(pl.multiple_of(step * 16, 16), 16)
        wide = att_ref[at, :].astype(jnp.float32)
        wide = wide - jnp.mean(wide, axis=-1, keepdims=True)
        spread = jnp.mean(wide * wide, axis=-1, keepdims=True)
        normed = wide * lax.rsqrt(spread + EPSILON)
        norm_ref[at, :] = (normed * (1.0 + mod_ref[1:2, :]) + mod_ref[0:1, :]).astype(norm_ref.dtype)
        return carry

    lax.fori_loop(0, rows // 16, normalise, 0)
    for copy, exists in sends:
        when(exists, copy.wait_send)


def attention(queries, key_rows, values, modulation):
    n = lax.axis_size("tile")
    rows = queries.shape[0]
    levels = halo_levels(n)
    slots = 3 * levels
    vmem = pl.BlockSpec(memory_space=pltpu.VMEM)
    hbm = pl.BlockSpec(memory_space=pl.ANY)
    return pl.pallas_call(
        functools.partial(attention_kernel, n, rows),
        name="halo_attention",
        out_shape=(
            jax.ShapeDtypeStruct((rows, D), jnp.bfloat16),
            jax.ShapeDtypeStruct((rows, D), jnp.bfloat16),
        ),
        in_specs=[vmem, hbm, hbm, vmem],
        out_specs=(vmem, vmem),
        scratch_shapes=[
            pltpu.VMEM((slots * rows, D), jnp.bfloat16),
            pltpu.VMEM((slots * rows, D), jnp.bfloat16),
            pltpu.SemaphoreType.DMA((4 * (2 + 3 * (levels - 1)),)),
            pltpu.SemaphoreType.DMA((slots, 4)),
            pltpu.SemaphoreType.DMA((2,)),
        ],
        compiler_params=pltpu.CompilerParams(
            collective_id=0, has_side_effects=True, vmem_limit_bytes=VMEM_LIMIT
        ),
    )(queries, key_rows, values, modulation)


def device(plane, yy, cc):
    return plane * SPLIT + yy * 2 + cc


def layer_kernel(
    n, rows, cap, chunks, backs, q_ref, k_ref, v_ref, mod_ref, routes_ref, gates_ref, first_ref, second_ref,
    out_ref, att, asked, bias, keys, vals, line, tokens, stage, chooser, spreader, tables, stats, normed,
    first, second, hidden, part, r1, r2, pair, acc_in, acc_out,
    own_sem, kv_send, kv_recv, table_send, table_recv, out_send, line_recv, beside_recv, twin_recv,
    rest_sem, back_send, s1_recv, s2_recv, pair_recv, acc_recv,
):
    planes = n // SPLIT
    width = first.shape[1]
    half = D // 2
    wide = half // chunks
    me = lax.axis_index("tile")
    p = lax.div(me, SPLIT)
    y = lax.div(lax.rem(me, SPLIT), 2)
    c = lax.rem(me, 2)
    beside = device(p, 1 - y, c)
    twin = device(p, y, 1 - c)
    low_half = p < planes // 2
    toward = jnp.where(low_half, 1, -1)
    inner = p + toward
    outer = p - toward
    at_end = jnp.logical_or(p == 0, p == planes - 1)
    middle = jnp.logical_not(at_end)
    outer_expert = jnp.where(low_half, 0, planes - 1)
    inner_device = device(inner, y, c)
    outer_device = device(jnp.where(at_end, p, outer), y, c)

    tile = lax.rem(me + TILE_COLS // 2, n)
    column = lax.rem(tile, TILE_COLS)
    partner = lax.rem(me + TILE_COLS, n)
    sides = [(-1, column > 0), (1, column < TILE_COLS - 1)]
    half_way = TILE_COLS // 2
    crossing = {-1: column == half_way, 1: column == half_way - 1}

    def part_of_plane(plane):
        return jnp.where(plane < planes // 2, half, 0)

    mine_from = part_of_plane(p)
    other_from = half - mine_from
    partner_plane = lax.rem(p + planes // 2, planes)

    def cols(j, base=0):
        return pl.ds(pl.multiple_of(base + j * wide, wide), wide)

    def halves(base):
        return pl.ds(pl.multiple_of(base, half), half)

    def lines(buf, s):
        return buf.at[pl.ds(pl.multiple_of(s * rows, rows), rows), :]

    loads = [
        pltpu.make_async_copy(q_ref.at[:, halves(mine_from)], lines(asked, 0), own_sem.at[0]),
        pltpu.make_async_copy(k_ref.at[:, halves(mine_from)], lines(keys, 1), own_sem.at[1]),
        pltpu.make_async_copy(v_ref.at[:, halves(mine_from)], lines(vals, 1), own_sem.at[2]),
        pltpu.make_async_copy(first_ref, first, own_sem.at[3]),
        pltpu.make_async_copy(second_ref, second, own_sem.at[4]),
    ]

    barrier = pltpu.get_barrier_semaphore()
    others = [lax.rem(me + step, n) for step in range(1, n)]
    for target in others:
        pl.semaphore_signal(barrier, inc=1, device_id={"tile": target}, device_id_type=MESH)

    def beside_tile(side):
        return lax.rem(me + side + jnp.where(crossing[side], TILE_COLS, 0) + n, n)

    def slot_there(level, side):
        return jnp.where(crossing[side], 1 - level, level) * 3 + 1 - side

    bufs = (keys, vals, asked)
    given = (k_ref, v_ref, q_ref)

    def place(i, s, j):
        return bufs[i].at[pl.ds(pl.multiple_of(s * rows, rows), rows), cols(j)]

    def over_vertical(i, j):
        return remote(
            given[i].at[:, cols(j, other_from)],
            place(i, 4 if i < 2 else 1, j),
            kv_send.at[0],
            kv_recv.at[4, j],
            partner,
        )

    def over_side(level, index, i, j):
        side = sides[index][0]
        there = slot_there(level, side)
        source = given[i].at[:, cols(j, mine_from)] if level == 0 else place(i, 4, j)
        return remote(
            source,
            place(i, there, j),
            kv_send.at[1 + level * 2 + index],
            kv_recv.at[there, j],
            beside_tile(side),
        )

    def landed(ref, sem):
        remote(ref, ref, own_sem.at[0], sem, me).wait_recv()

    def send_own(j):
        for i in range(3):
            over_vertical(i, j).start()

    def send_side(j):
        for i in (0, 1):
            for index, (_, exists) in enumerate(sides):
                when(exists, over_side(0, index, i, j).start)

    def bytes_of(count, at):
        return keys.at[pl.ds(0, count * rows), at]

    def send_vertical(j):
        landed(bytes_of(3, cols(j)), kv_recv.at[4, j])
        for i in (0, 1):
            for index, (_, exists) in enumerate(sides):
                when(exists, over_side(1, index, i, j).start)

    pl.semaphore_wait(barrier, n - 1)
    send_own(0)
    send_side(0)
    for load in loads[:3]:
        load.start()

    expert = lax.broadcasted_iota(jnp.int32, (8, rows), 0)
    named = [routes_ref[k : k + 1, :] == expert for k in (0, 1)]
    member = jnp.logical_or(named[0], named[1])
    upto = (
        lax.broadcasted_iota(jnp.int32, (rows, rows), 0) <= lax.broadcasted_iota(jnp.int32, (rows, rows), 1)
    ).astype(jnp.float32).astype(jnp.bfloat16)
    count = jnp.dot(
        member.astype(jnp.float32).astype(jnp.bfloat16), upto, preferred_element_type=jnp.float32
    )
    gate = sum(
        jnp.where(named[k], gates_ref[k : k + 1, :].astype(jnp.float32), 0.0) for k in (0, 1)
    )
    tables[me, 0:8, :] = jnp.where(member, count - 1.0, -1.0)
    stats[me, 8:16, :] = jnp.where(member, count - 1.0, -1.0)
    tables[me, 8:16, :] = gate / 1024.0

    column_planes = [lax.rem(p + step, planes) for step in range(1, planes)]

    def tell_column(step):
        there = device(column_planes[step], y, c)
        return remote(tables.at[me], tables.at[me], table_send.at[0], table_recv.at[0], there)

    for step in range(planes - 1):
        tell_column(step).start()
    for j in range(1, max(AHEAD, ASIDE)):
        if j < min(AHEAD, chunks):
            send_own(j)
        if j < min(ASIDE, chunks):
            send_side(j)

    span = 6 * rows
    where = lax.broadcasted_iota(jnp.int32, (8, span), 1)
    penalty = jnp.zeros((8, span), jnp.float32)
    for s in range(6):
        for side, exists in sides:
            if side != s % 3 - 1:
                continue
            here = (where >= s * rows) & (where < (s + 1) * rows)
            penalty = jnp.where(here, jnp.where(exists, 0.0, MASKED), penalty)

            def clear(s=s):
                for buf in (keys, vals):
                    buf[s * rows : (s + 1) * rows, :] = jnp.zeros((rows, half), buf.dtype)

            pl.when(jnp.logical_not(exists))(clear)
    bias[...] = penalty

    def tell_all():
        return [
            remote(stats.at[me], stats.at[me], table_send.at[1], table_recv.at[1], target)
            for target in others
        ]

    for load in loads[:3]:
        load.wait()
    for load in loads[3:]:
        load.start()

    slot_line = lax.broadcasted_iota(jnp.int32, (cap, rows), 0).astype(jnp.float32)

    def chosen(tile_there, e):
        return tables[tile_there, pl.ds(e, 1), :] == slot_line

    def picked_column(which, row):
        return jnp.sum(jnp.where(which, row, 0.0), axis=1, keepdims=True)

    def choose():
        landed(tables.at[pl.ds(0, planes - 1)], table_recv.at[0])
        chooser[...] = jnp.zeros(chooser.shape, chooser.dtype)
        for plane in range(planes):
            for place_in, e in ((0, p), (1, outer_expert)):
                found = chosen(device(plane, y, c), e).astype(jnp.float32).astype(jnp.bfloat16)
                at = place_in * 2 * cap
                spreader[plane, place_in * cap : (place_in + 1) * cap, :] = found
                chooser[plane, at : at + cap, :rows] = found
                chooser[(plane + planes // 2) % planes, at + cap : at + 2 * cap, rows:] = found

    scale = 1.0 / math.sqrt(HEAD_DIM)

    def attend(j):
        for level in (0, 1):
            for side, exists in sides:
                s = level * 3 + 1 + side
                when(exists, functools.partial(landed, bytes_of(2, cols(j)), kv_recv.at[s, j]))
        for extra in range(wide // HEAD_DIM):
            at = pl.ds(pl.multiple_of(j * wide + extra * HEAD_DIM, HEAD_DIM), HEAD_DIM)
            scores = lax.dot_general(
                asked[:, at], keys[:, at], (((1,), (1,)), ((), ())), preferred_element_type=jnp.float32
            )
            scores = scores * scale + bias[0:1, :]
            raised = jnp.exp(scores - jnp.max(scores, axis=-1, keepdims=True))
            probs = (raised * (1.0 / jnp.sum(raised, axis=-1, keepdims=True))).astype(jnp.bfloat16)
            att[:, at] = jnp.dot(probs, vals[:, at], preferred_element_type=jnp.float32).astype(att.dtype)

    def raw_copy(k, src, j):
        source = att.at[:, cols(j)] if k == 0 else line.at[src, :, cols(j)]
        return remote(source, line.at[src, :, cols(j)], out_send.at[k, 0], line_recv.at[src, j], inner_device)

    def outer_copy(k, src, j):
        there = device(src, y, c)
        return remote(
            stage.at[src, :, cols(j)],
            tokens.at[there, :, cols(j)],
            out_send.at[k, 1],
            line_recv.at[src, j],
            outer_device,
        )

    def rest_copy(src, j):
        ref = line.at[src, pl.ds(rows, rows), cols(j)]
        return remote(ref, ref, rest_sem.at[0], rest_sem.at[1], outer_device)

    def plane_copy(k, src, j, index):
        ref = tokens.at[device(src, y, c), :, cols(j)]
        recv = beside_recv.at[src, j] if index == 0 else twin_recv.at[device(src, y, c)]
        return remote(ref, ref, out_send.at[k, 2 + index], recv, (beside, twin)[index])

    def twin_copy(k, src, j):
        there = device(src, 1 - y, c)
        ref = tokens.at[there, :, cols(j)]
        return remote(ref, ref, out_send.at[k, 4], twin_recv.at[there], twin)

    far = jnp.where(at_end, p + 3 * toward, p + 2 * toward)
    second_plane = jnp.where(at_end, p + 2 * toward, outer)
    sources = [
        (p, BEHIND, True, middle),
        (inner, BEHIND + HOP, False, middle),
        (second_plane, BEHIND + HOP * jnp.where(at_end, 2, 1), middle, False),
        (far, BEHIND + HOP * jnp.where(at_end, 3, 2), False, middle),
    ]

    def relay(k, j):
        src, behind, whole, out = sources[k]
        jj = j - behind

        def go():
            there = device(src, y, c)
            if k > 0:
                pl.when(at_end)(
                    lambda: landed(tokens.at[there, :, cols(jj)], line_recv.at[src, jj])
                )
                pl.when(middle)(lambda: landed(line.at[src, :, cols(jj)], line_recv.at[src, jj]))
            if whole is not False:
                when(whole, raw_copy(k, src, jj).start)
            if k == 1:
                pl.when(middle)(rest_copy(src, jj).start)

            def pick():
                rows_here = att[:, cols(jj)] if k == 0 else line[src, :, cols(jj)]
                picked = jnp.dot(chooser[src], rows_here, preferred_element_type=jnp.float32).astype(
                    tokens.dtype
                )
                tokens[there, :, cols(jj)] = picked[: 2 * cap]
                stage[src, :, cols(jj)] = picked[2 * cap :]

            when(True if k == 0 else middle, pick)
            if out is not False:
                when(out, outer_copy(k, src, jj).start)
            for index in (0, 1):
                plane_copy(k, src, jj, index).start()

        pl.when(jnp.logical_and(jj >= 0, jj < chunks))(go)

    def pass_on(k, j):
        src, behind, _, _ = sources[k]
        jj = j - behind - HOP

        def go():
            there = device(src, 1 - y, c)
            landed(tokens.at[there, :, cols(jj)], beside_recv.at[src, jj])
            twin_copy(k, src, jj).start()

        pl.when(jnp.logical_and(jj >= 0, jj < chunks))(go)

    def move(j):
        for k in range(planes):
            relay(k, j)
        for k in range(planes):
            pass_on(k, j)

    def stream(j, carry):
        pl.when(j < chunks)(lambda: send_vertical(j))

        pl.when(j + AHEAD < chunks)(lambda: send_own(j + AHEAD))
        pl.when(j + ASIDE < chunks)(lambda: send_side(j + ASIDE))
        pl.when(j == BEHIND)(choose)
        pl.when(j >= BEHIND)(lambda: attend(j - BEHIND))
        move(j)
        return carry

    lax.fori_loop(0, chunks + BEHIND, stream, 0)

    def drain(j, carry):
        move(j)
        return carry

    lax.fori_loop(chunks + BEHIND, chunks + BEHIND + DRAIN[0], drain, 0)

    token = lax.broadcasted_iota(jnp.int32, (16, rows), 1)
    line_of = lax.broadcasted_iota(jnp.int32, (16, rows), 0)
    row_number = lax.broadcasted_iota(jnp.int32, (8, rows), 0)
    found = jnp.zeros((8, rows), jnp.float32)
    for step in range(2 * rows // 16):
        some = att[step * 16 : (step + 1) * 16, :].astype(jnp.float32)
        mean = jnp.mean(some, axis=-1, keepdims=True)
        some = some - mean
        spread = jnp.mean(some * some, axis=-1, keepdims=True)
        which, at = divmod(step * 16, rows)
        for kind, value in enumerate((mean, spread)):
            row = jnp.sum(jnp.where(token == line_of + at, value, 0.0), axis=0, keepdims=True)
            found = found + jnp.where(row_number == 2 * which + kind, row, 0.0)
    stats[me, 0:8, :] = found
    for copy in tell_all():
        copy.start()

    lax.fori_loop(chunks + BEHIND + DRAIN[0], chunks + BEHIND + DRAIN[1], drain, 0)
    landed(stats.at[pl.ds(0, n - 1)], table_recv.at[1])
    for load in loads[3:]:
        load.wait()

    order = [
        jnp.where(at_end, p + 2 * toward, inner),
        jnp.where(at_end, p + 3 * toward, p + 2 * toward),
        jnp.where(at_end, inner, outer),
        p,
    ]
    def arrive(plane):
        for source in (plane, lax.rem(plane + planes // 2, planes)):
            for yy in (0, 1):
                there = device(source, yy, 1 - c)
                landed(tokens.at[there], twin_recv.at[there])

    group = SPLIT * cap
    chunk = 512
    span_back = D // backs

    def home_of(i):
        return jnp.where(i == 0, order[0], jnp.where(i == 1, order[1], jnp.where(i == 2, order[2], order[3])))

    def block(buf, index, count, j):
        return buf.at[pl.ds(pl.multiple_of(index * cap, 16), count * cap), back_cols(j)]

    def back_cols(j):
        return pl.ds(pl.multiple_of(j * span_back, span_back), span_back)

    def start_group(plane):
        def normalise(t, carry):
            yy, cc = lax.rem(t, 2), lax.div(t, 2)
            there = device(plane, yy, cc)
            across = lax.rem(there + TILE_COLS, n)
            mean_here, mean_there = stats[there, 0:1, :], stats[across, 2:3, :]
            apart = 0.5 * (mean_here - mean_there)
            spread = 0.5 * (stats[there, 1:2, :] + stats[across, 3:4, :]) + apart * apart
            which = stats[there, pl.ds(8 + p, 1), :] == slot_line
            mean = picked_column(which, 0.5 * (mean_here + mean_there))
            rate = picked_column(which, lax.rsqrt(spread + EPSILON))
            at = pl.ds(pl.multiple_of(t * cap, 16), cap)
            base = part_of_plane(plane)
            for source, lower, start in ((there, 0, base), (across, cap, half - base)):
                for step in range(half // chunk):
                    some = slice(step * chunk, (step + 1) * chunk)
                    to = pl.ds(pl.multiple_of(start + step * chunk, chunk), chunk)
                    value = (tokens[source, lower : lower + cap, some].astype(jnp.float32) - mean) * rate
                    normed[at, to] = (value * (1.0 + mod_ref[1:2, to]) + mod_ref[0:1, to]).astype(
                        normed.dtype
                    )
            return carry

        lax.fori_loop(0, SPLIT, normalise, 0)
        raw = jnp.dot(normed[...], first[...], preferred_element_type=jnp.float32)
        hidden[...] = jax.nn.gelu(raw, approximate=True).astype(hidden.dtype)

    def to_twin(plane, j):
        return remote(
            block(part, plane * SPLIT + (1 - c) * 2, 2, j),
            block(r1, plane * 2, 2, j),
            back_send.at[plane, 0],
            s1_recv.at[plane, j],
            twin,
        )

    def to_beside(plane, j):
        return remote(
            block(part, plane * SPLIT + c * 2 + 1 - y, 1, j),
            block(r2, plane, 1, j),
            back_send.at[plane, 1],
            s2_recv.at[plane, j],
            beside,
        )

    def slots_home(plane, j):
        return remote(
            pair.at[plane, pl.ds(0, cap), back_cols(j)],
            pair.at[plane, pl.ds(cap, cap), back_cols(j)],
            back_send.at[plane, 2],
            pair_recv.at[plane, j],
            inner_device,
        )

    def rows_home(plane, j):
        return remote(
            acc_out.at[plane, :, back_cols(j)],
            acc_in.at[plane, :, back_cols(j)],
            back_send.at[plane, 3],
            acc_recv.at[plane, j],
            device(jnp.where(plane == outer, outer, inner), y, c),
        )

    def produce(i, j):
        plane = home_of(i)
        pl.when(jnp.logical_and(j == 0, i < 2))(lambda: arrive(plane))
        pl.when(j == 0)(lambda: start_group(plane))
        raw = jnp.dot(hidden[...], second[:, back_cols(j)], preferred_element_type=jnp.float32)
        mine = pl.ds(pl.multiple_of(plane * group, 16), group)
        part[mine, back_cols(j)] = raw.astype(part.dtype)
        to_twin(plane, j).start()

    def fold_twin(i, j):
        plane = home_of(i)
        landed(block(r1, plane * 2, 2, j), s1_recv.at[plane, j])
        for yy in (1 - y, y):
            at = pl.ds(pl.multiple_of((plane * SPLIT + c * 2 + yy) * cap, 16), cap)
            there = pl.ds(pl.multiple_of((plane * 2 + yy) * cap, 16), cap)
            total = part[at, back_cols(j)].astype(jnp.float32) + r1[there, back_cols(j)].astype(jnp.float32)
            part[at, back_cols(j)] = total.astype(part.dtype)
            if yy is not y:
                to_beside(plane, j).start()

    def fold_beside(i, j):
        plane = home_of(i)
        there = device(plane, y, c)
        landed(block(r2, plane, 1, j), s2_recv.at[plane, j])
        weight = picked_column(chosen(there, p), tables[there, pl.ds(8 + p, 1), :])
        ours = pl.ds(pl.multiple_of((plane * SPLIT + c * 2 + y) * cap, 16), cap)
        theirs = pl.ds(pl.multiple_of(plane * cap, 16), cap)
        total = part[ours, back_cols(j)].astype(jnp.float32) + r2[theirs, back_cols(j)].astype(jnp.float32)
        pair[plane, :cap, back_cols(j)] = (total * weight).astype(pair.dtype)
        pl.when(jnp.logical_and(at_end, plane != p))(slots_home(plane, j).start)

    def spread_out(plane, both, at):
        amount = 2 * cap if both else cap
        return lax.dot_general(
            spreader[plane, :amount, :],
            pair[plane, :amount, at],
            (((0,), (0,)), ((), ())),
            preferred_element_type=jnp.float32,
        )

    def fold_home(i, j):
        plane = home_of(i)
        at = back_cols(j)

        def fold(both, extra, last):
            if both:
                landed(pair.at[plane, pl.ds(cap, cap), at], pair_recv.at[plane, j])
            if extra:
                landed(acc_in.at[plane, :, at], acc_recv.at[plane, j])
            total = spread_out(plane, both, at)
            if extra:
                total = total + acc_in[plane, :, at].astype(jnp.float32)
            if last:
                out_ref[:, at] = (mod_ref[2:3, at] * total + out_ref[:, at].astype(jnp.float32)).astype(
                    out_ref.dtype
                )
            else:
                acc_out[plane, :, at] = total.astype(acc_out.dtype)
                rows_home(plane, j).start()

        pl.when(jnp.logical_and(at_end, i == 3))(lambda: fold(False, True, True))
        pl.when(jnp.logical_and(middle, i == 3))(lambda: fold(True, True, True))
        pl.when(jnp.logical_and(middle, i == 2))(lambda: fold(False, True, False))
        pl.when(jnp.logical_and(middle, i < 2))(lambda: fold(True, False, False))

    units = planes * backs

    def give_back(u, carry):
        for behind, act in ((0, produce), (BACK_LAGS[0], fold_twin), (BACK_LAGS[1], fold_beside), (BACK_LAGS[2], fold_home)):
            at = u - behind
            i, j = lax.div(at, backs), lax.rem(at, backs)
            pl.when(jnp.logical_and(at >= 0, at < units))(functools.partial(act, i, j))
        return carry

    lax.fori_loop(0, EARLY, give_back, 0)
    lax.fori_loop(chunks + BEHIND + DRAIN[1], chunks + BEHIND + 4 * HOP, drain, 0)
    pl.when(at_end)(lambda: landed(line.at[partner_plane, pl.ds(rows, rows), :], rest_sem.at[1]))
    out_ref[:, halves(mine_from)] = att[:rows, :]
    out_ref[:, halves(other_from)] = line[partner_plane, rows:, :]
    lax.fori_loop(EARLY, units + BACK_LAGS[2], give_back, 0)

    def gone(ref, sem):
        remote(ref, ref, sem, own_sem.at[0], twin).wait_send()

    every = pl.ds(0, half)
    gone(bytes_of(3, every), kv_send.at[0])
    for level in (0, 1):
        for index, (_, exists) in enumerate(sides):
            when(exists, functools.partial(gone, bytes_of(2, every), kv_send.at[1 + level * 2 + index]))
    for k, (_, _, whole, out) in enumerate(sources):
        if whole is not False:
            when(whole, functools.partial(gone, line.at[0], out_send.at[k, 0]))
        if out is not False:
            when(out, functools.partial(gone, stage.at[0], out_send.at[k, 1]))
        for index in range(3):
            gone(tokens.at[0], out_send.at[k, 2 + index])
    pl.when(middle)(lambda: gone(line.at[0, pl.ds(0, rows), :], rest_sem.at[0]))
    gone(tables.at[pl.ds(0, planes - 1)], table_send.at[0])
    gone(stats.at[pl.ds(0, n - 1)], table_send.at[1])
    for plane in range(planes):
        gone(r1.at[pl.ds(0, 2 * cap), :], back_send.at[plane, 0])
        gone(r1.at[pl.ds(0, cap), :], back_send.at[plane, 1])
        away = p != plane
        pl.when(jnp.logical_and(at_end, away))(
            functools.partial(gone, r1.at[pl.ds(0, cap), :], back_send.at[plane, 2])
        )
        pl.when(jnp.logical_and(middle, away))(functools.partial(gone, acc_in.at[0], back_send.at[plane, 3]))


def kernel_bytes(n, rows, cap, width):
    planes = n // SPLIT
    lines = 2 * 6 * rows + 2 * n * cap + planes * (6 * cap + 3 * rows) + SPLIT * cap + 3 * rows
    return 2 * (lines * D + 2 * width * D)


def layer(queries, key_rows, values, modulation, expert_in, expert_out, routes, gate_fixed):
    n = lax.axis_size("tile")
    rows = queries.shape[0]
    width = expert_in.shape[1]
    planes = n // SPLIT
    cap = 3 * rows // planes
    chunks, backs = CHUNKS, BACK_CHUNKS
    vmem = pl.BlockSpec(memory_space=pltpu.VMEM)
    hbm = pl.BlockSpec(memory_space=pl.ANY)
    dma = pltpu.SemaphoreType.DMA
    bf = jnp.bfloat16
    return pl.pallas_call(
        functools.partial(layer_kernel, n, rows, cap, CHUNKS, BACK_CHUNKS),
        name="whole_layer",
        out_shape=pltpu.VMEM((rows, D), bf),
        in_specs=[hbm, hbm, hbm, vmem, vmem, vmem, hbm, hbm],
        out_specs=vmem,
        scratch_shapes=[
            pltpu.VMEM((2 * rows, D // 2), bf),
            pltpu.VMEM((2 * rows, D // 2), bf),
            pltpu.VMEM((8, 6 * rows), jnp.float32),
            pltpu.VMEM((6 * rows, D // 2), bf),
            pltpu.VMEM((6 * rows, D // 2), bf),
            pltpu.VMEM((planes, 2 * rows, D // 2), bf),
            pltpu.VMEM((n, 2 * cap, D // 2), bf),
            pltpu.VMEM((planes, 2 * cap, D // 2), bf),
            pltpu.VMEM((planes, 4 * cap, 2 * rows), bf),
            pltpu.VMEM((planes, 2 * cap, rows), bf),
            pltpu.VMEM((n, 16, rows), jnp.float32),
            pltpu.VMEM((n, 16, rows), jnp.float32),
            pltpu.VMEM((SPLIT * cap, D), bf),
            pltpu.VMEM((D, width), bf),
            pltpu.VMEM((width, D), bf),
            pltpu.VMEM((SPLIT * cap, width), bf),
            pltpu.VMEM((n * cap, D), bf),
            pltpu.VMEM((planes * 2 * cap, D), bf),
            pltpu.VMEM((planes * cap, D), bf),
            pltpu.VMEM((planes, 2 * cap, D), bf),
            pltpu.VMEM((planes, rows, D), bf),
            pltpu.VMEM((planes, rows, D), bf),
            dma((5,)),
            dma((5,)),
            dma((6, chunks)),
            dma((2,)),
            dma((2,)),
            dma((planes, 5)),
            dma((planes, chunks)),
            dma((planes, chunks)),
            dma((n,)),
            dma((2,)),
            dma((planes, 4)),
            dma((planes, backs)),
            dma((planes, backs)),
            dma((planes, backs)),
            dma((planes, backs)),
        ],
        compiler_params=pltpu.CompilerParams(
            collective_id=1, has_side_effects=True, vmem_limit_bytes=VMEM_LIMIT
        ),
    )(queries, key_rows, values, modulation, routes.T, gate_fixed.T, expert_in, expert_out)


def slot_table(flat, experts_count):
    onehot = (flat[:, None] == jnp.arange(experts_count, dtype=jnp.int32)[None, :]).astype(
        jnp.int32
    )
    before = jnp.cumsum(onehot, axis=0) - onehot
    return jnp.sum(before * onehot, axis=1)


def expert_apply(rows, first_weight, second_weight):
    hidden = jax.nn.gelu(
        jnp.dot(rows, first_weight, preferred_element_type=jnp.float32), approximate=True
    ).astype(jnp.bfloat16)
    return jnp.dot(hidden, second_weight, preferred_element_type=jnp.float32).astype(jnp.bfloat16)


def experts_sparse(normed, attended, modulation, expert_in, expert_out, routes, gate_fixed):
    devices = lax.axis_size("tile")
    rows_dev = normed.shape[0]
    experts_count = devices // SPLIT
    capacity = 3 * rows_dev // experts_count
    flat = routes.reshape(-1)
    slots = slot_table(flat, experts_count)
    target = flat * capacity + slots
    chooser = (
        target[None, :] == jnp.arange(experts_count * capacity, dtype=jnp.int32)[:, None]
    ).astype(jnp.bfloat16)
    chooser = chooser.reshape(experts_count * capacity, rows_dev, 2).sum(axis=2)
    buffer = jnp.dot(chooser, normed, preferred_element_type=jnp.float32).astype(jnp.bfloat16)
    copies = jnp.broadcast_to(
        buffer.reshape(experts_count, 1, capacity, D), (experts_count, SPLIT, capacity, D)
    ).reshape(devices, capacity, D)
    received = lax.all_to_all(copies, "tile", split_axis=0, concat_axis=0, tiled=True)
    sources = received.shape[0]
    count = received.shape[1]
    partial_value = expert_apply(received.reshape(sources * count, D), expert_in, expert_out)
    returned = lax.all_to_all(
        partial_value.reshape(sources, count, D), "tile", split_axis=0, concat_axis=0, tiled=True
    )
    summed = jnp.sum(
        returned.reshape(experts_count, SPLIT, capacity, D).astype(jnp.float32), axis=1
    )
    expert_rows = summed.astype(jnp.bfloat16).reshape(experts_count * capacity, D)
    picked = jnp.take(expert_rows, target, axis=0).reshape(rows_dev, 2, D)
    gate_scale = gate_fixed.astype(jnp.float32) / 1024.0
    mixture = jnp.sum(picked.astype(jnp.float32) * gate_scale[:, :, None], axis=1)
    return (attended.astype(jnp.float32) + modulation[2] * mixture).astype(jnp.bfloat16)


def shards(queries, key_rows, values, modulation, expert_in, expert_out, routes, gate_fixed):
    n = lax.axis_size("tile")
    cap = 3 * queries.shape[0] // (n // SPLIT)
    if n == 2 * TILE_COLS and cap % 16 == 0 and kernel_bytes(n, queries.shape[0], cap, expert_in.shape[1]) < VMEM_LIMIT * 7 // 8:
        return layer(queries, key_rows, values, modulation, expert_in, expert_out, routes, gate_fixed)
    attended, normed = attention(queries, key_rows, values, modulation)
    return experts_sparse(normed, attended, modulation, expert_in, expert_out, routes, gate_fixed)


def solution(mesh):
    placed = (
        P(("groups", "tile"), None),
        P(("groups", "tile"), None),
        P(("groups", "tile"), None),
        P("groups", None),
        P(None, "tile"),
        P("tile", None),
        P(("groups", "tile"), None),
        P(("groups", "tile"), None),
    )
    return jax.shard_map(
        shards, mesh=mesh, in_specs=placed, out_specs=P(("groups", "tile"), None), check_vma=False
    )
```

```python
import functools
import math

import jax
import jax.numpy as jnp
from jax import lax
from jax.experimental import pallas as pl
from jax.experimental.pallas import tpu as pltpu
from jax.sharding import PartitionSpec as P

HEAD_DIM = 128
D = 4096
SPLIT = 4
TILE_COLS = 8

EPSILON = 1e-06
MASKED = -1e30
MESH = pl.DeviceIdType.MESH
VMEM_LIMIT = 60 * 1024 * 1024
CHUNKS = 8
AHEAD = 2
ASIDE = 2
BEHIND = 1
HOP = 2
PASS = 4
DRAIN = (2, 8)
EARLY = 2
BACK_CHUNKS = 4
BACK_LAGS = (1, 4, 6)


def when(cond, body):
    if cond is True:
        body()
    else:
        pl.when(cond)(body)


def both(a, b):
    if a is True:
        return b
    if b is True:
        return a
    return jnp.logical_and(a, b)


def remote(src, dst, send_sem, recv_sem, target):
    return pltpu.make_async_remote_copy(
        src_ref=src,
        dst_ref=dst,
        send_sem=send_sem,
        recv_sem=recv_sem,
        device_id={"tile": target},
        device_id_type=MESH,
    )


def halo_levels(n):
    grid_rows = n // TILE_COLS
    if grid_rows < 2:
        return 1
    return 2 if grid_rows == 2 else 3


def attention_kernel(
    n, rows, q_ref, k_ref, v_ref, mod_ref, att_ref, norm_ref, keys, vals, send_sem, recv_sem, own_sem,
):
    me = lax.axis_index("tile")
    grid_rows = n // TILE_COLS
    tile = lax.rem(me + TILE_COLS // 2, n)
    row = lax.div(tile, TILE_COLS)
    col = lax.rem(tile, TILE_COLS)
    if grid_rows < 2:
        verticals = []
    elif grid_rows == 2:
        verticals = [(1, TILE_COLS, True, 1)]
    else:
        verticals = [(1, n - TILE_COLS, row > 0, 2), (2, TILE_COLS, row < grid_rows - 1, 1)]
    sides = [(-1, col > 0), (1, col < TILE_COLS - 1)]
    here = {level: exists for level, _, exists, _ in verticals}
    here[0] = True

    def slot(level, side):
        return level * 3 + 1 + side

    def place(buf, s):
        return buf.at[pl.ds(s * rows, rows), :]

    def over(offset):
        return lax.rem(me + offset + n, n)

    half = rows // 2
    middle = TILE_COLS // 2
    crossing = {side: col == (middle if side < 0 else middle - 1) for side, _ in sides}
    two = grid_rows == 2

    def part_of(buf, s, h):
        return buf.at[pl.ds(pl.multiple_of(s * rows + h * half, half), half), :]

    own = [
        pltpu.make_async_copy(src, place(buf, slot(0, 0)), own_sem.at[i])
        for i, (src, buf) in enumerate(((k_ref, keys), (v_ref, vals)))
    ]
    for copy in own:
        copy.start()

    def beside(side):
        if not two:
            return over(side)
        return jnp.where(crossing[side], over(side + TILE_COLS), over(side))

    def level_there(level, side):
        return jnp.where(crossing[side], 1 - level, level) if two else level

    barrier = pltpu.get_barrier_semaphore()
    partners = [(over(offset), exists) for _, offset, exists, _ in verticals]
    partners += [(beside(side), exists) for side, exists in sides]
    for target, exists in partners:

        def greet(target=target):
            pl.semaphore_signal(barrier, inc=1, device_id={"tile": target}, device_id_type=MESH)

        when(exists, greet)
    expected = sum(1 if exists is True else jnp.where(exists, 1, 0) for _, exists in partners)
    pl.semaphore_wait(barrier, expected)

    sends = []
    pieces = [(i, h) for i in (0, 1) for h in (0, 1)]
    bufs = (keys, vals)

    def push(i, h, src, there, target, exists):
        copy = remote(
            src,
            part_of(bufs[i], there, h),
            send_sem.at[len(sends)],
            recv_sem.at[there, i * 2 + h],
            target,
        )
        when(exists, copy.start)
        sends.append((copy, exists))

    def arrived(s, exists, i, h):
        ref = part_of(bufs[i], s, h)
        when(exists, remote(ref, ref, send_sem.at[0], recv_sem.at[s, i * 2 + h], me).wait_recv)

    def own_part(i, h):
        return (k_ref, v_ref)[i].at[pl.ds(h * half, half), :]

    for i, h in pieces:
        for level, offset, exists, there in verticals:
            push(i, h, own_part(i, h), slot(there, 0), over(offset), exists)
    for i, h in pieces:
        for side, exists in sides:
            push(i, h, own_part(i, h), slot(level_there(0, side), -side), beside(side), exists)
    for s in range(3 * (1 + len(verticals))):
        level, side = s // 3, s % 3 - 1
        exists = here[level]
        for other, side_exists in sides:
            if other == side:
                exists = both(exists, side_exists)
        if exists is True:
            continue

        def clear(s=s):
            for buf in (keys, vals):
                buf[pl.ds(s * rows, rows), :] = jnp.zeros((rows, D), buf.dtype)

        pl.when(jnp.logical_not(exists))(clear)
    for i, h in pieces:
        for level, offset, exists, there in verticals:
            arrived(slot(level, 0), exists, i, h)
            for side, side_exists in sides:
                push(
                    i,
                    h,
                    part_of(bufs[i], slot(level, 0), h),
                    slot(level_there(level, side), -side),
                    beside(side),
                    both(exists, side_exists),
                )
    for copy in own:
        copy.wait()
    for i, h in pieces:
        for level, exists in sorted(here.items(), key=lambda item: item[0]):
            for side, side_exists in sides:
                arrived(slot(level, side), both(exists, side_exists), i, h)

    span = 3 * (1 + len(verticals)) * rows
    where = lax.broadcasted_iota(jnp.int32, (rows, span), 1)
    bias = jnp.zeros((rows, span), jnp.float32)
    for s in range(span // rows):
        level, side = s // 3, s % 3 - 1
        exists = here[level]
        for other, side_exists in sides:
            if other == side:
                exists = both(exists, side_exists)
        if exists is True:
            continue
        penalty = jnp.where(exists, 0.0, MASKED)
        bias = jnp.where((where >= s * rows) & (where < (s + 1) * rows), penalty, bias)
    scale = 1.0 / math.sqrt(HEAD_DIM)
    together = 8

    def heads(step, carry):
        for extra in range(together):
            at = pl.ds(pl.multiple_of((step * together + extra) * HEAD_DIM, HEAD_DIM), HEAD_DIM)
            scores = lax.dot_general(
                q_ref[:, at], keys[:, at], (((1,), (1,)), ((), ())), preferred_element_type=jnp.float32
            )
            scores = scores * scale + bias
            raised = jnp.exp(scores - jnp.max(scores, axis=-1, keepdims=True))
            probs = (raised * (1.0 / jnp.sum(raised, axis=-1, keepdims=True))).astype(jnp.bfloat16)
            att_ref[:, at] = jnp.dot(probs, vals[:, at], preferred_element_type=jnp.float32).astype(
                att_ref.dtype
            )
        return carry

    lax.fori_loop(0, D // HEAD_DIM // together, heads, 0)

    def normalise(step, carry):
        at = pl.ds(pl.multiple_of(step * 16, 16), 16)
        wide = att_ref[at, :].astype(jnp.float32)
        wide = wide - jnp.mean(wide, axis=-1, keepdims=True)
        spread = jnp.mean(wide * wide, axis=-1, keepdims=True)
        normed = wide * lax.rsqrt(spread + EPSILON)
        norm_ref[at, :] = (normed * (1.0 + mod_ref[1:2, :]) + mod_ref[0:1, :]).astype(norm_ref.dtype)
        return carry

    lax.fori_loop(0, rows // 16, normalise, 0)
    for copy, exists in sends:
        when(exists, copy.wait_send)


def attention(queries, key_rows, values, modulation):
    n = lax.axis_size("tile")
    rows = queries.shape[0]
    levels = halo_levels(n)
    slots = 3 * levels
    vmem = pl.BlockSpec(memory_space=pltpu.VMEM)
    hbm = pl.BlockSpec(memory_space=pl.ANY)
    return pl.pallas_call(
        functools.partial(attention_kernel, n, rows),
        name="halo_attention",
        out_shape=(
            jax.ShapeDtypeStruct((rows, D), jnp.bfloat16),
            jax.ShapeDtypeStruct((rows, D), jnp.bfloat16),
        ),
        in_specs=[vmem, hbm, hbm, vmem],
        out_specs=(vmem, vmem),
        scratch_shapes=[
            pltpu.VMEM((slots * rows, D), jnp.bfloat16),
            pltpu.VMEM((slots * rows, D), jnp.bfloat16),
            pltpu.SemaphoreType.DMA((4 * (2 + 3 * (levels - 1)),)),
            pltpu.SemaphoreType.DMA((slots, 4)),
            pltpu.SemaphoreType.DMA((2,)),
        ],
        compiler_params=pltpu.CompilerParams(
            collective_id=0, has_side_effects=True, vmem_limit_bytes=VMEM_LIMIT
        ),
    )(queries, key_rows, values, modulation)


def device(plane, yy, cc):
    return plane * SPLIT + yy * 2 + cc


def layer_kernel(
    n, rows, cap, chunks, backs, q_ref, k_ref, v_ref, mod_ref, routes_ref, gates_ref, first_ref, second_ref,
    out_ref, att, asked, bias, keys, vals, line, tokens, stage, chooser, spreader, tables, stats, normed,
    first, second, hidden, part, r1, r2, pair, acc_in, acc_out,
    own_sem, kv_send, kv_recv, table_send, table_recv, out_send, line_recv, beside_recv, twin_recv,
    rest_sem, back_send, s1_recv, s2_recv, pair_recv, acc_recv,
):
    planes = n // SPLIT
    width = first.shape[1]
    half = D // 2
    wide = half // chunks
    me = lax.axis_index("tile")
    p = lax.div(me, SPLIT)
    y = lax.div(lax.rem(me, SPLIT), 2)
    c = lax.rem(me, 2)
    beside = device(p, 1 - y, c)
    twin = device(p, y, 1 - c)
    low_half = p < planes // 2
    toward = jnp.where(low_half, 1, -1)
    inner = p + toward
    outer = p - toward
    at_end = jnp.logical_or(p == 0, p == planes - 1)
    middle = jnp.logical_not(at_end)
    outer_expert = jnp.where(low_half, 0, planes - 1)
    inner_device = device(inner, y, c)
    outer_device = device(jnp.where(at_end, p, outer), y, c)

    tile = lax.rem(me + TILE_COLS // 2, n)
    column = lax.rem(tile, TILE_COLS)
    partner = lax.rem(me + TILE_COLS, n)
    sides = [(-1, column > 0), (1, column < TILE_COLS - 1)]
    half_way = TILE_COLS // 2
    crossing = {-1: column == half_way, 1: column == half_way - 1}

    def part_of_plane(plane):
        return jnp.where(plane < planes // 2, half, 0)

    mine_from = part_of_plane(p)
    other_from = half - mine_from
    partner_plane = lax.rem(p + planes // 2, planes)

    def cols(j, base=0):
        return pl.ds(pl.multiple_of(base + j * wide, wide), wide)

    def halves(base):
        return pl.ds(pl.multiple_of(base, half), half)

    def lines(buf, s):
        return buf.at[pl.ds(pl.multiple_of(s * rows, rows), rows), :]

    loads = [
        pltpu.make_async_copy(q_ref.at[:, halves(mine_from)], lines(asked, 0), own_sem.at[0]),
        pltpu.make_async_copy(k_ref.at[:, halves(mine_from)], lines(keys, 1), own_sem.at[1]),
        pltpu.make_async_copy(v_ref.at[:, halves(mine_from)], lines(vals, 1), own_sem.at[2]),
        pltpu.make_async_copy(first_ref, first, own_sem.at[3]),
        pltpu.make_async_copy(second_ref, second, own_sem.at[4]),
    ]

    barrier = pltpu.get_barrier_semaphore()
    others = [lax.rem(me + step, n) for step in range(1, n)]
    for target in others:
        pl.semaphore_signal(barrier, inc=1, device_id={"tile": target}, device_id_type=MESH)

    def beside_tile(side):
        return lax.rem(me + side + jnp.where(crossing[side], TILE_COLS, 0) + n, n)

    def slot_there(level, side):
        return jnp.where(crossing[side], 1 - level, level) * 3 + 1 - side

    bufs = (keys, vals, asked)
    given = (k_ref, v_ref, q_ref)

    def place(i, s, j):
        return bufs[i].at[pl.ds(pl.multiple_of(s * rows, rows), rows), cols(j)]

    def over_vertical(i, j):
        return remote(
            given[i].at[:, cols(j, other_from)],
            place(i, 4 if i < 2 else 1, j),
            kv_send.at[0],
            kv_recv.at[4, j],
            partner,
        )

    def over_side(level, index, i, j):
        side = sides[index][0]
        there = slot_there(level, side)
        source = given[i].at[:, cols(j, mine_from)] if level == 0 else place(i, 4, j)
        return remote(
            source,
            place(i, there, j),
            kv_send.at[1 + level * 2 + index],
            kv_recv.at[there, j],
            beside_tile(side),
        )

    def landed(ref, sem):
        remote(ref, ref, own_sem.at[0], sem, me).wait_recv()

    def send_own(j):
        for i in range(3):
            over_vertical(i, j).start()

    def send_side(j):
        for i in (0, 1):
            for index, (_, exists) in enumerate(sides):
                when(exists, over_side(0, index, i, j).start)

    def bytes_of(count, at):
        return keys.at[pl.ds(0, count * rows), at]

    def send_vertical(j):
        landed(bytes_of(3, cols(j)), kv_recv.at[4, j])
        for i in (0, 1):
            for index, (_, exists) in enumerate(sides):
                when(exists, over_side(1, index, i, j).start)

    pl.semaphore_wait(barrier, n - 1)
    send_own(0)
    send_side(0)
    for load in loads[:3]:
        load.start()

    expert = lax.broadcasted_iota(jnp.int32, (8, rows), 0)
    named = [routes_ref[k : k + 1, :] == expert for k in (0, 1)]
    member = jnp.logical_or(named[0], named[1])
    upto = (
        lax.broadcasted_iota(jnp.int32, (rows, rows), 0) <= lax.broadcasted_iota(jnp.int32, (rows, rows), 1)
    ).astype(jnp.float32).astype(jnp.bfloat16)
    count = jnp.dot(
        member.astype(jnp.float32).astype(jnp.bfloat16), upto, preferred_element_type=jnp.float32
    )
    gate = sum(
        jnp.where(named[k], gates_ref[k : k + 1, :].astype(jnp.float32), 0.0) for k in (0, 1)
    )
    tables[me, 0:8, :] = jnp.where(member, count - 1.0, -1.0)
    stats[me, 8:16, :] = jnp.where(member, count - 1.0, -1.0)
    tables[me, 8:16, :] = gate / 1024.0

    column_planes = [lax.rem(p + step, planes) for step in range(1, planes)]

    def tell_column(step):
        there = device(column_planes[step], y, c)
        return remote(tables.at[me], tables.at[me], table_send.at[0], table_recv.at[0], there)

    for step in range(planes - 1):
        tell_column(step).start()
    for j in range(1, max(AHEAD, ASIDE)):
        if j < min(AHEAD, chunks):
            send_own(j)
        if j < min(ASIDE, chunks):
            send_side(j)

    span = 6 * rows
    where = lax.broadcasted_iota(jnp.int32, (8, span), 1)
    penalty = jnp.zeros((8, span), jnp.float32)
    for s in range(6):
        for side, exists in sides:
            if side != s % 3 - 1:
                continue
            here = (where >= s * rows) & (where < (s + 1) * rows)
            penalty = jnp.where(here, jnp.where(exists, 0.0, MASKED), penalty)

            def clear(s=s):
                for buf in (keys, vals):
                    buf[s * rows : (s + 1) * rows, :] = jnp.zeros((rows, half), buf.dtype)

            pl.when(jnp.logical_not(exists))(clear)
    bias[...] = penalty

    def tell_all():
        return [
            remote(stats.at[me], stats.at[me], table_send.at[1], table_recv.at[1], target)
            for target in others
        ]

    for load in loads[:3]:
        load.wait()
    for load in loads[3:]:
        load.start()

    slot_line = lax.broadcasted_iota(jnp.int32, (cap, rows), 0).astype(jnp.float32)

    def chosen(tile_there, e):
        return tables[tile_there, pl.ds(e, 1), :] == slot_line

    def picked_column(which, row):
        return jnp.sum(jnp.where(which, row, 0.0), axis=1, keepdims=True)

    def choose():
        landed(tables.at[pl.ds(0, planes - 1)], table_recv.at[0])
        chooser[...] = jnp.zeros(chooser.shape, chooser.dtype)
        for plane in range(planes):
            for place_in, e in ((0, p), (1, outer_expert)):
                found = chosen(device(plane, y, c), e).astype(jnp.float32).astype(jnp.bfloat16)
                at = place_in * 2 * cap
                spreader[plane, place_in * cap : (place_in + 1) * cap, :] = found
                chooser[plane, at : at + cap, :rows] = found
                chooser[(plane + planes // 2) % planes, at + cap : at + 2 * cap, rows:] = found

    scale = 1.0 / math.sqrt(HEAD_DIM)

    def attend(j):
        for level in (0, 1):
            for side, exists in sides:
                s = level * 3 + 1 + side
                when(exists, functools.partial(landed, bytes_of(2, cols(j)), kv_recv.at[s, j]))
        for extra in range(wide // HEAD_DIM):
            at = pl.ds(pl.multiple_of(j * wide + extra * HEAD_DIM, HEAD_DIM), HEAD_DIM)
            scores = lax.dot_general(
                asked[:, at], keys[:, at], (((1,), (1,)), ((), ())), preferred_element_type=jnp.float32
            )
            scores = scores * scale + bias[0:1, :]
            raised = jnp.exp(scores - jnp.max(scores, axis=-1, keepdims=True))
            probs = (raised * (1.0 / jnp.sum(raised, axis=-1, keepdims=True))).astype(jnp.bfloat16)
            att[:, at] = jnp.dot(probs, vals[:, at], preferred_element_type=jnp.float32).astype(att.dtype)

    def raw_copy(k, src, j):
        source = att.at[:, cols(j)] if k == 0 else line.at[src, :, cols(j)]
        return remote(source, line.at[src, :, cols(j)], out_send.at[k, 0], line_recv.at[src, j], inner_device)

    def outer_copy(k, src, j):
        there = device(src, y, c)
        return remote(
            stage.at[src, :, cols(j)],
            tokens.at[there, :, cols(j)],
            out_send.at[k, 1],
            line_recv.at[src, j],
            outer_device,
        )

    def rest_copy(src, j):
        ref = line.at[src, pl.ds(rows, rows), cols(j)]
        return remote(ref, ref, rest_sem.at[0], rest_sem.at[1], outer_device)

    def plane_copy(k, src, j, index):
        ref = tokens.at[device(src, y, c), :, cols(j)]
        recv = beside_recv.at[src, j] if index == 0 else twin_recv.at[device(src, y, c)]
        return remote(ref, ref, out_send.at[k, 2 + index], recv, (beside, twin)[index])

    def twin_copy(k, src, j):
        there = device(src, 1 - y, c)
        ref = tokens.at[there, :, cols(j)]
        return remote(ref, ref, out_send.at[k, 4], twin_recv.at[there], twin)

    far = jnp.where(at_end, p + 3 * toward, p + 2 * toward)
    second_plane = jnp.where(at_end, p + 2 * toward, outer)
    sources = [
        (p, BEHIND, True, middle),
        (inner, BEHIND + HOP, False, middle),
        (second_plane, BEHIND + HOP * jnp.where(at_end, 2, 1), middle, False),
        (far, BEHIND + HOP * jnp.where(at_end, 3, 2), False, middle),
    ]

    def relay(k, j):
        src, behind, whole, out = sources[k]
        jj = j - behind

        def go():
            there = device(src, y, c)
            if k > 0:
                pl.when(at_end)(
                    lambda: landed(tokens.at[there, :, cols(jj)], line_recv.at[src, jj])
                )
                pl.when(middle)(lambda: landed(line.at[src, :, cols(jj)], line_recv.at[src, jj]))
            if whole is not False:
                when(whole, raw_copy(k, src, jj).start)
            if k == 1:
                pl.when(middle)(rest_copy(src, jj).start)

            def pick():
                rows_here = att[:, cols(jj)] if k == 0 else line[src, :, cols(jj)]
                picked = jnp.dot(chooser[src], rows_here, preferred_element_type=jnp.float32).astype(
                    tokens.dtype
                )
                tokens[there, :, cols(jj)] = picked[: 2 * cap]
                stage[src, :, cols(jj)] = picked[2 * cap :]

            when(True if k == 0 else middle, pick)
            if out is not False:
                when(out, outer_copy(k, src, jj).start)
            for index in (0, 1):
                plane_copy(k, src, jj, index).start()

        pl.when(jnp.logical_and(jj >= 0, jj < chunks))(go)

    def pass_on(k, j):
        src, behind, _, _ = sources[k]
        jj = j - behind - PASS

        def go():
            there = device(src, 1 - y, c)
            landed(tokens.at[there, :, cols(jj)], beside_recv.at[src, jj])
            twin_copy(k, src, jj).start()

        pl.when(jnp.logical_and(jj >= 0, jj < chunks))(go)

    def move(j):
        for k in range(planes):
            relay(k, j)
        for k in range(planes):
            pass_on(k, j)

    def stream(j, carry):
        pl.when(j < chunks)(lambda: send_vertical(j))

        pl.when(j + AHEAD < chunks)(lambda: send_own(j + AHEAD))
        pl.when(j + ASIDE < chunks)(lambda: send_side(j + ASIDE))
        pl.when(j == BEHIND)(choose)
        pl.when(j >= BEHIND)(lambda: attend(j - BEHIND))
        move(j)
        return carry

    lax.fori_loop(0, chunks + BEHIND, stream, 0)

    def drain(j, carry):
        move(j)
        return carry

    lax.fori_loop(chunks + BEHIND, chunks + BEHIND + DRAIN[0], drain, 0)

    token = lax.broadcasted_iota(jnp.int32, (16, rows), 1)
    line_of = lax.broadcasted_iota(jnp.int32, (16, rows), 0)
    row_number = lax.broadcasted_iota(jnp.int32, (8, rows), 0)
    found = jnp.zeros((8, rows), jnp.float32)
    for step in range(2 * rows // 16):
        some = att[step * 16 : (step + 1) * 16, :].astype(jnp.float32)
        mean = jnp.mean(some, axis=-1, keepdims=True)
        some = some - mean
        spread = jnp.mean(some * some, axis=-1, keepdims=True)
        which, at = divmod(step * 16, rows)
        for kind, value in enumerate((mean, spread)):
            row = jnp.sum(jnp.where(token == line_of + at, value, 0.0), axis=0, keepdims=True)
            found = found + jnp.where(row_number == 2 * which + kind, row, 0.0)
    stats[me, 0:8, :] = found
    for copy in tell_all():
        copy.start()

    lax.fori_loop(chunks + BEHIND + DRAIN[0], chunks + BEHIND + DRAIN[1], drain, 0)
    landed(stats.at[pl.ds(0, n - 1)], table_recv.at[1])
    for load in loads[3:]:
        load.wait()

    order = [
        jnp.where(at_end, p + 2 * toward, inner),
        jnp.where(at_end, p + 3 * toward, p + 2 * toward),
        jnp.where(at_end, inner, outer),
        p,
    ]
    def arrive(plane):
        for source in (plane, lax.rem(plane + planes // 2, planes)):
            for yy in (0, 1):
                there = device(source, yy, 1 - c)
                landed(tokens.at[there], twin_recv.at[there])

    group = SPLIT * cap
    chunk = 512
    span_back = D // backs

    def home_of(i):
        return jnp.where(i == 0, order[0], jnp.where(i == 1, order[1], jnp.where(i == 2, order[2], order[3])))

    def block(buf, index, count, j):
        return buf.at[pl.ds(pl.multiple_of(index * cap, 16), count * cap), back_cols(j)]

    def back_cols(j):
        return pl.ds(pl.multiple_of(j * span_back, span_back), span_back)

    def start_group(plane):
        def normalise(t, carry):
            yy, cc = lax.rem(t, 2), lax.div(t, 2)
            there = device(plane, yy, cc)
            across = lax.rem(there + TILE_COLS, n)
            mean_here, mean_there = stats[there, 0:1, :], stats[across, 2:3, :]
            apart = 0.5 * (mean_here - mean_there)
            spread = 0.5 * (stats[there, 1:2, :] + stats[across, 3:4, :]) + apart * apart
            which = stats[there, pl.ds(8 + p, 1), :] == slot_line
            mean = picked_column(which, 0.5 * (mean_here + mean_there))
            rate = picked_column(which, lax.rsqrt(spread + EPSILON))
            at = pl.ds(pl.multiple_of(t * cap, 16), cap)
            base = part_of_plane(plane)
            for source, lower, start in ((there, 0, base), (across, cap, half - base)):
                for step in range(half // chunk):
                    some = slice(step * chunk, (step + 1) * chunk)
                    to = pl.ds(pl.multiple_of(start + step * chunk, chunk), chunk)
                    value = (tokens[source, lower : lower + cap, some].astype(jnp.float32) - mean) * rate
                    normed[at, to] = (value * (1.0 + mod_ref[1:2, to]) + mod_ref[0:1, to]).astype(
                        normed.dtype
                    )
            return carry

        lax.fori_loop(0, SPLIT, normalise, 0)
        raw = jnp.dot(normed[...], first[...], preferred_element_type=jnp.float32)
        hidden[...] = jax.nn.gelu(raw, approximate=True).astype(hidden.dtype)

    def to_twin(plane, j):
        return remote(
            block(part, plane * SPLIT + (1 - c) * 2, 2, j),
            block(r1, plane * 2, 2, j),
            back_send.at[plane, 0],
            s1_recv.at[plane, j],
            twin,
        )

    def to_beside(plane, j):
        return remote(
            block(part, plane * SPLIT + c * 2 + 1 - y, 1, j),
            block(r2, plane, 1, j),
            back_send.at[plane, 1],
            s2_recv.at[plane, j],
            beside,
        )

    def slots_home(plane, j):
        return remote(
            pair.at[plane, pl.ds(0, cap), back_cols(j)],
            pair.at[plane, pl.ds(cap, cap), back_cols(j)],
            back_send.at[plane, 2],
            pair_recv.at[plane, j],
            inner_device,
        )

    def rows_home(plane, j):
        return remote(
            acc_out.at[plane, :, back_cols(j)],
            acc_in.at[plane, :, back_cols(j)],
            back_send.at[plane, 3],
            acc_recv.at[plane, j],
            device(jnp.where(plane == outer, outer, inner), y, c),
        )

    def produce(i, j):
        plane = home_of(i)
        pl.when(jnp.logical_and(j == 0, i < 2))(lambda: arrive(plane))
        pl.when(j == 0)(lambda: start_group(plane))
        raw = jnp.dot(hidden[...], second[:, back_cols(j)], preferred_element_type=jnp.float32)
        mine = pl.ds(pl.multiple_of(plane * group, 16), group)
        part[mine, back_cols(j)] = raw.astype(part.dtype)
        to_twin(plane, j).start()

    def fold_twin(i, j):
        plane = home_of(i)
        landed(block(r1, plane * 2, 2, j), s1_recv.at[plane, j])
        for yy in (1 - y, y):
            at = pl.ds(pl.multiple_of((plane * SPLIT + c * 2 + yy) * cap, 16), cap)
            there = pl.ds(pl.multiple_of((plane * 2 + yy) * cap, 16), cap)
            total = part[at, back_cols(j)].astype(jnp.float32) + r1[there, back_cols(j)].astype(jnp.float32)
            part[at, back_cols(j)] = total.astype(part.dtype)
            if yy is not y:
                to_beside(plane, j).start()

    def fold_beside(i, j):
        plane = home_of(i)
        there = device(plane, y, c)
        landed(block(r2, plane, 1, j), s2_recv.at[plane, j])
        weight = picked_column(chosen(there, p), tables[there, pl.ds(8 + p, 1), :])
        ours = pl.ds(pl.multiple_of((plane * SPLIT + c * 2 + y) * cap, 16), cap)
        theirs = pl.ds(pl.multiple_of(plane * cap, 16), cap)
        total = part[ours, back_cols(j)].astype(jnp.float32) + r2[theirs, back_cols(j)].astype(jnp.float32)
        pair[plane, :cap, back_cols(j)] = (total * weight).astype(pair.dtype)
        pl.when(jnp.logical_and(at_end, plane != p))(slots_home(plane, j).start)

    def spread_out(plane, both, at):
        amount = 2 * cap if both else cap
        return lax.dot_general(
            spreader[plane, :amount, :],
            pair[plane, :amount, at],
            (((0,), (0,)), ((), ())),
            preferred_element_type=jnp.float32,
        )

    def fold_home(i, j):
        plane = home_of(i)
        at = back_cols(j)

        def fold(both, extra, last):
            if both:
                landed(pair.at[plane, pl.ds(cap, cap), at], pair_recv.at[plane, j])
            if extra:
                landed(acc_in.at[plane, :, at], acc_recv.at[plane, j])
            total = spread_out(plane, both, at)
            if extra:
                total = total + acc_in[plane, :, at].astype(jnp.float32)
            if last:
                out_ref[:, at] = (mod_ref[2:3, at] * total + out_ref[:, at].astype(jnp.float32)).astype(
                    out_ref.dtype
                )
            else:
                acc_out[plane, :, at] = total.astype(acc_out.dtype)
                rows_home(plane, j).start()

        pl.when(jnp.logical_and(at_end, i == 3))(lambda: fold(False, True, True))
        pl.when(jnp.logical_and(middle, i == 3))(lambda: fold(True, True, True))
        pl.when(jnp.logical_and(middle, i == 2))(lambda: fold(False, True, False))
        pl.when(jnp.logical_and(middle, i < 2))(lambda: fold(True, False, False))

    units = planes * backs

    def give_back(u, carry):
        for behind, act in ((0, produce), (BACK_LAGS[0], fold_twin), (BACK_LAGS[1], fold_beside), (BACK_LAGS[2], fold_home)):
            at = u - behind
            i, j = lax.div(at, backs), lax.rem(at, backs)
            pl.when(jnp.logical_and(at >= 0, at < units))(functools.partial(act, i, j))
        return carry

    lax.fori_loop(0, EARLY, give_back, 0)
    lax.fori_loop(chunks + BEHIND + DRAIN[1], chunks + BEHIND + 3 * HOP + PASS, drain, 0)
    pl.when(at_end)(lambda: landed(line.at[partner_plane, pl.ds(rows, rows), :], rest_sem.at[1]))
    out_ref[:, halves(mine_from)] = att[:rows, :]
    out_ref[:, halves(other_from)] = line[partner_plane, rows:, :]
    lax.fori_loop(EARLY, units + BACK_LAGS[2], give_back, 0)

    def gone(ref, sem):
        remote(ref, ref, sem, own_sem.at[0], twin).wait_send()

    every = pl.ds(0, half)
    gone(bytes_of(3, every), kv_send.at[0])
    for level in (0, 1):
        for index, (_, exists) in enumerate(sides):
            when(exists, functools.partial(gone, bytes_of(2, every), kv_send.at[1 + level * 2 + index]))
    for k, (_, _, whole, out) in enumerate(sources):
        if whole is not False:
            when(whole, functools.partial(gone, line.at[0], out_send.at[k, 0]))
        if out is not False:
            when(out, functools.partial(gone, stage.at[0], out_send.at[k, 1]))
        for index in range(3):
            gone(tokens.at[0], out_send.at[k, 2 + index])
    pl.when(middle)(lambda: gone(line.at[0, pl.ds(0, rows), :], rest_sem.at[0]))
    gone(tables.at[pl.ds(0, planes - 1)], table_send.at[0])
    gone(stats.at[pl.ds(0, n - 1)], table_send.at[1])
    for plane in range(planes):
        gone(r1.at[pl.ds(0, 2 * cap), :], back_send.at[plane, 0])
        gone(r1.at[pl.ds(0, cap), :], back_send.at[plane, 1])
        away = p != plane
        pl.when(jnp.logical_and(at_end, away))(
            functools.partial(gone, r1.at[pl.ds(0, cap), :], back_send.at[plane, 2])
        )
        pl.when(jnp.logical_and(middle, away))(functools.partial(gone, acc_in.at[0], back_send.at[plane, 3]))


def kernel_bytes(n, rows, cap, width):
    planes = n // SPLIT
    lines = 2 * 6 * rows + 2 * n * cap + planes * (6 * cap + 3 * rows) + SPLIT * cap + 3 * rows
    return 2 * (lines * D + 2 * width * D)


def layer(queries, key_rows, values, modulation, expert_in, expert_out, routes, gate_fixed):
    n = lax.axis_size("tile")
    rows = queries.shape[0]
    width = expert_in.shape[1]
    planes = n // SPLIT
    cap = 3 * rows // planes
    chunks, backs = CHUNKS, BACK_CHUNKS
    vmem = pl.BlockSpec(memory_space=pltpu.VMEM)
    hbm = pl.BlockSpec(memory_space=pl.ANY)
    dma = pltpu.SemaphoreType.DMA
    bf = jnp.bfloat16
    return pl.pallas_call(
        functools.partial(layer_kernel, n, rows, cap, CHUNKS, BACK_CHUNKS),
        name="whole_layer",
        out_shape=pltpu.VMEM((rows, D), bf),
        in_specs=[hbm, hbm, hbm, vmem, vmem, vmem, hbm, hbm],
        out_specs=vmem,
        scratch_shapes=[
            pltpu.VMEM((2 * rows, D // 2), bf),
            pltpu.VMEM((2 * rows, D // 2), bf),
            pltpu.VMEM((8, 6 * rows), jnp.float32),
            pltpu.VMEM((6 * rows, D // 2), bf),
            pltpu.VMEM((6 * rows, D // 2), bf),
            pltpu.VMEM((planes, 2 * rows, D // 2), bf),
            pltpu.VMEM((n, 2 * cap, D // 2), bf),
            pltpu.VMEM((planes, 2 * cap, D // 2), bf),
            pltpu.VMEM((planes, 4 * cap, 2 * rows), bf),
            pltpu.VMEM((planes, 2 * cap, rows), bf),
            pltpu.VMEM((n, 16, rows), jnp.float32),
            pltpu.VMEM((n, 16, rows), jnp.float32),
            pltpu.VMEM((SPLIT * cap, D), bf),
            pltpu.VMEM((D, width), bf),
            pltpu.VMEM((width, D), bf),
            pltpu.VMEM((SPLIT * cap, width), bf),
            pltpu.VMEM((n * cap, D), bf),
            pltpu.VMEM((planes * 2 * cap, D), bf),
            pltpu.VMEM((planes * cap, D), bf),
            pltpu.VMEM((planes, 2 * cap, D), bf),
            pltpu.VMEM((planes, rows, D), bf),
            pltpu.VMEM((planes, rows, D), bf),
            dma((5,)),
            dma((5,)),
            dma((6, chunks)),
            dma((2,)),
            dma((2,)),
            dma((planes, 5)),
            dma((planes, chunks)),
            dma((planes, chunks)),
            dma((n,)),
            dma((2,)),
            dma((planes, 4)),
            dma((planes, backs)),
            dma((planes, backs)),
            dma((planes, backs)),
            dma((planes, backs)),
        ],
        compiler_params=pltpu.CompilerParams(
            collective_id=1, has_side_effects=True, vmem_limit_bytes=VMEM_LIMIT
        ),
    )(queries, key_rows, values, modulation, routes.T, gate_fixed.T, expert_in, expert_out)


def slot_table(flat, experts_count):
    onehot = (flat[:, None] == jnp.arange(experts_count, dtype=jnp.int32)[None, :]).astype(
        jnp.int32
    )
    before = jnp.cumsum(onehot, axis=0) - onehot
    return jnp.sum(before * onehot, axis=1)


def expert_apply(rows, first_weight, second_weight):
    hidden = jax.nn.gelu(
        jnp.dot(rows, first_weight, preferred_element_type=jnp.float32), approximate=True
    ).astype(jnp.bfloat16)
    return jnp.dot(hidden, second_weight, preferred_element_type=jnp.float32).astype(jnp.bfloat16)


def experts_sparse(normed, attended, modulation, expert_in, expert_out, routes, gate_fixed):
    devices = lax.axis_size("tile")
    rows_dev = normed.shape[0]
    experts_count = devices // SPLIT
    capacity = 3 * rows_dev // experts_count
    flat = routes.reshape(-1)
    slots = slot_table(flat, experts_count)
    target = flat * capacity + slots
    chooser = (
        target[None, :] == jnp.arange(experts_count * capacity, dtype=jnp.int32)[:, None]
    ).astype(jnp.bfloat16)
    chooser = chooser.reshape(experts_count * capacity, rows_dev, 2).sum(axis=2)
    buffer = jnp.dot(chooser, normed, preferred_element_type=jnp.float32).astype(jnp.bfloat16)
    copies = jnp.broadcast_to(
        buffer.reshape(experts_count, 1, capacity, D), (experts_count, SPLIT, capacity, D)
    ).reshape(devices, capacity, D)
    received = lax.all_to_all(copies, "tile", split_axis=0, concat_axis=0, tiled=True)
    sources = received.shape[0]
    count = received.shape[1]
    partial_value = expert_apply(received.reshape(sources * count, D), expert_in, expert_out)
    returned = lax.all_to_all(
        partial_value.reshape(sources, count, D), "tile", split_axis=0, concat_axis=0, tiled=True
    )
    summed = jnp.sum(
        returned.reshape(experts_count, SPLIT, capacity, D).astype(jnp.float32), axis=1
    )
    expert_rows = summed.astype(jnp.bfloat16).reshape(experts_count * capacity, D)
    picked = jnp.take(expert_rows, target, axis=0).reshape(rows_dev, 2, D)
    gate_scale = gate_fixed.astype(jnp.float32) / 1024.0
    mixture = jnp.sum(picked.astype(jnp.float32) * gate_scale[:, :, None], axis=1)
    return (attended.astype(jnp.float32) + modulation[2] * mixture).astype(jnp.bfloat16)


def shards(queries, key_rows, values, modulation, expert_in, expert_out, routes, gate_fixed):
    n = lax.axis_size("tile")
    cap = 3 * queries.shape[0] // (n // SPLIT)
    if n == 2 * TILE_COLS and cap % 16 == 0 and kernel_bytes(n, queries.shape[0], cap, expert_in.shape[1]) < VMEM_LIMIT * 7 // 8:
        return layer(queries, key_rows, values, modulation, expert_in, expert_out, routes, gate_fixed)
    attended, normed = attention(queries, key_rows, values, modulation)
    return experts_sparse(normed, attended, modulation, expert_in, expert_out, routes, gate_fixed)


def solution(mesh):
    placed = (
        P(("groups", "tile"), None),
        P(("groups", "tile"), None),
        P(("groups", "tile"), None),
        P("groups", None),
        P(None, "tile"),
        P("tile", None),
        P(("groups", "tile"), None),
        P(("groups", "tile"), None),
    )
    return jax.shard_map(
        shards, mesh=mesh, in_specs=placed, out_specs=P(("groups", "tile"), None), check_vma=False
    )
```

```python
import functools
import math

import jax
import jax.numpy as jnp
from jax import lax
from jax.experimental import pallas as pl
from jax.experimental.pallas import tpu as pltpu
from jax.sharding import PartitionSpec as P

HEAD_DIM = 128
D = 4096
SPLIT = 4
TILE_COLS = 8

EPSILON = 1e-06
MASKED = -1e30
MESH = pl.DeviceIdType.MESH
VMEM_LIMIT = 60 * 1024 * 1024
CHUNKS = 8
AHEAD = 2
ASIDE = 2
BEHIND = 1
HOP = 2
PASS = 4
DRAIN = (2, 8)
EARLY = 2
BACK_CHUNKS = 4
BACK_LAGS = (1, 4, 7)


def when(cond, body):
    if cond is True:
        body()
    else:
        pl.when(cond)(body)


def both(a, b):
    if a is True:
        return b
    if b is True:
        return a
    return jnp.logical_and(a, b)


def remote(src, dst, send_sem, recv_sem, target):
    return pltpu.make_async_remote_copy(
        src_ref=src,
        dst_ref=dst,
        send_sem=send_sem,
        recv_sem=recv_sem,
        device_id={"tile": target},
        device_id_type=MESH,
    )


def halo_levels(n):
    grid_rows = n // TILE_COLS
    if grid_rows < 2:
        return 1
    return 2 if grid_rows == 2 else 3


def attention_kernel(
    n, rows, q_ref, k_ref, v_ref, mod_ref, att_ref, norm_ref, keys, vals, send_sem, recv_sem, own_sem,
):
    me = lax.axis_index("tile")
    grid_rows = n // TILE_COLS
    tile = lax.rem(me + TILE_COLS // 2, n)
    row = lax.div(tile, TILE_COLS)
    col = lax.rem(tile, TILE_COLS)
    if grid_rows < 2:
        verticals = []
    elif grid_rows == 2:
        verticals = [(1, TILE_COLS, True, 1)]
    else:
        verticals = [(1, n - TILE_COLS, row > 0, 2), (2, TILE_COLS, row < grid_rows - 1, 1)]
    sides = [(-1, col > 0), (1, col < TILE_COLS - 1)]
    here = {level: exists for level, _, exists, _ in verticals}
    here[0] = True

    def slot(level, side):
        return level * 3 + 1 + side

    def place(buf, s):
        return buf.at[pl.ds(s * rows, rows), :]

    def over(offset):
        return lax.rem(me + offset + n, n)

    half = rows // 2
    middle = TILE_COLS // 2
    crossing = {side: col == (middle if side < 0 else middle - 1) for side, _ in sides}
    two = grid_rows == 2

    def part_of(buf, s, h):
        return buf.at[pl.ds(pl.multiple_of(s * rows + h * half, half), half), :]

    own = [
        pltpu.make_async_copy(src, place(buf, slot(0, 0)), own_sem.at[i])
        for i, (src, buf) in enumerate(((k_ref, keys), (v_ref, vals)))
    ]
    for copy in own:
        copy.start()

    def beside(side):
        if not two:
            return over(side)
        return jnp.where(crossing[side], over(side + TILE_COLS), over(side))

    def level_there(level, side):
        return jnp.where(crossing[side], 1 - level, level) if two else level

    barrier = pltpu.get_barrier_semaphore()
    partners = [(over(offset), exists) for _, offset, exists, _ in verticals]
    partners += [(beside(side), exists) for side, exists in sides]
    for target, exists in partners:

        def greet(target=target):
            pl.semaphore_signal(barrier, inc=1, device_id={"tile": target}, device_id_type=MESH)

        when(exists, greet)
    expected = sum(1 if exists is True else jnp.where(exists, 1, 0) for _, exists in partners)
    pl.semaphore_wait(barrier, expected)

    sends = []
    pieces = [(i, h) for i in (0, 1) for h in (0, 1)]
    bufs = (keys, vals)

    def push(i, h, src, there, target, exists):
        copy = remote(
            src,
            part_of(bufs[i], there, h),
            send_sem.at[len(sends)],
            recv_sem.at[there, i * 2 + h],
            target,
        )
        when(exists, copy.start)
        sends.append((copy, exists))

    def arrived(s, exists, i, h):
        ref = part_of(bufs[i], s, h)
        when(exists, remote(ref, ref, send_sem.at[0], recv_sem.at[s, i * 2 + h], me).wait_recv)

    def own_part(i, h):
        return (k_ref, v_ref)[i].at[pl.ds(h * half, half), :]

    for i, h in pieces:
        for level, offset, exists, there in verticals:
            push(i, h, own_part(i, h), slot(there, 0), over(offset), exists)
    for i, h in pieces:
        for side, exists in sides:
            push(i, h, own_part(i, h), slot(level_there(0, side), -side), beside(side), exists)
    for s in range(3 * (1 + len(verticals))):
        level, side = s // 3, s % 3 - 1
        exists = here[level]
        for other, side_exists in sides:
            if other == side:
                exists = both(exists, side_exists)
        if exists is True:
            continue

        def clear(s=s):
            for buf in (keys, vals):
                buf[pl.ds(s * rows, rows), :] = jnp.zeros((rows, D), buf.dtype)

        pl.when(jnp.logical_not(exists))(clear)
    for i, h in pieces:
        for level, offset, exists, there in verticals:
            arrived(slot(level, 0), exists, i, h)
            for side, side_exists in sides:
                push(
                    i,
                    h,
                    part_of(bufs[i], slot(level, 0), h),
                    slot(level_there(level, side), -side),
                    beside(side),
                    both(exists, side_exists),
                )
    for copy in own:
        copy.wait()
    for i, h in pieces:
        for level, exists in sorted(here.items(), key=lambda item: item[0]):
            for side, side_exists in sides:
                arrived(slot(level, side), both(exists, side_exists), i, h)

    span = 3 * (1 + len(verticals)) * rows
    where = lax.broadcasted_iota(jnp.int32, (rows, span), 1)
    bias = jnp.zeros((rows, span), jnp.float32)
    for s in range(span // rows):
        level, side = s // 3, s % 3 - 1
        exists = here[level]
        for other, side_exists in sides:
            if other == side:
                exists = both(exists, side_exists)
        if exists is True:
            continue
        penalty = jnp.where(exists, 0.0, MASKED)
        bias = jnp.where((where >= s * rows) & (where < (s + 1) * rows), penalty, bias)
    scale = 1.0 / math.sqrt(HEAD_DIM)
    together = 8

    def heads(step, carry):
        for extra in range(together):
            at = pl.ds(pl.multiple_of((step * together + extra) * HEAD_DIM, HEAD_DIM), HEAD_DIM)
            scores = lax.dot_general(
                q_ref[:, at], keys[:, at], (((1,), (1,)), ((), ())), preferred_element_type=jnp.float32
            )
            scores = scores * scale + bias
            raised = jnp.exp(scores - jnp.max(scores, axis=-1, keepdims=True))
            probs = (raised * (1.0 / jnp.sum(raised, axis=-1, keepdims=True))).astype(jnp.bfloat16)
            att_ref[:, at] = jnp.dot(probs, vals[:, at], preferred_element_type=jnp.float32).astype(
                att_ref.dtype
            )
        return carry

    lax.fori_loop(0, D // HEAD_DIM // together, heads, 0)

    def normalise(step, carry):
        at = pl.ds(pl.multiple_of(step * 16, 16), 16)
        wide = att_ref[at, :].astype(jnp.float32)
        wide = wide - jnp.mean(wide, axis=-1, keepdims=True)
        spread = jnp.mean(wide * wide, axis=-1, keepdims=True)
        normed = wide * lax.rsqrt(spread + EPSILON)
        norm_ref[at, :] = (normed * (1.0 + mod_ref[1:2, :]) + mod_ref[0:1, :]).astype(norm_ref.dtype)
        return carry

    lax.fori_loop(0, rows // 16, normalise, 0)
    for copy, exists in sends:
        when(exists, copy.wait_send)


def attention(queries, key_rows, values, modulation):
    n = lax.axis_size("tile")
    rows = queries.shape[0]
    levels = halo_levels(n)
    slots = 3 * levels
    vmem = pl.BlockSpec(memory_space=pltpu.VMEM)
    hbm = pl.BlockSpec(memory_space=pl.ANY)
    return pl.pallas_call(
        functools.partial(attention_kernel, n, rows),
        name="halo_attention",
        out_shape=(
            jax.ShapeDtypeStruct((rows, D), jnp.bfloat16),
            jax.ShapeDtypeStruct((rows, D), jnp.bfloat16),
        ),
        in_specs=[vmem, hbm, hbm, vmem],
        out_specs=(vmem, vmem),
        scratch_shapes=[
            pltpu.VMEM((slots * rows, D), jnp.bfloat16),
            pltpu.VMEM((slots * rows, D), jnp.bfloat16),
            pltpu.SemaphoreType.DMA((4 * (2 + 3 * (levels - 1)),)),
            pltpu.SemaphoreType.DMA((slots, 4)),
            pltpu.SemaphoreType.DMA((2,)),
        ],
        compiler_params=pltpu.CompilerParams(
            collective_id=0, has_side_effects=True, vmem_limit_bytes=VMEM_LIMIT
        ),
    )(queries, key_rows, values, modulation)


def device(plane, yy, cc):
    return plane * SPLIT + yy * 2 + cc


def layer_kernel(
    n, rows, cap, chunks, backs, q_ref, k_ref, v_ref, mod_ref, routes_ref, gates_ref, first_ref, second_ref,
    out_ref, att, asked, bias, keys, vals, line, tokens, stage, chooser, spreader, tables, stats, normed,
    first, second, hidden, part, r1, r2, pair, acc_in, acc_out,
    own_sem, kv_send, kv_recv, table_send, table_recv, out_send, line_recv, beside_recv, twin_recv,
    rest_sem, back_send, s1_recv, s2_recv, pair_recv, acc_recv,
):
    planes = n // SPLIT
    width = first.shape[1]
    half = D // 2
    wide = half // chunks
    me = lax.axis_index("tile")
    p = lax.div(me, SPLIT)
    y = lax.div(lax.rem(me, SPLIT), 2)
    c = lax.rem(me, 2)
    beside = device(p, 1 - y, c)
    twin = device(p, y, 1 - c)
    low_half = p < planes // 2
    toward = jnp.where(low_half, 1, -1)
    inner = p + toward
    outer = p - toward
    at_end = jnp.logical_or(p == 0, p == planes - 1)
    middle = jnp.logical_not(at_end)
    outer_expert = jnp.where(low_half, 0, planes - 1)
    inner_device = device(inner, y, c)
    outer_device = device(jnp.where(at_end, p, outer), y, c)

    tile = lax.rem(me + TILE_COLS // 2, n)
    column = lax.rem(tile, TILE_COLS)
    partner = lax.rem(me + TILE_COLS, n)
    sides = [(-1, column > 0), (1, column < TILE_COLS - 1)]
    half_way = TILE_COLS // 2
    crossing = {-1: column == half_way, 1: column == half_way - 1}

    def part_of_plane(plane):
        return jnp.where(plane < planes // 2, half, 0)

    mine_from = part_of_plane(p)
    other_from = half - mine_from
    partner_plane = lax.rem(p + planes // 2, planes)

    def cols(j, base=0):
        return pl.ds(pl.multiple_of(base + j * wide, wide), wide)

    def halves(base):
        return pl.ds(pl.multiple_of(base, half), half)

    def lines(buf, s):
        return buf.at[pl.ds(pl.multiple_of(s * rows, rows), rows), :]

    loads = [
        pltpu.make_async_copy(q_ref.at[:, halves(mine_from)], lines(asked, 0), own_sem.at[0]),
        pltpu.make_async_copy(k_ref.at[:, halves(mine_from)], lines(keys, 1), own_sem.at[1]),
        pltpu.make_async_copy(v_ref.at[:, halves(mine_from)], lines(vals, 1), own_sem.at[2]),
        pltpu.make_async_copy(first_ref, first, own_sem.at[3]),
        pltpu.make_async_copy(second_ref, second, own_sem.at[4]),
    ]

    barrier = pltpu.get_barrier_semaphore()
    others = [lax.rem(me + step, n) for step in range(1, n)]
    for target in others:
        pl.semaphore_signal(barrier, inc=1, device_id={"tile": target}, device_id_type=MESH)

    def beside_tile(side):
        return lax.rem(me + side + jnp.where(crossing[side], TILE_COLS, 0) + n, n)

    def slot_there(level, side):
        return jnp.where(crossing[side], 1 - level, level) * 3 + 1 - side

    bufs = (keys, vals, asked)
    given = (k_ref, v_ref, q_ref)

    def place(i, s, j):
        return bufs[i].at[pl.ds(pl.multiple_of(s * rows, rows), rows), cols(j)]

    def over_vertical(i, j):
        return remote(
            given[i].at[:, cols(j, other_from)],
            place(i, 4 if i < 2 else 1, j),
            kv_send.at[0],
            kv_recv.at[4, j],
            partner,
        )

    def over_side(level, index, i, j):
        side = sides[index][0]
        there = slot_there(level, side)
        source = given[i].at[:, cols(j, mine_from)] if level == 0 else place(i, 4, j)
        return remote(
            source,
            place(i, there, j),
            kv_send.at[1 + level * 2 + index],
            kv_recv.at[there, j],
            beside_tile(side),
        )

    def landed(ref, sem):
        remote(ref, ref, own_sem.at[0], sem, me).wait_recv()

    def send_own(j):
        for i in range(3):
            over_vertical(i, j).start()

    def send_side(j):
        for i in (0, 1):
            for index, (_, exists) in enumerate(sides):
                when(exists, over_side(0, index, i, j).start)

    def bytes_of(count, at):
        return keys.at[pl.ds(0, count * rows), at]

    def send_vertical(j):
        landed(bytes_of(3, cols(j)), kv_recv.at[4, j])
        for i in (0, 1):
            for index, (_, exists) in enumerate(sides):
                when(exists, over_side(1, index, i, j).start)

    pl.semaphore_wait(barrier, n - 1)
    send_own(0)
    send_side(0)
    for load in loads[:3]:
        load.start()

    expert = lax.broadcasted_iota(jnp.int32, (8, rows), 0)
    named = [routes_ref[k : k + 1, :] == expert for k in (0, 1)]
    member = jnp.logical_or(named[0], named[1])
    upto = (
        lax.broadcasted_iota(jnp.int32, (rows, rows), 0) <= lax.broadcasted_iota(jnp.int32, (rows, rows), 1)
    ).astype(jnp.float32).astype(jnp.bfloat16)
    count = jnp.dot(
        member.astype(jnp.float32).astype(jnp.bfloat16), upto, preferred_element_type=jnp.float32
    )
    gate = sum(
        jnp.where(named[k], gates_ref[k : k + 1, :].astype(jnp.float32), 0.0) for k in (0, 1)
    )
    tables[me, 0:8, :] = jnp.where(member, count - 1.0, -1.0)
    stats[me, 8:16, :] = jnp.where(member, count - 1.0, -1.0)
    tables[me, 8:16, :] = gate / 1024.0

    column_planes = [lax.rem(p + step, planes) for step in range(1, planes)]

    def tell_column(step):
        there = device(column_planes[step], y, c)
        return remote(tables.at[me], tables.at[me], table_send.at[0], table_recv.at[0], there)

    for step in range(planes - 1):
        tell_column(step).start()
    for j in range(1, max(AHEAD, ASIDE)):
        if j < min(AHEAD, chunks):
            send_own(j)
        if j < min(ASIDE, chunks):
            send_side(j)

    span = 6 * rows
    where = lax.broadcasted_iota(jnp.int32, (8, span), 1)
    penalty = jnp.zeros((8, span), jnp.float32)
    for s in range(6):
        for side, exists in sides:
            if side != s % 3 - 1:
                continue
            here = (where >= s * rows) & (where < (s + 1) * rows)
            penalty = jnp.where(here, jnp.where(exists, 0.0, MASKED), penalty)

            def clear(s=s):
                for buf in (keys, vals):
                    buf[s * rows : (s + 1) * rows, :] = jnp.zeros((rows, half), buf.dtype)

            pl.when(jnp.logical_not(exists))(clear)
    bias[...] = penalty
    chooser[...] = jnp.zeros(chooser.shape, chooser.dtype)

    def tell_all():
        return [
            remote(stats.at[me], stats.at[me], table_send.at[1], table_recv.at[1], target)
            for target in others
        ]

    for load in loads[:3]:
        load.wait()
    for load in loads[3:]:
        load.start()

    slot_line = lax.broadcasted_iota(jnp.int32, (cap, rows), 0).astype(jnp.float32)

    def chosen(tile_there, e):
        return tables[tile_there, pl.ds(e, 1), :] == slot_line

    def picked_column(which, row):
        return jnp.sum(jnp.where(which, row, 0.0), axis=1, keepdims=True)

    def choose():
        landed(tables.at[pl.ds(0, planes - 1)], table_recv.at[0])
        for plane in range(planes):
            for place_in, e in ((0, p), (1, outer_expert)):
                found = chosen(device(plane, y, c), e).astype(jnp.float32).astype(jnp.bfloat16)
                at = place_in * 2 * cap
                spreader[plane, place_in * cap : (place_in + 1) * cap, :] = found
                chooser[plane, at : at + cap, :rows] = found
                chooser[(plane + planes // 2) % planes, at + cap : at + 2 * cap, rows:] = found

    scale = 1.0 / math.sqrt(HEAD_DIM)

    def attend(j):
        for level in (0, 1):
            for side, exists in sides:
                s = level * 3 + 1 + side
                when(exists, functools.partial(landed, bytes_of(2, cols(j)), kv_recv.at[s, j]))
        for extra in range(wide // HEAD_DIM):
            at = pl.ds(pl.multiple_of(j * wide + extra * HEAD_DIM, HEAD_DIM), HEAD_DIM)
            scores = lax.dot_general(
                asked[:, at], keys[:, at], (((1,), (1,)), ((), ())), preferred_element_type=jnp.float32
            )
            scores = scores * scale + bias[0:1, :]
            raised = jnp.exp(scores - jnp.max(scores, axis=-1, keepdims=True))
            probs = (raised * (1.0 / jnp.sum(raised, axis=-1, keepdims=True))).astype(jnp.bfloat16)
            att[:, at] = jnp.dot(probs, vals[:, at], preferred_element_type=jnp.float32).astype(att.dtype)

    def raw_copy(k, src, j):
        source = att.at[:, cols(j)] if k == 0 else line.at[src, :, cols(j)]
        return remote(source, line.at[src, :, cols(j)], out_send.at[k, 0], line_recv.at[src, j], inner_device)

    def outer_copy(k, src, j):
        there = device(src, y, c)
        return remote(
            stage.at[src, :, cols(j)],
            tokens.at[there, :, cols(j)],
            out_send.at[k, 1],
            line_recv.at[src, j],
            outer_device,
        )

    def rest_copy(src, j):
        ref = line.at[src, pl.ds(rows, rows), cols(j)]
        return remote(ref, ref, rest_sem.at[0], rest_sem.at[1], outer_device)

    def plane_copy(k, src, j, index):
        ref = tokens.at[device(src, y, c), :, cols(j)]
        recv = beside_recv.at[src, j] if index == 0 else twin_recv.at[device(src, y, c)]
        return remote(ref, ref, out_send.at[k, 2 + index], recv, (beside, twin)[index])

    def twin_copy(k, src, j):
        there = device(src, 1 - y, c)
        ref = tokens.at[there, :, cols(j)]
        return remote(ref, ref, out_send.at[k, 4], twin_recv.at[there], twin)

    far = jnp.where(at_end, p + 3 * toward, p + 2 * toward)
    second_plane = jnp.where(at_end, p + 2 * toward, outer)
    sources = [
        (p, BEHIND, True, middle),
        (inner, BEHIND + HOP, False, middle),
        (second_plane, BEHIND + HOP * jnp.where(at_end, 2, 1), middle, False),
        (far, BEHIND + HOP * jnp.where(at_end, 3, 2), False, middle),
    ]

    def relay(k, j):
        src, behind, whole, out = sources[k]
        jj = j - behind

        def go():
            there = device(src, y, c)
            if k > 0:
                pl.when(at_end)(
                    lambda: landed(tokens.at[there, :, cols(jj)], line_recv.at[src, jj])
                )
                pl.when(middle)(lambda: landed(line.at[src, :, cols(jj)], line_recv.at[src, jj]))
            if whole is not False:
                when(whole, raw_copy(k, src, jj).start)
            if k == 1:
                pl.when(middle)(rest_copy(src, jj).start)

            def pick():
                rows_here = att[:, cols(jj)] if k == 0 else line[src, :, cols(jj)]
                picked = jnp.dot(chooser[src], rows_here, preferred_element_type=jnp.float32).astype(
                    tokens.dtype
                )
                tokens[there, :, cols(jj)] = picked[: 2 * cap]
                stage[src, :, cols(jj)] = picked[2 * cap :]

            when(True if k == 0 else middle, pick)
            if out is not False:
                when(out, outer_copy(k, src, jj).start)
            for index in (0, 1):
                plane_copy(k, src, jj, index).start()

        pl.when(jnp.logical_and(jj >= 0, jj < chunks))(go)

    def pass_on(k, j):
        src, behind, _, _ = sources[k]
        jj = j - behind - PASS

        def go():
            there = device(src, 1 - y, c)
            landed(tokens.at[there, :, cols(jj)], beside_recv.at[src, jj])
            twin_copy(k, src, jj).start()

        pl.when(jnp.logical_and(jj >= 0, jj < chunks))(go)

    def move(j):
        for k in range(planes):
            relay(k, j)
        for k in range(planes):
            pass_on(k, j)

    def stream(j, carry):
        pl.when(j < chunks)(lambda: send_vertical(j))

        pl.when(j + AHEAD < chunks)(lambda: send_own(j + AHEAD))
        pl.when(j + ASIDE < chunks)(lambda: send_side(j + ASIDE))
        pl.when(j == BEHIND)(choose)
        pl.when(j >= BEHIND)(lambda: attend(j - BEHIND))
        move(j)
        return carry

    lax.fori_loop(0, chunks + BEHIND, stream, 0)

    def drain(j, carry):
        move(j)
        return carry

    lax.fori_loop(chunks + BEHIND, chunks + BEHIND + DRAIN[0], drain, 0)

    token = lax.broadcasted_iota(jnp.int32, (16, rows), 1)
    line_of = lax.broadcasted_iota(jnp.int32, (16, rows), 0)
    row_number = lax.broadcasted_iota(jnp.int32, (8, rows), 0)
    found = jnp.zeros((8, rows), jnp.float32)
    for step in range(2 * rows // 16):
        some = att[step * 16 : (step + 1) * 16, :].astype(jnp.float32)
        mean = jnp.mean(some, axis=-1, keepdims=True)
        some = some - mean
        spread = jnp.mean(some * some, axis=-1, keepdims=True)
        which, at = divmod(step * 16, rows)
        for kind, value in enumerate((mean, spread)):
            row = jnp.sum(jnp.where(token == line_of + at, value, 0.0), axis=0, keepdims=True)
            found = found + jnp.where(row_number == 2 * which + kind, row, 0.0)
    stats[me, 0:8, :] = found
    for copy in tell_all():
        copy.start()

    lax.fori_loop(chunks + BEHIND + DRAIN[0], chunks + BEHIND + DRAIN[1], drain, 0)
    landed(stats.at[pl.ds(0, n - 1)], table_recv.at[1])
    for load in loads[3:]:
        load.wait()

    order = [
        jnp.where(at_end, p + 2 * toward, inner),
        jnp.where(at_end, p + 3 * toward, p + 2 * toward),
        jnp.where(at_end, inner, outer),
        p,
    ]
    def arrive(plane):
        for source in (plane, lax.rem(plane + planes // 2, planes)):
            for yy in (0, 1):
                there = device(source, yy, 1 - c)
                landed(tokens.at[there], twin_recv.at[there])

    group = SPLIT * cap
    chunk = 512
    span_back = D // backs

    def home_of(i):
        return jnp.where(i == 0, order[0], jnp.where(i == 1, order[1], jnp.where(i == 2, order[2], order[3])))

    def block(buf, index, count, j):
        return buf.at[pl.ds(pl.multiple_of(index * cap, 16), count * cap), back_cols(j)]

    def back_cols(j):
        return pl.ds(pl.multiple_of(j * span_back, span_back), span_back)

    def start_group(plane):
        def normalise(t, carry):
            yy, cc = lax.rem(t, 2), lax.div(t, 2)
            there = device(plane, yy, cc)
            across = lax.rem(there + TILE_COLS, n)
            mean_here, mean_there = stats[there, 0:1, :], stats[across, 2:3, :]
            apart = 0.5 * (mean_here - mean_there)
            spread = 0.5 * (stats[there, 1:2, :] + stats[across, 3:4, :]) + apart * apart
            which = stats[there, pl.ds(8 + p, 1), :] == slot_line
            mean = picked_column(which, 0.5 * (mean_here + mean_there))
            rate = picked_column(which, lax.rsqrt(spread + EPSILON))
            at = pl.ds(pl.multiple_of(t * cap, 16), cap)
            base = part_of_plane(plane)
            for source, lower, start in ((there, 0, base), (across, cap, half - base)):
                for step in range(half // chunk):
                    some = slice(step * chunk, (step + 1) * chunk)
                    to = pl.ds(pl.multiple_of(start + step * chunk, chunk), chunk)
                    value = (tokens[source, lower : lower + cap, some].astype(jnp.float32) - mean) * rate
                    normed[at, to] = (value * (1.0 + mod_ref[1:2, to]) + mod_ref[0:1, to]).astype(
                        normed.dtype
                    )
            return carry

        lax.fori_loop(0, SPLIT, normalise, 0)
        raw = jnp.dot(normed[...], first[...], preferred_element_type=jnp.float32)
        hidden[...] = jax.nn.gelu(raw, approximate=True).astype(hidden.dtype)

    def to_twin(plane, j):
        return remote(
            block(part, plane * SPLIT + (1 - c) * 2, 2, j),
            block(r1, plane * 2, 2, j),
            back_send.at[plane, 0],
            s1_recv.at[plane, j],
            twin,
        )

    def to_beside(plane, j):
        return remote(
            block(part, plane * SPLIT + c * 2 + 1 - y, 1, j),
            block(r2, plane, 1, j),
            back_send.at[plane, 1],
            s2_recv.at[plane, j],
            beside,
        )

    def slots_home(plane, j):
        return remote(
            pair.at[plane, pl.ds(0, cap), back_cols(j)],
            pair.at[plane, pl.ds(cap, cap), back_cols(j)],
            back_send.at[plane, 2],
            pair_recv.at[plane, j],
            inner_device,
        )

    def rows_home(plane, j):
        return remote(
            acc_out.at[plane, :, back_cols(j)],
            acc_in.at[plane, :, back_cols(j)],
            back_send.at[plane, 3],
            acc_recv.at[plane, j],
            device(jnp.where(plane == outer, outer, inner), y, c),
        )

    def produce(i, j):
        plane = home_of(i)
        pl.when(jnp.logical_and(j == 0, i < 2))(lambda: arrive(plane))
        pl.when(j == 0)(lambda: start_group(plane))
        raw = jnp.dot(hidden[...], second[:, back_cols(j)], preferred_element_type=jnp.float32)
        mine = pl.ds(pl.multiple_of(plane * group, 16), group)
        part[mine, back_cols(j)] = raw.astype(part.dtype)
        to_twin(plane, j).start()

    def fold_twin(i, j):
        plane = home_of(i)
        landed(block(r1, plane * 2, 2, j), s1_recv.at[plane, j])
        for yy in (1 - y, y):
            at = pl.ds(pl.multiple_of((plane * SPLIT + c * 2 + yy) * cap, 16), cap)
            there = pl.ds(pl.multiple_of((plane * 2 + yy) * cap, 16), cap)
            total = part[at, back_cols(j)].astype(jnp.float32) + r1[there, back_cols(j)].astype(jnp.float32)
            part[at, back_cols(j)] = total.astype(part.dtype)
            if yy is not y:
                to_beside(plane, j).start()

    def fold_beside(i, j):
        plane = home_of(i)
        there = device(plane, y, c)
        landed(block(r2, plane, 1, j), s2_recv.at[plane, j])
        weight = picked_column(chosen(there, p), tables[there, pl.ds(8 + p, 1), :])
        ours = pl.ds(pl.multiple_of((plane * SPLIT + c * 2 + y) * cap, 16), cap)
        theirs = pl.ds(pl.multiple_of(plane * cap, 16), cap)
        total = part[ours, back_cols(j)].astype(jnp.float32) + r2[theirs, back_cols(j)].astype(jnp.float32)
        pair[plane, :cap, back_cols(j)] = (total * weight).astype(pair.dtype)
        pl.when(jnp.logical_and(at_end, plane != p))(slots_home(plane, j).start)

    def spread_out(plane, both, at):
        amount = 2 * cap if both else cap
        return lax.dot_general(
            spreader[plane, :amount, :],
            pair[plane, :amount, at],
            (((0,), (0,)), ((), ())),
            preferred_element_type=jnp.float32,
        )

    def fold_home(i, j):
        plane = home_of(i)
        at = back_cols(j)

        def fold(both, extra, last):
            if both:
                landed(pair.at[plane, pl.ds(cap, cap), at], pair_recv.at[plane, j])
            if extra:
                landed(acc_in.at[plane, :, at], acc_recv.at[plane, j])
            total = spread_out(plane, both, at)
            if extra:
                total = total + acc_in[plane, :, at].astype(jnp.float32)
            if last:
                out_ref[:, at] = (mod_ref[2:3, at] * total + out_ref[:, at].astype(jnp.float32)).astype(
                    out_ref.dtype
                )
            else:
                acc_out[plane, :, at] = total.astype(acc_out.dtype)
                rows_home(plane, j).start()

        pl.when(jnp.logical_and(at_end, i == 3))(lambda: fold(False, True, True))
        pl.when(jnp.logical_and(middle, i == 3))(lambda: fold(True, True, True))
        pl.when(jnp.logical_and(middle, i == 2))(lambda: fold(False, True, False))
        pl.when(jnp.logical_and(middle, i < 2))(lambda: fold(True, False, False))

    units = planes * backs

    def begin_result():
        pl.when(at_end)(lambda: landed(line.at[partner_plane, pl.ds(rows, rows), :], rest_sem.at[1]))
        out_ref[:, halves(mine_from)] = att[:rows, :]
        out_ref[:, halves(other_from)] = line[partner_plane, rows:, :]

    def give_back(u, carry):
        pl.when(u == 2 * backs + 2)(begin_result)
        for behind, act in ((0, produce), (BACK_LAGS[0], fold_twin), (BACK_LAGS[1], fold_beside), (BACK_LAGS[2], fold_home)):
            at = u - behind
            i, j = lax.div(at, backs), lax.rem(at, backs)
            pl.when(jnp.logical_and(at >= 0, at < units))(functools.partial(act, i, j))
        return carry

    lax.fori_loop(0, EARLY, give_back, 0)
    lax.fori_loop(chunks + BEHIND + DRAIN[1], chunks + BEHIND + 3 * HOP + PASS, drain, 0)
    lax.fori_loop(EARLY, units + BACK_LAGS[2], give_back, 0)

    def gone(ref, sem):
        remote(ref, ref, sem, own_sem.at[0], twin).wait_send()

    every = pl.ds(0, half)
    gone(bytes_of(3, every), kv_send.at[0])
    for level in (0, 1):
        for index, (_, exists) in enumerate(sides):
            when(exists, functools.partial(gone, bytes_of(2, every), kv_send.at[1 + level * 2 + index]))
    for k, (_, _, whole, out) in enumerate(sources):
        if whole is not False:
            when(whole, functools.partial(gone, line.at[0], out_send.at[k, 0]))
        if out is not False:
            when(out, functools.partial(gone, stage.at[0], out_send.at[k, 1]))
        for index in range(3):
            gone(tokens.at[0], out_send.at[k, 2 + index])
    pl.when(middle)(lambda: gone(line.at[0, pl.ds(0, rows), :], rest_sem.at[0]))
    gone(tables.at[pl.ds(0, planes - 1)], table_send.at[0])
    gone(stats.at[pl.ds(0, n - 1)], table_send.at[1])
    for plane in range(planes):
        gone(r1.at[pl.ds(0, 2 * cap), :], back_send.at[plane, 0])
        gone(r1.at[pl.ds(0, cap), :], back_send.at[plane, 1])
        away = p != plane
        pl.when(jnp.logical_and(at_end, away))(
            functools.partial(gone, r1.at[pl.ds(0, cap), :], back_send.at[plane, 2])
        )
        pl.when(jnp.logical_and(middle, away))(functools.partial(gone, acc_in.at[0], back_send.at[plane, 3]))


def kernel_bytes(n, rows, cap, width):
    planes = n // SPLIT
    lines = 2 * 6 * rows + 2 * n * cap + planes * (6 * cap + 3 * rows) + SPLIT * cap + 3 * rows
    return 2 * (lines * D + 2 * width * D)


def layer(queries, key_rows, values, modulation, expert_in, expert_out, routes, gate_fixed):
    n = lax.axis_size("tile")
    rows = queries.shape[0]
    width = expert_in.shape[1]
    planes = n // SPLIT
    cap = 3 * rows // planes
    chunks, backs = CHUNKS, BACK_CHUNKS
    vmem = pl.BlockSpec(memory_space=pltpu.VMEM)
    hbm = pl.BlockSpec(memory_space=pl.ANY)
    dma = pltpu.SemaphoreType.DMA
    bf = jnp.bfloat16
    return pl.pallas_call(
        functools.partial(layer_kernel, n, rows, cap, CHUNKS, BACK_CHUNKS),
        name="whole_layer",
        out_shape=pltpu.VMEM((rows, D), bf),
        in_specs=[hbm, hbm, hbm, vmem, vmem, vmem, hbm, hbm],
        out_specs=vmem,
        scratch_shapes=[
            pltpu.VMEM((2 * rows, D // 2), bf),
            pltpu.VMEM((2 * rows, D // 2), bf),
            pltpu.VMEM((8, 6 * rows), jnp.float32),
            pltpu.VMEM((6 * rows, D // 2), bf),
            pltpu.VMEM((6 * rows, D // 2), bf),
            pltpu.VMEM((planes, 2 * rows, D // 2), bf),
            pltpu.VMEM((n, 2 * cap, D // 2), bf),
            pltpu.VMEM((planes, 2 * cap, D // 2), bf),
            pltpu.VMEM((planes, 4 * cap, 2 * rows), bf),
            pltpu.VMEM((planes, 2 * cap, rows), bf),
            pltpu.VMEM((n, 16, rows), jnp.float32),
            pltpu.VMEM((n, 16, rows), jnp.float32),
            pltpu.VMEM((SPLIT * cap, D), bf),
            pltpu.VMEM((D, width), bf),
            pltpu.VMEM((width, D), bf),
            pltpu.VMEM((SPLIT * cap, width), bf),
            pltpu.VMEM((n * cap, D), bf),
            pltpu.VMEM((planes * 2 * cap, D), bf),
            pltpu.VMEM((planes * cap, D), bf),
            pltpu.VMEM((planes, 2 * cap, D), bf),
            pltpu.VMEM((planes, rows, D), bf),
            pltpu.VMEM((planes, rows, D), bf),
            dma((5,)),
            dma((5,)),
            dma((6, chunks)),
            dma((2,)),
            dma((2,)),
            dma((planes, 5)),
            dma((planes, chunks)),
            dma((planes, chunks)),
            dma((n,)),
            dma((2,)),
            dma((planes, 4)),
            dma((planes, backs)),
            dma((planes, backs)),
            dma((planes, backs)),
            dma((planes, backs)),
        ],
        compiler_params=pltpu.CompilerParams(
            collective_id=1, has_side_effects=True, vmem_limit_bytes=VMEM_LIMIT
        ),
    )(queries, key_rows, values, modulation, routes.T, gate_fixed.T, expert_in, expert_out)


def slot_table(flat, experts_count):
    onehot = (flat[:, None] == jnp.arange(experts_count, dtype=jnp.int32)[None, :]).astype(
        jnp.int32
    )
    before = jnp.cumsum(onehot, axis=0) - onehot
    return jnp.sum(before * onehot, axis=1)


def expert_apply(rows, first_weight, second_weight):
    hidden = jax.nn.gelu(
        jnp.dot(rows, first_weight, preferred_element_type=jnp.float32), approximate=True
    ).astype(jnp.bfloat16)
    return jnp.dot(hidden, second_weight, preferred_element_type=jnp.float32).astype(jnp.bfloat16)


def experts_sparse(normed, attended, modulation, expert_in, expert_out, routes, gate_fixed):
    devices = lax.axis_size("tile")
    rows_dev = normed.shape[0]
    experts_count = devices // SPLIT
    capacity = 3 * rows_dev // experts_count
    flat = routes.reshape(-1)
    slots = slot_table(flat, experts_count)
    target = flat * capacity + slots
    chooser = (
        target[None, :] == jnp.arange(experts_count * capacity, dtype=jnp.int32)[:, None]
    ).astype(jnp.bfloat16)
    chooser = chooser.reshape(experts_count * capacity, rows_dev, 2).sum(axis=2)
    buffer = jnp.dot(chooser, normed, preferred_element_type=jnp.float32).astype(jnp.bfloat16)
    copies = jnp.broadcast_to(
        buffer.reshape(experts_count, 1, capacity, D), (experts_count, SPLIT, capacity, D)
    ).reshape(devices, capacity, D)
    received = lax.all_to_all(copies, "tile", split_axis=0, concat_axis=0, tiled=True)
    sources = received.shape[0]
    count = received.shape[1]
    partial_value = expert_apply(received.reshape(sources * count, D), expert_in, expert_out)
    returned = lax.all_to_all(
        partial_value.reshape(sources, count, D), "tile", split_axis=0, concat_axis=0, tiled=True
    )
    summed = jnp.sum(
        returned.reshape(experts_count, SPLIT, capacity, D).astype(jnp.float32), axis=1
    )
    expert_rows = summed.astype(jnp.bfloat16).reshape(experts_count * capacity, D)
    picked = jnp.take(expert_rows, target, axis=0).reshape(rows_dev, 2, D)
    gate_scale = gate_fixed.astype(jnp.float32) / 1024.0
    mixture = jnp.sum(picked.astype(jnp.float32) * gate_scale[:, :, None], axis=1)
    return (attended.astype(jnp.float32) + modulation[2] * mixture).astype(jnp.bfloat16)


def shards(queries, key_rows, values, modulation, expert_in, expert_out, routes, gate_fixed):
    n = lax.axis_size("tile")
    cap = 3 * queries.shape[0] // (n // SPLIT)
    if n == 2 * TILE_COLS and cap % 16 == 0 and kernel_bytes(n, queries.shape[0], cap, expert_in.shape[1]) < VMEM_LIMIT * 7 // 8:
        return layer(queries, key_rows, values, modulation, expert_in, expert_out, routes, gate_fixed)
    attended, normed = attention(queries, key_rows, values, modulation)
    return experts_sparse(normed, attended, modulation, expert_in, expert_out, routes, gate_fixed)


def solution(mesh):
    placed = (
        P(("groups", "tile"), None),
        P(("groups", "tile"), None),
        P(("groups", "tile"), None),
        P("groups", None),
        P(None, "tile"),
        P("tile", None),
        P(("groups", "tile"), None),
        P(("groups", "tile"), None),
    )
    return jax.shard_map(
        shards, mesh=mesh, in_specs=placed, out_specs=P(("groups", "tile"), None), check_vma=False
    )
```

```python
import functools
import math

import jax
import jax.numpy as jnp
from jax import lax
from jax.experimental import pallas as pl
from jax.experimental.pallas import tpu as pltpu
from jax.sharding import PartitionSpec as P

HEAD_DIM = 128
D = 4096
SPLIT = 4
TILE_COLS = 8

EPSILON = 1e-06
MASKED = -1e30
MESH = pl.DeviceIdType.MESH
VMEM_LIMIT = 60 * 1024 * 1024
CHUNKS = 8
AHEAD = 2
ASIDE = 2
BEHIND = 1
HOP = 2
PASS = 4
DRAIN = (1, 8)
EARLY = 2
BACK_CHUNKS = 4
BACK_LAGS = (1, 4, 7)


def when(cond, body):
    if cond is True:
        body()
    else:
        pl.when(cond)(body)


def both(a, b):
    if a is True:
        return b
    if b is True:
        return a
    return jnp.logical_and(a, b)


def remote(src, dst, send_sem, recv_sem, target):
    return pltpu.make_async_remote_copy(
        src_ref=src,
        dst_ref=dst,
        send_sem=send_sem,
        recv_sem=recv_sem,
        device_id={"tile": target},
        device_id_type=MESH,
    )


def halo_levels(n):
    grid_rows = n // TILE_COLS
    if grid_rows < 2:
        return 1
    return 2 if grid_rows == 2 else 3


def attention_kernel(
    n, rows, q_ref, k_ref, v_ref, mod_ref, att_ref, norm_ref, keys, vals, send_sem, recv_sem, own_sem,
):
    me = lax.axis_index("tile")
    grid_rows = n // TILE_COLS
    tile = lax.rem(me + TILE_COLS // 2, n)
    row = lax.div(tile, TILE_COLS)
    col = lax.rem(tile, TILE_COLS)
    if grid_rows < 2:
        verticals = []
    elif grid_rows == 2:
        verticals = [(1, TILE_COLS, True, 1)]
    else:
        verticals = [(1, n - TILE_COLS, row > 0, 2), (2, TILE_COLS, row < grid_rows - 1, 1)]
    sides = [(-1, col > 0), (1, col < TILE_COLS - 1)]
    here = {level: exists for level, _, exists, _ in verticals}
    here[0] = True

    def slot(level, side):
        return level * 3 + 1 + side

    def place(buf, s):
        return buf.at[pl.ds(s * rows, rows), :]

    def over(offset):
        return lax.rem(me + offset + n, n)

    half = rows // 2
    middle = TILE_COLS // 2
    crossing = {side: col == (middle if side < 0 else middle - 1) for side, _ in sides}
    two = grid_rows == 2

    def part_of(buf, s, h):
        return buf.at[pl.ds(pl.multiple_of(s * rows + h * half, half), half), :]

    own = [
        pltpu.make_async_copy(src, place(buf, slot(0, 0)), own_sem.at[i])
        for i, (src, buf) in enumerate(((k_ref, keys), (v_ref, vals)))
    ]
    for copy in own:
        copy.start()

    def beside(side):
        if not two:
            return over(side)
        return jnp.where(crossing[side], over(side + TILE_COLS), over(side))

    def level_there(level, side):
        return jnp.where(crossing[side], 1 - level, level) if two else level

    barrier = pltpu.get_barrier_semaphore()
    partners = [(over(offset), exists) for _, offset, exists, _ in verticals]
    partners += [(beside(side), exists) for side, exists in sides]
    for target, exists in partners:

        def greet(target=target):
            pl.semaphore_signal(barrier, inc=1, device_id={"tile": target}, device_id_type=MESH)

        when(exists, greet)
    expected = sum(1 if exists is True else jnp.where(exists, 1, 0) for _, exists in partners)
    pl.semaphore_wait(barrier, expected)

    sends = []
    pieces = [(i, h) for i in (0, 1) for h in (0, 1)]
    bufs = (keys, vals)

    def push(i, h, src, there, target, exists):
        copy = remote(
            src,
            part_of(bufs[i], there, h),
            send_sem.at[len(sends)],
            recv_sem.at[there, i * 2 + h],
            target,
        )
        when(exists, copy.start)
        sends.append((copy, exists))

    def arrived(s, exists, i, h):
        ref = part_of(bufs[i], s, h)
        when(exists, remote(ref, ref, send_sem.at[0], recv_sem.at[s, i * 2 + h], me).wait_recv)

    def own_part(i, h):
        return (k_ref, v_ref)[i].at[pl.ds(h * half, half), :]

    for i, h in pieces:
        for level, offset, exists, there in verticals:
            push(i, h, own_part(i, h), slot(there, 0), over(offset), exists)
    for i, h in pieces:
        for side, exists in sides:
            push(i, h, own_part(i, h), slot(level_there(0, side), -side), beside(side), exists)
    for s in range(3 * (1 + len(verticals))):
        level, side = s // 3, s % 3 - 1
        exists = here[level]
        for other, side_exists in sides:
            if other == side:
                exists = both(exists, side_exists)
        if exists is True:
            continue

        def clear(s=s):
            for buf in (keys, vals):
                buf[pl.ds(s * rows, rows), :] = jnp.zeros((rows, D), buf.dtype)

        pl.when(jnp.logical_not(exists))(clear)
    for i, h in pieces:
        for level, offset, exists, there in verticals:
            arrived(slot(level, 0), exists, i, h)
            for side, side_exists in sides:
                push(
                    i,
                    h,
                    part_of(bufs[i], slot(level, 0), h),
                    slot(level_there(level, side), -side),
                    beside(side),
                    both(exists, side_exists),
                )
    for copy in own:
        copy.wait()
    for i, h in pieces:
        for level, exists in sorted(here.items(), key=lambda item: item[0]):
            for side, side_exists in sides:
                arrived(slot(level, side), both(exists, side_exists), i, h)

    span = 3 * (1 + len(verticals)) * rows
    where = lax.broadcasted_iota(jnp.int32, (rows, span), 1)
    bias = jnp.zeros((rows, span), jnp.float32)
    for s in range(span // rows):
        level, side = s // 3, s % 3 - 1
        exists = here[level]
        for other, side_exists in sides:
            if other == side:
                exists = both(exists, side_exists)
        if exists is True:
            continue
        penalty = jnp.where(exists, 0.0, MASKED)
        bias = jnp.where((where >= s * rows) & (where < (s + 1) * rows), penalty, bias)
    scale = 1.0 / math.sqrt(HEAD_DIM)
    together = 8

    def heads(step, carry):
        for extra in range(together):
            at = pl.ds(pl.multiple_of((step * together + extra) * HEAD_DIM, HEAD_DIM), HEAD_DIM)
            scores = lax.dot_general(
                q_ref[:, at], keys[:, at], (((1,), (1,)), ((), ())), preferred_element_type=jnp.float32
            )
            scores = scores * scale + bias
            raised = jnp.exp(scores - jnp.max(scores, axis=-1, keepdims=True))
            probs = (raised * (1.0 / jnp.sum(raised, axis=-1, keepdims=True))).astype(jnp.bfloat16)
            att_ref[:, at] = jnp.dot(probs, vals[:, at], preferred_element_type=jnp.float32).astype(
                att_ref.dtype
            )
        return carry

    lax.fori_loop(0, D // HEAD_DIM // together, heads, 0)

    def normalise(step, carry):
        at = pl.ds(pl.multiple_of(step * 16, 16), 16)
        wide = att_ref[at, :].astype(jnp.float32)
        wide = wide - jnp.mean(wide, axis=-1, keepdims=True)
        spread = jnp.mean(wide * wide, axis=-1, keepdims=True)
        normed = wide * lax.rsqrt(spread + EPSILON)
        norm_ref[at, :] = (normed * (1.0 + mod_ref[1:2, :]) + mod_ref[0:1, :]).astype(norm_ref.dtype)
        return carry

    lax.fori_loop(0, rows // 16, normalise, 0)
    for copy, exists in sends:
        when(exists, copy.wait_send)


def attention(queries, key_rows, values, modulation):
    n = lax.axis_size("tile")
    rows = queries.shape[0]
    levels = halo_levels(n)
    slots = 3 * levels
    vmem = pl.BlockSpec(memory_space=pltpu.VMEM)
    hbm = pl.BlockSpec(memory_space=pl.ANY)
    return pl.pallas_call(
        functools.partial(attention_kernel, n, rows),
        name="halo_attention",
        out_shape=(
            jax.ShapeDtypeStruct((rows, D), jnp.bfloat16),
            jax.ShapeDtypeStruct((rows, D), jnp.bfloat16),
        ),
        in_specs=[vmem, hbm, hbm, vmem],
        out_specs=(vmem, vmem),
        scratch_shapes=[
            pltpu.VMEM((slots * rows, D), jnp.bfloat16),
            pltpu.VMEM((slots * rows, D), jnp.bfloat16),
            pltpu.SemaphoreType.DMA((4 * (2 + 3 * (levels - 1)),)),
            pltpu.SemaphoreType.DMA((slots, 4)),
            pltpu.SemaphoreType.DMA((2,)),
        ],
        compiler_params=pltpu.CompilerParams(
            collective_id=0, has_side_effects=True, vmem_limit_bytes=VMEM_LIMIT
        ),
    )(queries, key_rows, values, modulation)


def device(plane, yy, cc):
    return plane * SPLIT + yy * 2 + cc


def layer_kernel(
    n, rows, cap, chunks, backs, q_ref, k_ref, v_ref, mod_ref, routes_ref, gates_ref, first_ref, second_ref,
    out_ref, att, asked, bias, keys, vals, line, tokens, stage, chooser, spreader, tables, stats, normed,
    first, second, hidden, part, r1, r2, pair, acc_in, acc_out,
    own_sem, kv_send, kv_recv, table_send, table_recv, out_send, line_recv, beside_recv, twin_recv,
    rest_sem, back_send, s1_recv, s2_recv, pair_recv, acc_recv,
):
    planes = n // SPLIT
    width = first.shape[1]
    half = D // 2
    wide = half // chunks
    me = lax.axis_index("tile")
    p = lax.div(me, SPLIT)
    y = lax.div(lax.rem(me, SPLIT), 2)
    c = lax.rem(me, 2)
    beside = device(p, 1 - y, c)
    twin = device(p, y, 1 - c)
    low_half = p < planes // 2
    toward = jnp.where(low_half, 1, -1)
    inner = p + toward
    outer = p - toward
    at_end = jnp.logical_or(p == 0, p == planes - 1)
    middle = jnp.logical_not(at_end)
    outer_expert = jnp.where(low_half, 0, planes - 1)
    inner_device = device(inner, y, c)
    outer_device = device(jnp.where(at_end, p, outer), y, c)

    tile = lax.rem(me + TILE_COLS // 2, n)
    column = lax.rem(tile, TILE_COLS)
    partner = lax.rem(me + TILE_COLS, n)
    sides = [(-1, column > 0), (1, column < TILE_COLS - 1)]
    half_way = TILE_COLS // 2
    crossing = {-1: column == half_way, 1: column == half_way - 1}

    def part_of_plane(plane):
        return jnp.where(plane < planes // 2, half, 0)

    mine_from = part_of_plane(p)
    other_from = half - mine_from
    partner_plane = lax.rem(p + planes // 2, planes)

    def cols(j, base=0):
        return pl.ds(pl.multiple_of(base + j * wide, wide), wide)

    def halves(base):
        return pl.ds(pl.multiple_of(base, half), half)

    def lines(buf, s):
        return buf.at[pl.ds(pl.multiple_of(s * rows, rows), rows), :]

    loads = [
        pltpu.make_async_copy(q_ref.at[:, halves(mine_from)], lines(asked, 0), own_sem.at[0]),
        pltpu.make_async_copy(k_ref.at[:, halves(mine_from)], lines(keys, 1), own_sem.at[1]),
        pltpu.make_async_copy(v_ref.at[:, halves(mine_from)], lines(vals, 1), own_sem.at[2]),
        pltpu.make_async_copy(first_ref, first, own_sem.at[3]),
        pltpu.make_async_copy(second_ref, second, own_sem.at[4]),
    ]

    barrier = pltpu.get_barrier_semaphore()
    others = [lax.rem(me + step, n) for step in range(1, n)]
    for target in others:
        pl.semaphore_signal(barrier, inc=1, device_id={"tile": target}, device_id_type=MESH)

    def beside_tile(side):
        return lax.rem(me + side + jnp.where(crossing[side], TILE_COLS, 0) + n, n)

    def slot_there(level, side):
        return jnp.where(crossing[side], 1 - level, level) * 3 + 1 - side

    bufs = (keys, vals, asked)
    given = (k_ref, v_ref, q_ref)

    def place(i, s, j):
        return bufs[i].at[pl.ds(pl.multiple_of(s * rows, rows), rows), cols(j)]

    def over_vertical(i, j):
        return remote(
            given[i].at[:, cols(j, other_from)],
            place(i, 4 if i < 2 else 1, j),
            kv_send.at[0],
            kv_recv.at[4, j],
            partner,
        )

    def over_side(level, index, i, j):
        side = sides[index][0]
        there = slot_there(level, side)
        source = given[i].at[:, cols(j, mine_from)] if level == 0 else place(i, 4, j)
        return remote(
            source,
            place(i, there, j),
            kv_send.at[1 + level * 2 + index],
            kv_recv.at[there, j],
            beside_tile(side),
        )

    def landed(ref, sem):
        remote(ref, ref, own_sem.at[0], sem, me).wait_recv()

    def send_own(j):
        for i in range(3):
            over_vertical(i, j).start()

    def send_side(j):
        for i in (0, 1):
            for index, (_, exists) in enumerate(sides):
                when(exists, over_side(0, index, i, j).start)

    def bytes_of(count, at):
        return keys.at[pl.ds(0, count * rows), at]

    def send_vertical(j):
        landed(bytes_of(3, cols(j)), kv_recv.at[4, j])
        for i in (0, 1):
            for index, (_, exists) in enumerate(sides):
                when(exists, over_side(1, index, i, j).start)

    pl.semaphore_wait(barrier, n - 1)
    send_own(0)
    send_side(0)
    for load in loads[:3]:
        load.start()

    expert = lax.broadcasted_iota(jnp.int32, (8, rows), 0)
    named = [routes_ref[k : k + 1, :] == expert for k in (0, 1)]
    member = jnp.logical_or(named[0], named[1])
    upto = (
        lax.broadcasted_iota(jnp.int32, (rows, rows), 0) <= lax.broadcasted_iota(jnp.int32, (rows, rows), 1)
    ).astype(jnp.float32).astype(jnp.bfloat16)
    count = jnp.dot(
        member.astype(jnp.float32).astype(jnp.bfloat16), upto, preferred_element_type=jnp.float32
    )
    gate = sum(
        jnp.where(named[k], gates_ref[k : k + 1, :].astype(jnp.float32), 0.0) for k in (0, 1)
    )
    tables[me, 0:8, :] = jnp.where(member, count - 1.0, -1.0)
    stats[me, 8:16, :] = jnp.where(member, count - 1.0, -1.0)
    tables[me, 8:16, :] = gate / 1024.0

    column_planes = [lax.rem(p + step, planes) for step in range(1, planes)]

    def tell_column(step):
        there = device(column_planes[step], y, c)
        return remote(tables.at[me], tables.at[me], table_send.at[0], table_recv.at[0], there)

    for step in range(planes - 1):
        tell_column(step).start()
    for j in range(1, max(AHEAD, ASIDE)):
        if j < min(AHEAD, chunks):
            send_own(j)
        if j < min(ASIDE, chunks):
            send_side(j)

    span = 6 * rows
    where = lax.broadcasted_iota(jnp.int32, (8, span), 1)
    penalty = jnp.zeros((8, span), jnp.float32)
    for s in range(6):
        for side, exists in sides:
            if side != s % 3 - 1:
                continue
            here = (where >= s * rows) & (where < (s + 1) * rows)
            penalty = jnp.where(here, jnp.where(exists, 0.0, MASKED), penalty)

            def clear(s=s):
                for buf in (keys, vals):
                    buf[s * rows : (s + 1) * rows, :] = jnp.zeros((rows, half), buf.dtype)

            pl.when(jnp.logical_not(exists))(clear)
    bias[...] = penalty
    chooser[...] = jnp.zeros(chooser.shape, chooser.dtype)

    def tell_all():
        return [
            remote(stats.at[me], stats.at[me], table_send.at[1], table_recv.at[1], target)
            for target in others
        ]

    for load in loads[:3]:
        load.wait()
    for load in loads[3:]:
        load.start()

    slot_line = lax.broadcasted_iota(jnp.int32, (cap, rows), 0).astype(jnp.float32)

    def chosen(tile_there, e):
        return tables[tile_there, pl.ds(e, 1), :] == slot_line

    def picked_column(which, row):
        return jnp.sum(jnp.where(which, row, 0.0), axis=1, keepdims=True)

    def choose():
        landed(tables.at[pl.ds(0, planes - 1)], table_recv.at[0])
        for plane in range(planes):
            for place_in, e in ((0, p), (1, outer_expert)):
                found = chosen(device(plane, y, c), e).astype(jnp.float32).astype(jnp.bfloat16)
                at = place_in * 2 * cap
                spreader[plane, place_in * cap : (place_in + 1) * cap, :] = found
                chooser[plane, at : at + cap, :rows] = found
                chooser[(plane + planes // 2) % planes, at + cap : at + 2 * cap, rows:] = found

    scale = 1.0 / math.sqrt(HEAD_DIM)

    def attend(j):
        for level in (0, 1):
            for side, exists in sides:
                s = level * 3 + 1 + side
                when(exists, functools.partial(landed, bytes_of(2, cols(j)), kv_recv.at[s, j]))
        for extra in range(wide // HEAD_DIM):
            at = pl.ds(pl.multiple_of(j * wide + extra * HEAD_DIM, HEAD_DIM), HEAD_DIM)
            scores = lax.dot_general(
                asked[:, at], keys[:, at], (((1,), (1,)), ((), ())), preferred_element_type=jnp.float32
            )
            scores = scores * scale + bias[0:1, :]
            raised = jnp.exp(scores - jnp.max(scores, axis=-1, keepdims=True))
            probs = (raised * (1.0 / jnp.sum(raised, axis=-1, keepdims=True))).astype(jnp.bfloat16)
            att[:, at] = jnp.dot(probs, vals[:, at], preferred_element_type=jnp.float32).astype(att.dtype)

    def raw_copy(k, src, j):
        source = att.at[:, cols(j)] if k == 0 else line.at[src, :, cols(j)]
        return remote(source, line.at[src, :, cols(j)], out_send.at[k, 0], line_recv.at[src, j], inner_device)

    def outer_copy(k, src, j):
        there = device(src, y, c)
        return remote(
            stage.at[src, :, cols(j)],
            tokens.at[there, :, cols(j)],
            out_send.at[k, 1],
            line_recv.at[src, j],
            outer_device,
        )

    def rest_copy(src, j):
        ref = line.at[src, pl.ds(rows, rows), cols(j)]
        return remote(ref, ref, rest_sem.at[0], rest_sem.at[1], outer_device)

    def plane_copy(k, src, j, index):
        ref = tokens.at[device(src, y, c), :, cols(j)]
        recv = beside_recv.at[src, j] if index == 0 else twin_recv.at[device(src, y, c)]
        return remote(ref, ref, out_send.at[k, 2 + index], recv, (beside, twin)[index])

    def twin_copy(k, src, j):
        there = device(src, 1 - y, c)
        ref = tokens.at[there, :, cols(j)]
        return remote(ref, ref, out_send.at[k, 4], twin_recv.at[there], twin)

    far = jnp.where(at_end, p + 3 * toward, p + 2 * toward)
    second_plane = jnp.where(at_end, p + 2 * toward, outer)
    sources = [
        (p, BEHIND, True, middle),
        (inner, BEHIND + HOP, False, middle),
        (second_plane, BEHIND + HOP * jnp.where(at_end, 2, 1), middle, False),
        (far, BEHIND + HOP * jnp.where(at_end, 3, 2), False, middle),
    ]

    def relay(k, j):
        src, behind, whole, out = sources[k]
        jj = j - behind

        def go():
            there = device(src, y, c)
            if k > 0:
                pl.when(at_end)(
                    lambda: landed(tokens.at[there, :, cols(jj)], line_recv.at[src, jj])
                )
                pl.when(middle)(lambda: landed(line.at[src, :, cols(jj)], line_recv.at[src, jj]))
            if whole is not False:
                when(whole, raw_copy(k, src, jj).start)
            if k == 1:
                pl.when(middle)(rest_copy(src, jj).start)

            def pick():
                rows_here = att[:, cols(jj)] if k == 0 else line[src, :, cols(jj)]
                picked = jnp.dot(chooser[src], rows_here, preferred_element_type=jnp.float32).astype(
                    tokens.dtype
                )
                tokens[there, :, cols(jj)] = picked[: 2 * cap]
                stage[src, :, cols(jj)] = picked[2 * cap :]

            when(True if k == 0 else middle, pick)
            if out is not False:
                when(out, outer_copy(k, src, jj).start)
            for index in (0, 1):
                plane_copy(k, src, jj, index).start()

        pl.when(jnp.logical_and(jj >= 0, jj < chunks))(go)

    def pass_on(k, j):
        src, behind, _, _ = sources[k]
        jj = j - behind - PASS

        def go():
            there = device(src, 1 - y, c)
            landed(tokens.at[there, :, cols(jj)], beside_recv.at[src, jj])
            twin_copy(k, src, jj).start()

        pl.when(jnp.logical_and(jj >= 0, jj < chunks))(go)

    def move(j):
        for k in range(planes):
            relay(k, j)
        for k in range(planes):
            pass_on(k, j)

    def stream(j, carry):
        pl.when(j < chunks)(lambda: send_vertical(j))

        pl.when(j + AHEAD < chunks)(lambda: send_own(j + AHEAD))
        pl.when(j + ASIDE < chunks)(lambda: send_side(j + ASIDE))
        pl.when(j == BEHIND)(choose)
        pl.when(j >= BEHIND)(lambda: attend(j - BEHIND))
        move(j)
        return carry

    lax.fori_loop(0, chunks + BEHIND, stream, 0)

    def drain(j, carry):
        move(j)
        return carry

    lax.fori_loop(chunks + BEHIND, chunks + BEHIND + DRAIN[0], drain, 0)

    token = lax.broadcasted_iota(jnp.int32, (16, rows), 1)
    line_of = lax.broadcasted_iota(jnp.int32, (16, rows), 0)
    row_number = lax.broadcasted_iota(jnp.int32, (8, rows), 0)
    found = jnp.zeros((8, rows), jnp.float32)
    for step in range(2 * rows // 16):
        some = att[step * 16 : (step + 1) * 16, :].astype(jnp.float32)
        mean = jnp.mean(some, axis=-1, keepdims=True)
        some = some - mean
        spread = jnp.mean(some * some, axis=-1, keepdims=True)
        which, at = divmod(step * 16, rows)
        for kind, value in enumerate((mean, spread)):
            row = jnp.sum(jnp.where(token == line_of + at, value, 0.0), axis=0, keepdims=True)
            found = found + jnp.where(row_number == 2 * which + kind, row, 0.0)
    stats[me, 0:8, :] = found
    for copy in tell_all():
        copy.start()

    lax.fori_loop(chunks + BEHIND + DRAIN[0], chunks + BEHIND + DRAIN[1], drain, 0)
    landed(stats.at[pl.ds(0, n - 1)], table_recv.at[1])
    for load in loads[3:]:
        load.wait()

    order = [
        jnp.where(at_end, p + 2 * toward, inner),
        jnp.where(at_end, p + 3 * toward, p + 2 * toward),
        jnp.where(at_end, inner, outer),
        p,
    ]
    def arrive(plane):
        for source in (plane, lax.rem(plane + planes // 2, planes)):
            for yy in (0, 1):
                there = device(source, yy, 1 - c)
                landed(tokens.at[there], twin_recv.at[there])

    group = SPLIT * cap
    chunk = 512
    span_back = D // backs

    def home_of(i):
        return jnp.where(i == 0, order[0], jnp.where(i == 1, order[1], jnp.where(i == 2, order[2], order[3])))

    def block(buf, index, count, j):
        return buf.at[pl.ds(pl.multiple_of(index * cap, 16), count * cap), back_cols(j)]

    def back_cols(j):
        return pl.ds(pl.multiple_of(j * span_back, span_back), span_back)

    def start_group(plane):
        def normalise(t, carry):
            yy, cc = lax.rem(t, 2), lax.div(t, 2)
            there = device(plane, yy, cc)
            across = lax.rem(there + TILE_COLS, n)
            mean_here, mean_there = stats[there, 0:1, :], stats[across, 2:3, :]
            apart = 0.5 * (mean_here - mean_there)
            spread = 0.5 * (stats[there, 1:2, :] + stats[across, 3:4, :]) + apart * apart
            which = stats[there, pl.ds(8 + p, 1), :] == slot_line
            mean = picked_column(which, 0.5 * (mean_here + mean_there))
            rate = picked_column(which, lax.rsqrt(spread + EPSILON))
            at = pl.ds(pl.multiple_of(t * cap, 16), cap)
            base = part_of_plane(plane)
            for source, lower, start in ((there, 0, base), (across, cap, half - base)):
                for step in range(half // chunk):
                    some = slice(step * chunk, (step + 1) * chunk)
                    to = pl.ds(pl.multiple_of(start + step * chunk, chunk), chunk)
                    value = (tokens[source, lower : lower + cap, some].astype(jnp.float32) - mean) * rate
                    normed[at, to] = (value * (1.0 + mod_ref[1:2, to]) + mod_ref[0:1, to]).astype(
                        normed.dtype
                    )
            return carry

        lax.fori_loop(0, SPLIT, normalise, 0)
        raw = jnp.dot(normed[...], first[...], preferred_element_type=jnp.float32)
        hidden[...] = jax.nn.gelu(raw, approximate=True).astype(hidden.dtype)

    def to_twin(plane, j):
        return remote(
            block(part, plane * SPLIT + (1 - c) * 2, 2, j),
            block(r1, plane * 2, 2, j),
            back_send.at[plane, 0],
            s1_recv.at[plane, j],
            twin,
        )

    def to_beside(plane, j):
        return remote(
            block(part, plane * SPLIT + c * 2 + 1 - y, 1, j),
            block(r2, plane, 1, j),
            back_send.at[plane, 1],
            s2_recv.at[plane, j],
            beside,
        )

    def slots_home(plane, j):
        return remote(
            pair.at[plane, pl.ds(0, cap), back_cols(j)],
            pair.at[plane, pl.ds(cap, cap), back_cols(j)],
            back_send.at[plane, 2],
            pair_recv.at[plane, j],
            inner_device,
        )

    def rows_home(plane, j):
        return remote(
            acc_out.at[plane, :, back_cols(j)],
            acc_in.at[plane, :, back_cols(j)],
            back_send.at[plane, 3],
            acc_recv.at[plane, j],
            device(jnp.where(plane == outer, outer, inner), y, c),
        )

    def produce(i, j):
        plane = home_of(i)
        pl.when(jnp.logical_and(j == 0, i < 2))(lambda: arrive(plane))
        pl.when(j == 0)(lambda: start_group(plane))
        raw = jnp.dot(hidden[...], second[:, back_cols(j)], preferred_element_type=jnp.float32)
        mine = pl.ds(pl.multiple_of(plane * group, 16), group)
        part[mine, back_cols(j)] = raw.astype(part.dtype)
        to_twin(plane, j).start()

    def fold_twin(i, j):
        plane = home_of(i)
        landed(block(r1, plane * 2, 2, j), s1_recv.at[plane, j])
        for yy in (1 - y, y):
            at = pl.ds(pl.multiple_of((plane * SPLIT + c * 2 + yy) * cap, 16), cap)
            there = pl.ds(pl.multiple_of((plane * 2 + yy) * cap, 16), cap)
            total = part[at, back_cols(j)].astype(jnp.float32) + r1[there, back_cols(j)].astype(jnp.float32)
            part[at, back_cols(j)] = total.astype(part.dtype)
            if yy is not y:
                to_beside(plane, j).start()

    def fold_beside(i, j):
        plane = home_of(i)
        there = device(plane, y, c)
        landed(block(r2, plane, 1, j), s2_recv.at[plane, j])
        weight = picked_column(chosen(there, p), tables[there, pl.ds(8 + p, 1), :])
        ours = pl.ds(pl.multiple_of((plane * SPLIT + c * 2 + y) * cap, 16), cap)
        theirs = pl.ds(pl.multiple_of(plane * cap, 16), cap)
        total = part[ours, back_cols(j)].astype(jnp.float32) + r2[theirs, back_cols(j)].astype(jnp.float32)
        pair[plane, :cap, back_cols(j)] = (total * weight).astype(pair.dtype)
        pl.when(jnp.logical_and(at_end, plane != p))(slots_home(plane, j).start)

    def spread_out(plane, both, at):
        amount = 2 * cap if both else cap
        return lax.dot_general(
            spreader[plane, :amount, :],
            pair[plane, :amount, at],
            (((0,), (0,)), ((), ())),
            preferred_element_type=jnp.float32,
        )

    def fold_home(i, j):
        plane = home_of(i)
        at = back_cols(j)

        def fold(both, extra, last):
            if both:
                landed(pair.at[plane, pl.ds(cap, cap), at], pair_recv.at[plane, j])
            if extra:
                landed(acc_in.at[plane, :, at], acc_recv.at[plane, j])
            total = spread_out(plane, both, at)
            if extra:
                total = total + acc_in[plane, :, at].astype(jnp.float32)
            if last:
                out_ref[:, at] = (mod_ref[2:3, at] * total + out_ref[:, at].astype(jnp.float32)).astype(
                    out_ref.dtype
                )
            else:
                acc_out[plane, :, at] = total.astype(acc_out.dtype)
                rows_home(plane, j).start()

        pl.when(jnp.logical_and(at_end, i == 3))(lambda: fold(False, True, True))
        pl.when(jnp.logical_and(middle, i == 3))(lambda: fold(True, True, True))
        pl.when(jnp.logical_and(middle, i == 2))(lambda: fold(False, True, False))
        pl.when(jnp.logical_and(middle, i < 2))(lambda: fold(True, False, False))

    units = planes * backs

    def begin_result():
        pl.when(at_end)(lambda: landed(line.at[partner_plane, pl.ds(rows, rows), :], rest_sem.at[1]))
        out_ref[:, halves(mine_from)] = att[:rows, :]
        out_ref[:, halves(other_from)] = line[partner_plane, rows:, :]

    def give_back(u, carry):
        pl.when(u == 2 * backs + 2)(begin_result)
        for behind, act in ((0, produce), (BACK_LAGS[0], fold_twin), (BACK_LAGS[1], fold_beside), (BACK_LAGS[2], fold_home)):
            at = u - behind
            i, j = lax.div(at, backs), lax.rem(at, backs)
            pl.when(jnp.logical_and(at >= 0, at < units))(functools.partial(act, i, j))
        return carry

    lax.fori_loop(0, EARLY, give_back, 0)
    lax.fori_loop(chunks + BEHIND + DRAIN[1], chunks + BEHIND + 3 * HOP + PASS, drain, 0)
    lax.fori_loop(EARLY, units + BACK_LAGS[2], give_back, 0)

    def gone(ref, sem):
        remote(ref, ref, sem, own_sem.at[0], twin).wait_send()

    every = pl.ds(0, half)
    gone(bytes_of(3, every), kv_send.at[0])
    for level in (0, 1):
        for index, (_, exists) in enumerate(sides):
            when(exists, functools.partial(gone, bytes_of(2, every), kv_send.at[1 + level * 2 + index]))
    for k, (_, _, whole, out) in enumerate(sources):
        if whole is not False:
            when(whole, functools.partial(gone, line.at[0], out_send.at[k, 0]))
        if out is not False:
            when(out, functools.partial(gone, stage.at[0], out_send.at[k, 1]))
        for index in range(3):
            gone(tokens.at[0], out_send.at[k, 2 + index])
    pl.when(middle)(lambda: gone(line.at[0, pl.ds(0, rows), :], rest_sem.at[0]))
    gone(tables.at[pl.ds(0, planes - 1)], table_send.at[0])
    gone(stats.at[pl.ds(0, n - 1)], table_send.at[1])
    for plane in range(planes):
        gone(r1.at[pl.ds(0, 2 * cap), :], back_send.at[plane, 0])
        gone(r1.at[pl.ds(0, cap), :], back_send.at[plane, 1])
        away = p != plane
        pl.when(jnp.logical_and(at_end, away))(
            functools.partial(gone, r1.at[pl.ds(0, cap), :], back_send.at[plane, 2])
        )
        pl.when(jnp.logical_and(middle, away))(functools.partial(gone, acc_in.at[0], back_send.at[plane, 3]))


def kernel_bytes(n, rows, cap, width):
    planes = n // SPLIT
    lines = 2 * 6 * rows + 2 * n * cap + planes * (6 * cap + 3 * rows) + SPLIT * cap + 3 * rows
    return 2 * (lines * D + 2 * width * D)


def layer(queries, key_rows, values, modulation, expert_in, expert_out, routes, gate_fixed):
    n = lax.axis_size("tile")
    rows = queries.shape[0]
    width = expert_in.shape[1]
    planes = n // SPLIT
    cap = 3 * rows // planes
    chunks, backs = CHUNKS, BACK_CHUNKS
    vmem = pl.BlockSpec(memory_space=pltpu.VMEM)
    hbm = pl.BlockSpec(memory_space=pl.ANY)
    dma = pltpu.SemaphoreType.DMA
    bf = jnp.bfloat16
    return pl.pallas_call(
        functools.partial(layer_kernel, n, rows, cap, CHUNKS, BACK_CHUNKS),
        name="whole_layer",
        out_shape=pltpu.VMEM((rows, D), bf),
        in_specs=[hbm, hbm, hbm, vmem, vmem, vmem, hbm, hbm],
        out_specs=vmem,
        scratch_shapes=[
            pltpu.VMEM((2 * rows, D // 2), bf),
            pltpu.VMEM((2 * rows, D // 2), bf),
            pltpu.VMEM((8, 6 * rows), jnp.float32),
            pltpu.VMEM((6 * rows, D // 2), bf),
            pltpu.VMEM((6 * rows, D // 2), bf),
            pltpu.VMEM((planes, 2 * rows, D // 2), bf),
            pltpu.VMEM((n, 2 * cap, D // 2), bf),
            pltpu.VMEM((planes, 2 * cap, D // 2), bf),
            pltpu.VMEM((planes, 4 * cap, 2 * rows), bf),
            pltpu.VMEM((planes, 2 * cap, rows), bf),
            pltpu.VMEM((n, 16, rows), jnp.float32),
            pltpu.VMEM((n, 16, rows), jnp.float32),
            pltpu.VMEM((SPLIT * cap, D), bf),
            pltpu.VMEM((D, width), bf),
            pltpu.VMEM((width, D), bf),
            pltpu.VMEM((SPLIT * cap, width), bf),
            pltpu.VMEM((n * cap, D), bf),
            pltpu.VMEM((planes * 2 * cap, D), bf),
            pltpu.VMEM((planes * cap, D), bf),
            pltpu.VMEM((planes, 2 * cap, D), bf),
            pltpu.VMEM((planes, rows, D), bf),
            pltpu.VMEM((planes, rows, D), bf),
            dma((5,)),
            dma((5,)),
            dma((6, chunks)),
            dma((2,)),
            dma((2,)),
            dma((planes, 5)),
            dma((planes, chunks)),
            dma((planes, chunks)),
            dma((n,)),
            dma((2,)),
            dma((planes, 4)),
            dma((planes, backs)),
            dma((planes, backs)),
            dma((planes, backs)),
            dma((planes, backs)),
        ],
        compiler_params=pltpu.CompilerParams(
            collective_id=1, has_side_effects=True, vmem_limit_bytes=VMEM_LIMIT
        ),
    )(queries, key_rows, values, modulation, routes.T, gate_fixed.T, expert_in, expert_out)


def slot_table(flat, experts_count):
    onehot = (flat[:, None] == jnp.arange(experts_count, dtype=jnp.int32)[None, :]).astype(
        jnp.int32
    )
    before = jnp.cumsum(onehot, axis=0) - onehot
    return jnp.sum(before * onehot, axis=1)


def expert_apply(rows, first_weight, second_weight):
    hidden = jax.nn.gelu(
        jnp.dot(rows, first_weight, preferred_element_type=jnp.float32), approximate=True
    ).astype(jnp.bfloat16)
    return jnp.dot(hidden, second_weight, preferred_element_type=jnp.float32).astype(jnp.bfloat16)


def experts_sparse(normed, attended, modulation, expert_in, expert_out, routes, gate_fixed):
    devices = lax.axis_size("tile")
    rows_dev = normed.shape[0]
    experts_count = devices // SPLIT
    capacity = 3 * rows_dev // experts_count
    flat = routes.reshape(-1)
    slots = slot_table(flat, experts_count)
    target = flat * capacity + slots
    chooser = (
        target[None, :] == jnp.arange(experts_count * capacity, dtype=jnp.int32)[:, None]
    ).astype(jnp.bfloat16)
    chooser = chooser.reshape(experts_count * capacity, rows_dev, 2).sum(axis=2)
    buffer = jnp.dot(chooser, normed, preferred_element_type=jnp.float32).astype(jnp.bfloat16)
    copies = jnp.broadcast_to(
        buffer.reshape(experts_count, 1, capacity, D), (experts_count, SPLIT, capacity, D)
    ).reshape(devices, capacity, D)
    received = lax.all_to_all(copies, "tile", split_axis=0, concat_axis=0, tiled=True)
    sources = received.shape[0]
    count = received.shape[1]
    partial_value = expert_apply(received.reshape(sources * count, D), expert_in, expert_out)
    returned = lax.all_to_all(
        partial_value.reshape(sources, count, D), "tile", split_axis=0, concat_axis=0, tiled=True
    )
    summed = jnp.sum(
        returned.reshape(experts_count, SPLIT, capacity, D).astype(jnp.float32), axis=1
    )
    expert_rows = summed.astype(jnp.bfloat16).reshape(experts_count * capacity, D)
    picked = jnp.take(expert_rows, target, axis=0).reshape(rows_dev, 2, D)
    gate_scale = gate_fixed.astype(jnp.float32) / 1024.0
    mixture = jnp.sum(picked.astype(jnp.float32) * gate_scale[:, :, None], axis=1)
    return (attended.astype(jnp.float32) + modulation[2] * mixture).astype(jnp.bfloat16)


def shards(queries, key_rows, values, modulation, expert_in, expert_out, routes, gate_fixed):
    n = lax.axis_size("tile")
    cap = 3 * queries.shape[0] // (n // SPLIT)
    if n == 2 * TILE_COLS and cap % 16 == 0 and kernel_bytes(n, queries.shape[0], cap, expert_in.shape[1]) < VMEM_LIMIT * 7 // 8:
        return layer(queries, key_rows, values, modulation, expert_in, expert_out, routes, gate_fixed)
    attended, normed = attention(queries, key_rows, values, modulation)
    return experts_sparse(normed, attended, modulation, expert_in, expert_out, routes, gate_fixed)


def solution(mesh):
    placed = (
        P(("groups", "tile"), None),
        P(("groups", "tile"), None),
        P(("groups", "tile"), None),
        P("groups", None),
        P(None, "tile"),
        P("tile", None),
        P(("groups", "tile"), None),
        P(("groups", "tile"), None),
    )
    return jax.shard_map(
        shards, mesh=mesh, in_specs=placed, out_specs=P(("groups", "tile"), None), check_vma=False
    )
```

```python
import functools
import math

import jax
import jax.numpy as jnp
from jax import lax
from jax.experimental import pallas as pl
from jax.experimental.pallas import tpu as pltpu
from jax.sharding import PartitionSpec as P

HEAD_DIM = 128
D = 4096
SPLIT = 4
TILE_COLS = 8

EPSILON = 1e-06
MASKED = -1e30
MESH = pl.DeviceIdType.MESH
VMEM_LIMIT = 60 * 1024 * 1024
CHUNKS = 8
AHEAD = 2
ASIDE = 2
BEHIND = 1
HOP = 2
PASS = 4
DRAIN = (1, 8)
EARLY = 3
BACK_CHUNKS = 4
BACK_LAGS = (1, 4, 7)


def when(cond, body):
    if cond is True:
        body()
    else:
        pl.when(cond)(body)


def both(a, b):
    if a is True:
        return b
    if b is True:
        return a
    return jnp.logical_and(a, b)


def remote(src, dst, send_sem, recv_sem, target):
    return pltpu.make_async_remote_copy(
        src_ref=src,
        dst_ref=dst,
        send_sem=send_sem,
        recv_sem=recv_sem,
        device_id={"tile": target},
        device_id_type=MESH,
    )


def halo_levels(n):
    grid_rows = n // TILE_COLS
    if grid_rows < 2:
        return 1
    return 2 if grid_rows == 2 else 3


def attention_kernel(
    n, rows, q_ref, k_ref, v_ref, mod_ref, att_ref, norm_ref, keys, vals, send_sem, recv_sem, own_sem,
):
    me = lax.axis_index("tile")
    grid_rows = n // TILE_COLS
    tile = lax.rem(me + TILE_COLS // 2, n)
    row = lax.div(tile, TILE_COLS)
    col = lax.rem(tile, TILE_COLS)
    if grid_rows < 2:
        verticals = []
    elif grid_rows == 2:
        verticals = [(1, TILE_COLS, True, 1)]
    else:
        verticals = [(1, n - TILE_COLS, row > 0, 2), (2, TILE_COLS, row < grid_rows - 1, 1)]
    sides = [(-1, col > 0), (1, col < TILE_COLS - 1)]
    here = {level: exists for level, _, exists, _ in verticals}
    here[0] = True

    def slot(level, side):
        return level * 3 + 1 + side

    def place(buf, s):
        return buf.at[pl.ds(s * rows, rows), :]

    def over(offset):
        return lax.rem(me + offset + n, n)

    half = rows // 2
    middle = TILE_COLS // 2
    crossing = {side: col == (middle if side < 0 else middle - 1) for side, _ in sides}
    two = grid_rows == 2

    def part_of(buf, s, h):
        return buf.at[pl.ds(pl.multiple_of(s * rows + h * half, half), half), :]

    own = [
        pltpu.make_async_copy(src, place(buf, slot(0, 0)), own_sem.at[i])
        for i, (src, buf) in enumerate(((k_ref, keys), (v_ref, vals)))
    ]
    for copy in own:
        copy.start()

    def beside(side):
        if not two:
            return over(side)
        return jnp.where(crossing[side], over(side + TILE_COLS), over(side))

    def level_there(level, side):
        return jnp.where(crossing[side], 1 - level, level) if two else level

    barrier = pltpu.get_barrier_semaphore()
    partners = [(over(offset), exists) for _, offset, exists, _ in verticals]
    partners += [(beside(side), exists) for side, exists in sides]
    for target, exists in partners:

        def greet(target=target):
            pl.semaphore_signal(barrier, inc=1, device_id={"tile": target}, device_id_type=MESH)

        when(exists, greet)
    expected = sum(1 if exists is True else jnp.where(exists, 1, 0) for _, exists in partners)
    pl.semaphore_wait(barrier, expected)

    sends = []
    pieces = [(i, h) for i in (0, 1) for h in (0, 1)]
    bufs = (keys, vals)

    def push(i, h, src, there, target, exists):
        copy = remote(
            src,
            part_of(bufs[i], there, h),
            send_sem.at[len(sends)],
            recv_sem.at[there, i * 2 + h],
            target,
        )
        when(exists, copy.start)
        sends.append((copy, exists))

    def arrived(s, exists, i, h):
        ref = part_of(bufs[i], s, h)
        when(exists, remote(ref, ref, send_sem.at[0], recv_sem.at[s, i * 2 + h], me).wait_recv)

    def own_part(i, h):
        return (k_ref, v_ref)[i].at[pl.ds(h * half, half), :]

    for i, h in pieces:
        for level, offset, exists, there in verticals:
            push(i, h, own_part(i, h), slot(there, 0), over(offset), exists)
    for i, h in pieces:
        for side, exists in sides:
            push(i, h, own_part(i, h), slot(level_there(0, side), -side), beside(side), exists)
    for s in range(3 * (1 + len(verticals))):
        level, side = s // 3, s % 3 - 1
        exists = here[level]
        for other, side_exists in sides:
            if other == side:
                exists = both(exists, side_exists)
        if exists is True:
            continue

        def clear(s=s):
            for buf in (keys, vals):
                buf[pl.ds(s * rows, rows), :] = jnp.zeros((rows, D), buf.dtype)

        pl.when(jnp.logical_not(exists))(clear)
    for i, h in pieces:
        for level, offset, exists, there in verticals:
            arrived(slot(level, 0), exists, i, h)
            for side, side_exists in sides:
                push(
                    i,
                    h,
                    part_of(bufs[i], slot(level, 0), h),
                    slot(level_there(level, side), -side),
                    beside(side),
                    both(exists, side_exists),
                )
    for copy in own:
        copy.wait()
    for i, h in pieces:
        for level, exists in sorted(here.items(), key=lambda item: item[0]):
            for side, side_exists in sides:
                arrived(slot(level, side), both(exists, side_exists), i, h)

    span = 3 * (1 + len(verticals)) * rows
    where = lax.broadcasted_iota(jnp.int32, (rows, span), 1)
    bias = jnp.zeros((rows, span), jnp.float32)
    for s in range(span // rows):
        level, side = s // 3, s % 3 - 1
        exists = here[level]
        for other, side_exists in sides:
            if other == side:
                exists = both(exists, side_exists)
        if exists is True:
            continue
        penalty = jnp.where(exists, 0.0, MASKED)
        bias = jnp.where((where >= s * rows) & (where < (s + 1) * rows), penalty, bias)
    scale = 1.0 / math.sqrt(HEAD_DIM)
    together = 8

    def heads(step, carry):
        for extra in range(together):
            at = pl.ds(pl.multiple_of((step * together + extra) * HEAD_DIM, HEAD_DIM), HEAD_DIM)
            scores = lax.dot_general(
                q_ref[:, at], keys[:, at], (((1,), (1,)), ((), ())), preferred_element_type=jnp.float32
            )
            scores = scores * scale + bias
            raised = jnp.exp(scores - jnp.max(scores, axis=-1, keepdims=True))
            probs = (raised * (1.0 / jnp.sum(raised, axis=-1, keepdims=True))).astype(jnp.bfloat16)
            att_ref[:, at] = jnp.dot(probs, vals[:, at], preferred_element_type=jnp.float32).astype(
                att_ref.dtype
            )
        return carry

    lax.fori_loop(0, D // HEAD_DIM // together, heads, 0)

    def normalise(step, carry):
        at = pl.ds(pl.multiple_of(step * 16, 16), 16)
        wide = att_ref[at, :].astype(jnp.float32)
        wide = wide - jnp.mean(wide, axis=-1, keepdims=True)
        spread = jnp.mean(wide * wide, axis=-1, keepdims=True)
        normed = wide * lax.rsqrt(spread + EPSILON)
        norm_ref[at, :] = (normed * (1.0 + mod_ref[1:2, :]) + mod_ref[0:1, :]).astype(norm_ref.dtype)
        return carry

    lax.fori_loop(0, rows // 16, normalise, 0)
    for copy, exists in sends:
        when(exists, copy.wait_send)


def attention(queries, key_rows, values, modulation):
    n = lax.axis_size("tile")
    rows = queries.shape[0]
    levels = halo_levels(n)
    slots = 3 * levels
    vmem = pl.BlockSpec(memory_space=pltpu.VMEM)
    hbm = pl.BlockSpec(memory_space=pl.ANY)
    return pl.pallas_call(
        functools.partial(attention_kernel, n, rows),
        name="halo_attention",
        out_shape=(
            jax.ShapeDtypeStruct((rows, D), jnp.bfloat16),
            jax.ShapeDtypeStruct((rows, D), jnp.bfloat16),
        ),
        in_specs=[vmem, hbm, hbm, vmem],
        out_specs=(vmem, vmem),
        scratch_shapes=[
            pltpu.VMEM((slots * rows, D), jnp.bfloat16),
            pltpu.VMEM((slots * rows, D), jnp.bfloat16),
            pltpu.SemaphoreType.DMA((4 * (2 + 3 * (levels - 1)),)),
            pltpu.SemaphoreType.DMA((slots, 4)),
            pltpu.SemaphoreType.DMA((2,)),
        ],
        compiler_params=pltpu.CompilerParams(
            collective_id=0, has_side_effects=True, vmem_limit_bytes=VMEM_LIMIT
        ),
    )(queries, key_rows, values, modulation)


def device(plane, yy, cc):
    return plane * SPLIT + yy * 2 + cc


def layer_kernel(
    n, rows, cap, chunks, backs, q_ref, k_ref, v_ref, mod_ref, routes_ref, gates_ref, first_ref, second_ref,
    out_ref, att, asked, bias, keys, vals, line, tokens, stage, chooser, spreader, tables, stats, normed,
    first, second, hidden, part, r1, r2, pair, acc_in, acc_out,
    own_sem, kv_send, kv_recv, table_send, table_recv, out_send, line_recv, beside_recv, twin_recv,
    rest_sem, back_send, s1_recv, s2_recv, pair_recv, acc_recv,
):
    planes = n // SPLIT
    width = first.shape[1]
    half = D // 2
    wide = half // chunks
    me = lax.axis_index("tile")
    p = lax.div(me, SPLIT)
    y = lax.div(lax.rem(me, SPLIT), 2)
    c = lax.rem(me, 2)
    beside = device(p, 1 - y, c)
    twin = device(p, y, 1 - c)
    low_half = p < planes // 2
    toward = jnp.where(low_half, 1, -1)
    inner = p + toward
    outer = p - toward
    at_end = jnp.logical_or(p == 0, p == planes - 1)
    middle = jnp.logical_not(at_end)
    outer_expert = jnp.where(low_half, 0, planes - 1)
    inner_device = device(inner, y, c)
    outer_device = device(jnp.where(at_end, p, outer), y, c)

    tile = lax.rem(me + TILE_COLS // 2, n)
    column = lax.rem(tile, TILE_COLS)
    partner = lax.rem(me + TILE_COLS, n)
    sides = [(-1, column > 0), (1, column < TILE_COLS - 1)]
    half_way = TILE_COLS // 2
    crossing = {-1: column == half_way, 1: column == half_way - 1}

    def part_of_plane(plane):
        return jnp.where(plane < planes // 2, half, 0)

    mine_from = part_of_plane(p)
    other_from = half - mine_from
    partner_plane = lax.rem(p + planes // 2, planes)

    def cols(j, base=0):
        return pl.ds(pl.multiple_of(base + j * wide, wide), wide)

    def halves(base):
        return pl.ds(pl.multiple_of(base, half), half)

    def lines(buf, s):
        return buf.at[pl.ds(pl.multiple_of(s * rows, rows), rows), :]

    loads = [
        pltpu.make_async_copy(q_ref.at[:, halves(mine_from)], lines(asked, 0), own_sem.at[0]),
        pltpu.make_async_copy(k_ref.at[:, halves(mine_from)], lines(keys, 1), own_sem.at[1]),
        pltpu.make_async_copy(v_ref.at[:, halves(mine_from)], lines(vals, 1), own_sem.at[2]),
        pltpu.make_async_copy(first_ref, first, own_sem.at[3]),
        pltpu.make_async_copy(second_ref, second, own_sem.at[4]),
    ]

    barrier = pltpu.get_barrier_semaphore()
    others = [lax.rem(me + step, n) for step in range(1, n)]
    for target in others:
        pl.semaphore_signal(barrier, inc=1, device_id={"tile": target}, device_id_type=MESH)

    def beside_tile(side):
        return lax.rem(me + side + jnp.where(crossing[side], TILE_COLS, 0) + n, n)

    def slot_there(level, side):
        return jnp.where(crossing[side], 1 - level, level) * 3 + 1 - side

    bufs = (keys, vals, asked)
    given = (k_ref, v_ref, q_ref)

    def place(i, s, j):
        return bufs[i].at[pl.ds(pl.multiple_of(s * rows, rows), rows), cols(j)]

    def over_vertical(i, j):
        return remote(
            given[i].at[:, cols(j, other_from)],
            place(i, 4 if i < 2 else 1, j),
            kv_send.at[0],
            kv_recv.at[4, j],
            partner,
        )

    def over_side(level, index, i, j):
        side = sides[index][0]
        there = slot_there(level, side)
        source = given[i].at[:, cols(j, mine_from)] if level == 0 else place(i, 4, j)
        return remote(
            source,
            place(i, there, j),
            kv_send.at[1 + level * 2 + index],
            kv_recv.at[there, j],
            beside_tile(side),
        )

    def landed(ref, sem):
        remote(ref, ref, own_sem.at[0], sem, me).wait_recv()

    def send_own(j):
        for i in range(3):
            over_vertical(i, j).start()

    def send_side(j):
        for i in (0, 1):
            for index, (_, exists) in enumerate(sides):
                when(exists, over_side(0, index, i, j).start)

    def bytes_of(count, at):
        return keys.at[pl.ds(0, count * rows), at]

    def send_vertical(j):
        landed(bytes_of(3, cols(j)), kv_recv.at[4, j])
        for i in (0, 1):
            for index, (_, exists) in enumerate(sides):
                when(exists, over_side(1, index, i, j).start)

    pl.semaphore_wait(barrier, n - 1)
    send_own(0)
    send_side(0)
    for load in loads[:3]:
        load.start()

    expert = lax.broadcasted_iota(jnp.int32, (8, rows), 0)
    named = [routes_ref[k : k + 1, :] == expert for k in (0, 1)]
    member = jnp.logical_or(named[0], named[1])
    upto = (
        lax.broadcasted_iota(jnp.int32, (rows, rows), 0) <= lax.broadcasted_iota(jnp.int32, (rows, rows), 1)
    ).astype(jnp.float32).astype(jnp.bfloat16)
    count = jnp.dot(
        member.astype(jnp.float32).astype(jnp.bfloat16), upto, preferred_element_type=jnp.float32
    )
    gate = sum(
        jnp.where(named[k], gates_ref[k : k + 1, :].astype(jnp.float32), 0.0) for k in (0, 1)
    )
    tables[me, 0:8, :] = jnp.where(member, count - 1.0, -1.0)
    stats[me, 8:16, :] = jnp.where(member, count - 1.0, -1.0)
    tables[me, 8:16, :] = gate / 1024.0

    column_planes = [lax.rem(p + step, planes) for step in range(1, planes)]

    def tell_column(step):
        there = device(column_planes[step], y, c)
        return remote(tables.at[me], tables.at[me], table_send.at[0], table_recv.at[0], there)

    for step in range(planes - 1):
        tell_column(step).start()
    for j in range(1, max(AHEAD, ASIDE)):
        if j < min(AHEAD, chunks):
            send_own(j)
        if j < min(ASIDE, chunks):
            send_side(j)

    span = 6 * rows
    where = lax.broadcasted_iota(jnp.int32, (8, span), 1)
    penalty = jnp.zeros((8, span), jnp.float32)
    for s in range(6):
        for side, exists in sides:
            if side != s % 3 - 1:
                continue
            here = (where >= s * rows) & (where < (s + 1) * rows)
            penalty = jnp.where(here, jnp.where(exists, 0.0, MASKED), penalty)

            def clear(s=s):
                for buf in (keys, vals):
                    buf[s * rows : (s + 1) * rows, :] = jnp.zeros((rows, half), buf.dtype)

            pl.when(jnp.logical_not(exists))(clear)
    bias[...] = penalty
    chooser[...] = jnp.zeros(chooser.shape, chooser.dtype)

    def tell_all():
        return [
            remote(stats.at[me], stats.at[me], table_send.at[1], table_recv.at[1], target)
            for target in others
        ]

    for load in loads[:3]:
        load.wait()
    for load in loads[3:]:
        load.start()

    slot_line = lax.broadcasted_iota(jnp.int32, (cap, rows), 0).astype(jnp.float32)

    def chosen(tile_there, e):
        return tables[tile_there, pl.ds(e, 1), :] == slot_line

    def picked_column(which, row):
        return jnp.sum(jnp.where(which, row, 0.0), axis=1, keepdims=True)

    def choose():
        landed(tables.at[pl.ds(0, planes - 1)], table_recv.at[0])
        for plane in range(planes):
            for place_in, e in ((0, p), (1, outer_expert)):
                found = chosen(device(plane, y, c), e).astype(jnp.float32).astype(jnp.bfloat16)
                at = place_in * 2 * cap
                spreader[plane, place_in * cap : (place_in + 1) * cap, :] = found
                chooser[plane, at : at + cap, :rows] = found
                chooser[(plane + planes // 2) % planes, at + cap : at + 2 * cap, rows:] = found

    scale = 1.0 / math.sqrt(HEAD_DIM)

    def attend(j):
        for level in (0, 1):
            for side, exists in sides:
                s = level * 3 + 1 + side
                when(exists, functools.partial(landed, bytes_of(2, cols(j)), kv_recv.at[s, j]))
        for extra in range(wide // HEAD_DIM):
            at = pl.ds(pl.multiple_of(j * wide + extra * HEAD_DIM, HEAD_DIM), HEAD_DIM)
            scores = lax.dot_general(
                asked[:, at], keys[:, at], (((1,), (1,)), ((), ())), preferred_element_type=jnp.float32
            )
            scores = scores * scale + bias[0:1, :]
            raised = jnp.exp(scores - jnp.max(scores, axis=-1, keepdims=True))
            probs = (raised * (1.0 / jnp.sum(raised, axis=-1, keepdims=True))).astype(jnp.bfloat16)
            att[:, at] = jnp.dot(probs, vals[:, at], preferred_element_type=jnp.float32).astype(att.dtype)

    def raw_copy(k, src, j):
        source = att.at[:, cols(j)] if k == 0 else line.at[src, :, cols(j)]
        return remote(source, line.at[src, :, cols(j)], out_send.at[k, 0], line_recv.at[src, j], inner_device)

    def outer_copy(k, src, j):
        there = device(src, y, c)
        return remote(
            stage.at[src, :, cols(j)],
            tokens.at[there, :, cols(j)],
            out_send.at[k, 1],
            line_recv.at[src, j],
            outer_device,
        )

    def rest_copy(src, j):
        ref = line.at[src, pl.ds(rows, rows), cols(j)]
        return remote(ref, ref, rest_sem.at[0], rest_sem.at[1], outer_device)

    def plane_copy(k, src, j, index):
        ref = tokens.at[device(src, y, c), :, cols(j)]
        recv = beside_recv.at[src, j] if index == 0 else twin_recv.at[device(src, y, c)]
        return remote(ref, ref, out_send.at[k, 2 + index], recv, (beside, twin)[index])

    def twin_copy(k, src, j):
        there = device(src, 1 - y, c)
        ref = tokens.at[there, :, cols(j)]
        return remote(ref, ref, out_send.at[k, 4], twin_recv.at[there], twin)

    far = jnp.where(at_end, p + 3 * toward, p + 2 * toward)
    second_plane = jnp.where(at_end, p + 2 * toward, outer)
    sources = [
        (p, BEHIND, True, middle),
        (inner, BEHIND + HOP, False, middle),
        (second_plane, BEHIND + HOP * jnp.where(at_end, 2, 1), middle, False),
        (far, BEHIND + HOP * jnp.where(at_end, 3, 2), False, middle),
    ]

    def relay(k, j):
        src, behind, whole, out = sources[k]
        jj = j - behind

        def go():
            there = device(src, y, c)
            if k > 0:
                pl.when(at_end)(
                    lambda: landed(tokens.at[there, :, cols(jj)], line_recv.at[src, jj])
                )
                pl.when(middle)(lambda: landed(line.at[src, :, cols(jj)], line_recv.at[src, jj]))
            if whole is not False:
                when(whole, raw_copy(k, src, jj).start)
            if k == 1:
                pl.when(middle)(rest_copy(src, jj).start)

            def pick():
                rows_here = att[:, cols(jj)] if k == 0 else line[src, :, cols(jj)]
                picked = jnp.dot(chooser[src], rows_here, preferred_element_type=jnp.float32).astype(
                    tokens.dtype
                )
                tokens[there, :, cols(jj)] = picked[: 2 * cap]
                stage[src, :, cols(jj)] = picked[2 * cap :]

            when(True if k == 0 else middle, pick)
            if out is not False:
                when(out, outer_copy(k, src, jj).start)
            for index in (0, 1):
                plane_copy(k, src, jj, index).start()

        pl.when(jnp.logical_and(jj >= 0, jj < chunks))(go)

    def pass_on(k, j):
        src, behind, _, _ = sources[k]
        jj = j - behind - PASS

        def go():
            there = device(src, 1 - y, c)
            landed(tokens.at[there, :, cols(jj)], beside_recv.at[src, jj])
            twin_copy(k, src, jj).start()

        pl.when(jnp.logical_and(jj >= 0, jj < chunks))(go)

    def move(j):
        for k in range(planes):
            relay(k, j)
        for k in range(planes):
            pass_on(k, j)

    def stream(j, carry):
        pl.when(j < chunks)(lambda: send_vertical(j))

        pl.when(j + AHEAD < chunks)(lambda: send_own(j + AHEAD))
        pl.when(j + ASIDE < chunks)(lambda: send_side(j + ASIDE))
        pl.when(j == BEHIND)(choose)
        pl.when(j >= BEHIND)(lambda: attend(j - BEHIND))
        move(j)
        return carry

    lax.fori_loop(0, chunks + BEHIND, stream, 0)

    def drain(j, carry):
        move(j)
        return carry

    lax.fori_loop(chunks + BEHIND, chunks + BEHIND + DRAIN[0], drain, 0)

    token = lax.broadcasted_iota(jnp.int32, (16, rows), 1)
    line_of = lax.broadcasted_iota(jnp.int32, (16, rows), 0)
    row_number = lax.broadcasted_iota(jnp.int32, (8, rows), 0)
    found = jnp.zeros((8, rows), jnp.float32)
    for step in range(2 * rows // 16):
        some = att[step * 16 : (step + 1) * 16, :].astype(jnp.float32)
        mean = jnp.mean(some, axis=-1, keepdims=True)
        some = some - mean
        spread = jnp.mean(some * some, axis=-1, keepdims=True)
        which, at = divmod(step * 16, rows)
        for kind, value in enumerate((mean, spread)):
            row = jnp.sum(jnp.where(token == line_of + at, value, 0.0), axis=0, keepdims=True)
            found = found + jnp.where(row_number == 2 * which + kind, row, 0.0)
    stats[me, 0:8, :] = found
    for copy in tell_all():
        copy.start()

    lax.fori_loop(chunks + BEHIND + DRAIN[0], chunks + BEHIND + DRAIN[1], drain, 0)
    landed(stats.at[pl.ds(0, n - 1)], table_recv.at[1])
    for load in loads[3:]:
        load.wait()

    order = [
        jnp.where(at_end, p + 2 * toward, inner),
        jnp.where(at_end, p + 3 * toward, p + 2 * toward),
        jnp.where(at_end, inner, outer),
        p,
    ]
    def arrive(plane):
        for source in (plane, lax.rem(plane + planes // 2, planes)):
            for yy in (0, 1):
                there = device(source, yy, 1 - c)
                landed(tokens.at[there], twin_recv.at[there])

    group = SPLIT * cap
    chunk = 512
    span_back = D // backs

    def home_of(i):
        return jnp.where(i == 0, order[0], jnp.where(i == 1, order[1], jnp.where(i == 2, order[2], order[3])))

    def block(buf, index, count, j):
        return buf.at[pl.ds(pl.multiple_of(index * cap, 16), count * cap), back_cols(j)]

    def back_cols(j):
        return pl.ds(pl.multiple_of(j * span_back, span_back), span_back)

    def start_group(plane):
        def normalise(t, carry):
            yy, cc = lax.rem(t, 2), lax.div(t, 2)
            there = device(plane, yy, cc)
            across = lax.rem(there + TILE_COLS, n)
            mean_here, mean_there = stats[there, 0:1, :], stats[across, 2:3, :]
            apart = 0.5 * (mean_here - mean_there)
            spread = 0.5 * (stats[there, 1:2, :] + stats[across, 3:4, :]) + apart * apart
            which = stats[there, pl.ds(8 + p, 1), :] == slot_line
            mean = picked_column(which, 0.5 * (mean_here + mean_there))
            rate = picked_column(which, lax.rsqrt(spread + EPSILON))
            at = pl.ds(pl.multiple_of(t * cap, 16), cap)
            base = part_of_plane(plane)
            for source, lower, start in ((there, 0, base), (across, cap, half - base)):
                for step in range(half // chunk):
                    some = slice(step * chunk, (step + 1) * chunk)
                    to = pl.ds(pl.multiple_of(start + step * chunk, chunk), chunk)
                    value = (tokens[source, lower : lower + cap, some].astype(jnp.float32) - mean) * rate
                    normed[at, to] = (value * (1.0 + mod_ref[1:2, to]) + mod_ref[0:1, to]).astype(
                        normed.dtype
                    )
            return carry

        lax.fori_loop(0, SPLIT, normalise, 0)
        raw = jnp.dot(normed[...], first[...], preferred_element_type=jnp.float32)
        hidden[...] = jax.nn.gelu(raw, approximate=True).astype(hidden.dtype)

    def to_twin(plane, j):
        return remote(
            block(part, plane * SPLIT + (1 - c) * 2, 2, j),
            block(r1, plane * 2, 2, j),
            back_send.at[plane, 0],
            s1_recv.at[plane, j],
            twin,
        )

    def to_beside(plane, j):
        return remote(
            block(part, plane * SPLIT + c * 2 + 1 - y, 1, j),
            block(r2, plane, 1, j),
            back_send.at[plane, 1],
            s2_recv.at[plane, j],
            beside,
        )

    def slots_home(plane, j):
        return remote(
            pair.at[plane, pl.ds(0, cap), back_cols(j)],
            pair.at[plane, pl.ds(cap, cap), back_cols(j)],
            back_send.at[plane, 2],
            pair_recv.at[plane, j],
            inner_device,
        )

    def rows_home(plane, j):
        return remote(
            acc_out.at[plane, :, back_cols(j)],
            acc_in.at[plane, :, back_cols(j)],
            back_send.at[plane, 3],
            acc_recv.at[plane, j],
            device(jnp.where(plane == outer, outer, inner), y, c),
        )

    def produce(i, j):
        plane = home_of(i)
        pl.when(jnp.logical_and(j == 0, i < 2))(lambda: arrive(plane))
        pl.when(j == 0)(lambda: start_group(plane))
        raw = jnp.dot(hidden[...], second[:, back_cols(j)], preferred_element_type=jnp.float32)
        mine = pl.ds(pl.multiple_of(plane * group, 16), group)
        part[mine, back_cols(j)] = raw.astype(part.dtype)
        to_twin(plane, j).start()

    def fold_twin(i, j):
        plane = home_of(i)
        landed(block(r1, plane * 2, 2, j), s1_recv.at[plane, j])
        for yy in (1 - y, y):
            at = pl.ds(pl.multiple_of((plane * SPLIT + c * 2 + yy) * cap, 16), cap)
            there = pl.ds(pl.multiple_of((plane * 2 + yy) * cap, 16), cap)
            total = part[at, back_cols(j)].astype(jnp.float32) + r1[there, back_cols(j)].astype(jnp.float32)
            part[at, back_cols(j)] = total.astype(part.dtype)
            if yy is not y:
                to_beside(plane, j).start()

    def fold_beside(i, j):
        plane = home_of(i)
        there = device(plane, y, c)
        landed(block(r2, plane, 1, j), s2_recv.at[plane, j])
        weight = picked_column(chosen(there, p), tables[there, pl.ds(8 + p, 1), :])
        ours = pl.ds(pl.multiple_of((plane * SPLIT + c * 2 + y) * cap, 16), cap)
        theirs = pl.ds(pl.multiple_of(plane * cap, 16), cap)
        total = part[ours, back_cols(j)].astype(jnp.float32) + r2[theirs, back_cols(j)].astype(jnp.float32)
        pair[plane, :cap, back_cols(j)] = (total * weight).astype(pair.dtype)
        pl.when(jnp.logical_and(at_end, plane != p))(slots_home(plane, j).start)

    def spread_out(plane, both, at):
        amount = 2 * cap if both else cap
        return lax.dot_general(
            spreader[plane, :amount, :],
            pair[plane, :amount, at],
            (((0,), (0,)), ((), ())),
            preferred_element_type=jnp.float32,
        )

    def fold_home(i, j):
        plane = home_of(i)
        at = back_cols(j)

        def fold(both, extra, last):
            if both:
                landed(pair.at[plane, pl.ds(cap, cap), at], pair_recv.at[plane, j])
            if extra:
                landed(acc_in.at[plane, :, at], acc_recv.at[plane, j])
            total = spread_out(plane, both, at)
            if extra:
                total = total + acc_in[plane, :, at].astype(jnp.float32)
            if last:
                out_ref[:, at] = (mod_ref[2:3, at] * total + out_ref[:, at].astype(jnp.float32)).astype(
                    out_ref.dtype
                )
            else:
                acc_out[plane, :, at] = total.astype(acc_out.dtype)
                rows_home(plane, j).start()

        pl.when(jnp.logical_and(at_end, i == 3))(lambda: fold(False, True, True))
        pl.when(jnp.logical_and(middle, i == 3))(lambda: fold(True, True, True))
        pl.when(jnp.logical_and(middle, i == 2))(lambda: fold(False, True, False))
        pl.when(jnp.logical_and(middle, i < 2))(lambda: fold(True, False, False))

    units = planes * backs

    def begin_result():
        pl.when(at_end)(lambda: landed(line.at[partner_plane, pl.ds(rows, rows), :], rest_sem.at[1]))
        out_ref[:, halves(mine_from)] = att[:rows, :]
        out_ref[:, halves(other_from)] = line[partner_plane, rows:, :]

    def give_back(u, carry):
        pl.when(u == 2 * backs + 2)(begin_result)
        for behind, act in ((0, produce), (BACK_LAGS[0], fold_twin), (BACK_LAGS[1], fold_beside), (BACK_LAGS[2], fold_home)):
            at = u - behind
            i, j = lax.div(at, backs), lax.rem(at, backs)
            pl.when(jnp.logical_and(at >= 0, at < units))(functools.partial(act, i, j))
        return carry

    lax.fori_loop(0, EARLY, give_back, 0)
    lax.fori_loop(chunks + BEHIND + DRAIN[1], chunks + BEHIND + 3 * HOP + PASS, drain, 0)
    lax.fori_loop(EARLY, units + BACK_LAGS[2], give_back, 0)

    def gone(ref, sem):
        remote(ref, ref, sem, own_sem.at[0], twin).wait_send()

    every = pl.ds(0, half)
    gone(bytes_of(3, every), kv_send.at[0])
    for level in (0, 1):
        for index, (_, exists) in enumerate(sides):
            when(exists, functools.partial(gone, bytes_of(2, every), kv_send.at[1 + level * 2 + index]))
    for k, (_, _, whole, out) in enumerate(sources):
        if whole is not False:
            when(whole, functools.partial(gone, line.at[0], out_send.at[k, 0]))
        if out is not False:
            when(out, functools.partial(gone, stage.at[0], out_send.at[k, 1]))
        for index in range(3):
            gone(tokens.at[0], out_send.at[k, 2 + index])
    pl.when(middle)(lambda: gone(line.at[0, pl.ds(0, rows), :], rest_sem.at[0]))
    gone(tables.at[pl.ds(0, planes - 1)], table_send.at[0])
    gone(stats.at[pl.ds(0, n - 1)], table_send.at[1])
    for plane in range(planes):
        gone(r1.at[pl.ds(0, 2 * cap), :], back_send.at[plane, 0])
        gone(r1.at[pl.ds(0, cap), :], back_send.at[plane, 1])
        away = p != plane
        pl.when(jnp.logical_and(at_end, away))(
            functools.partial(gone, r1.at[pl.ds(0, cap), :], back_send.at[plane, 2])
        )
        pl.when(jnp.logical_and(middle, away))(functools.partial(gone, acc_in.at[0], back_send.at[plane, 3]))


def kernel_bytes(n, rows, cap, width):
    planes = n // SPLIT
    lines = 2 * 6 * rows + 2 * n * cap + planes * (6 * cap + 3 * rows) + SPLIT * cap + 3 * rows
    return 2 * (lines * D + 2 * width * D)


def layer(queries, key_rows, values, modulation, expert_in, expert_out, routes, gate_fixed):
    n = lax.axis_size("tile")
    rows = queries.shape[0]
    width = expert_in.shape[1]
    planes = n // SPLIT
    cap = 3 * rows // planes
    chunks, backs = CHUNKS, BACK_CHUNKS
    vmem = pl.BlockSpec(memory_space=pltpu.VMEM)
    hbm = pl.BlockSpec(memory_space=pl.ANY)
    dma = pltpu.SemaphoreType.DMA
    bf = jnp.bfloat16
    return pl.pallas_call(
        functools.partial(layer_kernel, n, rows, cap, CHUNKS, BACK_CHUNKS),
        name="whole_layer",
        out_shape=pltpu.VMEM((rows, D), bf),
        in_specs=[hbm, hbm, hbm, vmem, vmem, vmem, hbm, hbm],
        out_specs=vmem,
        scratch_shapes=[
            pltpu.VMEM((2 * rows, D // 2), bf),
            pltpu.VMEM((2 * rows, D // 2), bf),
            pltpu.VMEM((8, 6 * rows), jnp.float32),
            pltpu.VMEM((6 * rows, D // 2), bf),
            pltpu.VMEM((6 * rows, D // 2), bf),
            pltpu.VMEM((planes, 2 * rows, D // 2), bf),
            pltpu.VMEM((n, 2 * cap, D // 2), bf),
            pltpu.VMEM((planes, 2 * cap, D // 2), bf),
            pltpu.VMEM((planes, 4 * cap, 2 * rows), bf),
            pltpu.VMEM((planes, 2 * cap, rows), bf),
            pltpu.VMEM((n, 16, rows), jnp.float32),
            pltpu.VMEM((n, 16, rows), jnp.float32),
            pltpu.VMEM((SPLIT * cap, D), bf),
            pltpu.VMEM((D, width), bf),
            pltpu.VMEM((width, D), bf),
            pltpu.VMEM((SPLIT * cap, width), bf),
            pltpu.VMEM((n * cap, D), bf),
            pltpu.VMEM((planes * 2 * cap, D), bf),
            pltpu.VMEM((planes * cap, D), bf),
            pltpu.VMEM((planes, 2 * cap, D), bf),
            pltpu.VMEM((planes, rows, D), bf),
            pltpu.VMEM((planes, rows, D), bf),
            dma((5,)),
            dma((5,)),
            dma((6, chunks)),
            dma((2,)),
            dma((2,)),
            dma((planes, 5)),
            dma((planes, chunks)),
            dma((planes, chunks)),
            dma((n,)),
            dma((2,)),
            dma((planes, 4)),
            dma((planes, backs)),
            dma((planes, backs)),
            dma((planes, backs)),
            dma((planes, backs)),
        ],
        compiler_params=pltpu.CompilerParams(
            collective_id=1, has_side_effects=True, vmem_limit_bytes=VMEM_LIMIT
        ),
    )(queries, key_rows, values, modulation, routes.T, gate_fixed.T, expert_in, expert_out)


def slot_table(flat, experts_count):
    onehot = (flat[:, None] == jnp.arange(experts_count, dtype=jnp.int32)[None, :]).astype(
        jnp.int32
    )
    before = jnp.cumsum(onehot, axis=0) - onehot
    return jnp.sum(before * onehot, axis=1)


def expert_apply(rows, first_weight, second_weight):
    hidden = jax.nn.gelu(
        jnp.dot(rows, first_weight, preferred_element_type=jnp.float32), approximate=True
    ).astype(jnp.bfloat16)
    return jnp.dot(hidden, second_weight, preferred_element_type=jnp.float32).astype(jnp.bfloat16)


def experts_sparse(normed, attended, modulation, expert_in, expert_out, routes, gate_fixed):
    devices = lax.axis_size("tile")
    rows_dev = normed.shape[0]
    experts_count = devices // SPLIT
    capacity = 3 * rows_dev // experts_count
    flat = routes.reshape(-1)
    slots = slot_table(flat, experts_count)
    target = flat * capacity + slots
    chooser = (
        target[None, :] == jnp.arange(experts_count * capacity, dtype=jnp.int32)[:, None]
    ).astype(jnp.bfloat16)
    chooser = chooser.reshape(experts_count * capacity, rows_dev, 2).sum(axis=2)
    buffer = jnp.dot(chooser, normed, preferred_element_type=jnp.float32).astype(jnp.bfloat16)
    copies = jnp.broadcast_to(
        buffer.reshape(experts_count, 1, capacity, D), (experts_count, SPLIT, capacity, D)
    ).reshape(devices, capacity, D)
    received = lax.all_to_all(copies, "tile", split_axis=0, concat_axis=0, tiled=True)
    sources = received.shape[0]
    count = received.shape[1]
    partial_value = expert_apply(received.reshape(sources * count, D), expert_in, expert_out)
    returned = lax.all_to_all(
        partial_value.reshape(sources, count, D), "tile", split_axis=0, concat_axis=0, tiled=True
    )
    summed = jnp.sum(
        returned.reshape(experts_count, SPLIT, capacity, D).astype(jnp.float32), axis=1
    )
    expert_rows = summed.astype(jnp.bfloat16).reshape(experts_count * capacity, D)
    picked = jnp.take(expert_rows, target, axis=0).reshape(rows_dev, 2, D)
    gate_scale = gate_fixed.astype(jnp.float32) / 1024.0
    mixture = jnp.sum(picked.astype(jnp.float32) * gate_scale[:, :, None], axis=1)
    return (attended.astype(jnp.float32) + modulation[2] * mixture).astype(jnp.bfloat16)


def shards(queries, key_rows, values, modulation, expert_in, expert_out, routes, gate_fixed):
    n = lax.axis_size("tile")
    cap = 3 * queries.shape[0] // (n // SPLIT)
    if n == 2 * TILE_COLS and cap % 16 == 0 and kernel_bytes(n, queries.shape[0], cap, expert_in.shape[1]) < VMEM_LIMIT * 7 // 8:
        return layer(queries, key_rows, values, modulation, expert_in, expert_out, routes, gate_fixed)
    attended, normed = attention(queries, key_rows, values, modulation)
    return experts_sparse(normed, attended, modulation, expert_in, expert_out, routes, gate_fixed)


def solution(mesh):
    placed = (
        P(("groups", "tile"), None),
        P(("groups", "tile"), None),
        P(("groups", "tile"), None),
        P("groups", None),
        P(None, "tile"),
        P("tile", None),
        P(("groups", "tile"), None),
        P(("groups", "tile"), None),
    )
    return jax.shard_map(
        shards, mesh=mesh, in_specs=placed, out_specs=P(("groups", "tile"), None), check_vma=False
    )
```
